256 devices in a mesh: lon: 64 (over z, x, y_hi), probe: 4 (over y_lo, core).
Axes of the slice: x: 4, y: 4 (y_hi: 2, y_lo: 2; y = y_hi * 2 + y_lo), z: 8, core: 2. Of those that a mesh axis runs over, the one named last changes fastest.
Arguments:
- increments: float32 [64, 1536, 8, 256], P('probe', 'lon'), may hold values from -6 to 6
- winds: float32 [2, 1536, 8, 256], P(None, 'lon'), may hold values from -0.2 to 0.2
- obs_weight: float32 [1536, 8, 256], P('lon'), may hold values from 0.1 to 10
Outputs:
- basis: float32 [64, 384, 512], P('probe', 'lon')
- upper: float32 [64, 64], replicated
The draws below stay inside these ranges and needn't reach their ends.
All inputs are finite; a program needn't handle non-finite values.
Results may differ from the reference program's by a relative error of at most 0.00011.
Values sent between devices are 32-bit elements; how exact they have to be, the bound alone decides.
A program may use at most 128 MiB of HBM per device.

```python
import math
import jax
import jax.numpy as jnp
from jax import lax

PROBES = 64
LEV = 8
NLAT = 256
NLON = 1536


def shard_levels(stream_key, shape, shards, smallest, largest):
    def one(position, blocks):
        steps = jax.random.uniform(jax.random.fold_in(jax.random.fold_in(stream_key, 6), position), (blocks,), jnp.float32, smallest / len(shards), largest / len(shards))
        return jnp.repeat(jnp.exp(steps), shape[position] // blocks).reshape((-1,) + (1,) * (len(shape) - position - 1))

    factor_of = one(*shards[0])
    for cut in shards[1:]:
        factor_of = factor_of * one(*cut)
    return factor_of


def normal_values(rng, extent, width, limit, split=(), kind=jnp.bfloat16):
    drawn = width * jax.random.normal(rng, extent, jnp.float32)
    if split:
        drawn = drawn * shard_levels(rng, extent, split, -0.22, 0.18)
    return jnp.clip(drawn, -limit, limit).astype(kind)


def setup_inputs(seed: int = 0) -> dict:
    seeds = jax.random.split(jax.random.key(seed), 4)
    return {
        "increments": normal_values(seeds[0], (PROBES, NLON, LEV, NLAT), 1.0, 6.0, ((0, 4), (1, 64)), jnp.float32),
        "winds": jnp.clip(jax.random.uniform(seeds[1], (2, NLON, LEV, NLAT), jnp.float32, -0.2, 0.2) * shard_levels(seeds[1], (2, NLON, LEV, NLAT), ((1, 64),), -0.4, 0.0), -0.2, 0.2),
        "obs_weight": jnp.clip(jnp.exp(math.log(10.0) - 4.6051702 * jax.random.uniform(seeds[2], (NLON, LEV, NLAT), jnp.float32) ** shard_levels(seeds[2], (NLON, LEV, NLAT), ((0, 64),), -0.2, 0.2)), 0.1, 10.0),
    }


def lat_mask(field):
    rows = lax.broadcasted_iota(jnp.int32, field.shape, field.ndim - 1)
    return jnp.where(rows > 0, field, jnp.zeros_like(field))

def below(field):
    return jnp.concatenate([jnp.zeros_like(field[..., :1]), field[..., :-1]], axis=-1)

def above(field):
    return jnp.concatenate([field[..., 1:], jnp.zeros_like(field[..., :1])], axis=-1)

def forward_step(field, east, north):
    a_pos = jnp.maximum(east, 0.0)
    b_neg = jnp.minimum(east, 0.0)
    c_pos = jnp.maximum(north, 0.0)
    d_neg = jnp.minimum(north, 0.0)
    flux_w = a_pos * jnp.roll(field, 1, axis=1) + b_neg * field
    flux_e = jnp.roll(flux_w, -1, axis=1)
    flux_s = c_pos * below(field) + d_neg * field
    flux_n = above(flux_s)
    return field - (flux_e - flux_w) - (flux_n - flux_s)

def adjoint_step(field, east, north):
    a_pos = jnp.maximum(east, 0.0)
    b_neg = jnp.minimum(east, 0.0)
    c_pos = jnp.maximum(north, 0.0)
    d_neg = jnp.minimum(north, 0.0)
    a_east = jnp.roll(a_pos, -1, axis=0)
    c_north = above(c_pos)
    west_val = jnp.roll(field, 1, axis=1)
    east_val = jnp.roll(field, -1, axis=1)
    return field * (1.0 - a_east + b_neg - c_north + d_neg) - b_neg * west_val + a_east * east_val - d_neg * below(field) + c_north * above(field)

def reference(increments, winds, obs_weight):
    east = winds[0]
    north = lat_mask(winds[1])
    probe_count = increments.shape[0]
    blocks = increments.reshape((probe_count // 8, 8) + increments.shape[1:])

    def apply_block(block):
        state = forward_step(forward_step(block, east, north), east, north)
        state = obs_weight * state
        state = adjoint_step(adjoint_step(state, east, north), east, north)
        sketch = block + state
        shape_now = sketch.shape
        coarse = jnp.mean(sketch.reshape(shape_now[0], shape_now[1] // 4, 4, shape_now[2], shape_now[3] // 4, 4), axis=(2, 5))
        return coarse
    coarse = lax.map(apply_block, blocks)
    coarse = coarse.reshape(probe_count, -1)
    gram = jnp.dot(coarse.astype(jnp.float32), coarse.T.astype(jnp.float32), precision=lax.Precision.HIGHEST, preferred_element_type=jnp.float32)
    lower = jnp.linalg.cholesky(gram)
    ident = jnp.eye(probe_count, dtype=jnp.float32)
    inverse = lax.linalg.triangular_solve(lower, ident, left_side=True, lower=True)
    basis = jnp.dot(inverse.astype(jnp.float32), coarse.astype(jnp.float32), precision=lax.Precision.HIGHEST, preferred_element_type=jnp.float32)
    basis = basis.reshape(probe_count, increments.shape[1] // 4, -1)
    return (basis, lower.T)
```

```python
import jax
import jax.numpy as jnp
from jax import lax
from jax.sharding import PartitionSpec as P


def from_behind(block, axis, distance):
    devices = range(lax.axis_size(axis))
    route = [((i - distance) % len(devices), i) for i in devices]
    return lax.ppermute(block, axis, route)


def butterfly_sum(block, axis):
    count = lax.axis_size(axis)
    if count & (count - 1):
        return lax.psum(block, axis)
    distance = 1
    while distance < count:
        route = [(i, i ^ distance) for i in range(count)]
        block = block + lax.ppermute(block, axis, route)
        distance *= 2
    return block


def padded(block, sides, width):
    for axis, dim in sides:
        count = lax.axis_size(axis)
        forward = [(i, i + 1) for i in range(count - 1)]
        forward.append((count - 1, 0))
        backward = [(target, source) for source, target in forward]
        low = lax.ppermute(
            lax.slice_in_dim(block, block.shape[dim] - width, None, axis=dim), axis, forward
        )
        high = lax.ppermute(lax.slice_in_dim(block, 0, width, axis=dim), axis, backward)
        block = jnp.concatenate([low, block, high], axis=dim)
    return block


def lat_mask(field):
    rows = lax.broadcasted_iota(jnp.int32, field.shape, field.ndim - 1)
    return jnp.where(rows > 0, field, jnp.zeros_like(field))


def below(field):
    return jnp.concatenate([jnp.zeros_like(field[..., :1]), field[..., :-1]], axis=-1)


def above(field):
    return jnp.concatenate([field[..., 1:], jnp.zeros_like(field[..., :1])], axis=-1)


def forward_core(widened, east, north):
    a_pos = jnp.maximum(east, 0.0)
    b_neg = jnp.minimum(east, 0.0)
    c_pos = jnp.maximum(north[1:-1], 0.0)
    d_neg = jnp.minimum(north[1:-1], 0.0)
    flux_w = a_pos[1:] * widened[:, :-1] + b_neg[1:] * widened[:, 1:]
    inner = widened[:, 1:-1]
    flux_s = c_pos * below(inner) + d_neg * inner
    flux_n = above(flux_s)
    return inner - (flux_w[:, 1:] - flux_w[:, :-1]) - (flux_n - flux_s)


def adjoint_core(widened, east, north):
    a_pos = jnp.maximum(east, 0.0)
    b_neg = jnp.minimum(east, 0.0)[1:-1]
    c_pos = jnp.maximum(north[1:-1], 0.0)
    d_neg = jnp.minimum(north[1:-1], 0.0)
    a_east = a_pos[2:]
    c_north = above(c_pos)
    inner = widened[:, 1:-1]
    west_val = widened[:, :-2]
    east_val = widened[:, 2:]
    return (
        inner * (1.0 - a_east + b_neg - c_north + d_neg)
        - b_neg * west_val
        + a_east * east_val
        - d_neg * below(inner)
        + c_north * above(inner)
    )


def body(increments, winds, obs_weight):
    east_local = winds[0]
    north_local = lat_mask(winds[1])
    next_first = from_behind(east_local[:1], "lon", -1)
    near_east = jnp.concatenate([jnp.zeros_like(next_first), east_local, next_first], axis=0)
    edge_zero = jnp.zeros_like(north_local[:1])
    near_north = jnp.concatenate([edge_zero, north_local, edge_zero], axis=0)

    def widen(field):
        return padded(field, (("lon", 1),), 1)

    state = increments
    for step in range(2):
        state = forward_core(widen(state), near_east, near_north)
    state = obs_weight * state
    for step in range(2):
        state = adjoint_core(widen(state), near_east, near_north)
    sketch = increments + state
    probe_count, lon_count, level_count, lat_count = sketch.shape
    coarse = jnp.mean(
        sketch.reshape(probe_count, lon_count // 4, 4, level_count, lat_count // 4, 4), axis=(2, 5)
    )
    coarse = coarse.reshape(probe_count, -1)
    all_probes = probe_count * lax.axis_size("probe")
    ident = jnp.eye(all_probes, dtype=jnp.float32)
    full_panel = lax.all_gather(coarse, "probe", axis=0, tiled=True)
    local_gram = jnp.dot(
        full_panel,
        full_panel.T,
        precision=lax.Precision.HIGHEST,
        preferred_element_type=jnp.float32,
    )
    gram = butterfly_sum(local_gram, "lon")
    lower = jnp.linalg.cholesky(gram)
    inverse = lax.linalg.triangular_solve(lower, ident, left_side=True, lower=True)
    own_rows = lax.dynamic_slice_in_dim(
        inverse, lax.axis_index("probe") * probe_count, probe_count, 0
    )
    basis = jnp.dot(
        own_rows, full_panel, precision=lax.Precision.HIGHEST, preferred_element_type=jnp.float32
    )
    return (basis.reshape(probe_count, lon_count // 4, -1), lower.T)


def solution(mesh):
    in_specs = (P("probe", "lon", None, None), P(None, "lon", None, None), P("lon", None, None))
    out_specs = (P("probe", "lon", None), P())
    return jax.shard_map(body, mesh=mesh, in_specs=in_specs, out_specs=out_specs, check_vma=False)
```

```python
import jax
import jax.numpy as jnp
from jax import lax
from jax.sharding import PartitionSpec as P


def from_behind(block, axis, distance):
    devices = range(lax.axis_size(axis))
    route = [((i - distance) % len(devices), i) for i in devices]
    return lax.ppermute(block, axis, route)


def butterfly_sum(block, axis, radix=8):
    count = lax.axis_size(axis)
    if count & (count - 1):
        return lax.psum(block, axis)
    stride = 1
    while stride < count:
        width = min(radix, count // stride)
        terms = [block]
        for j in range(1, width):
            route = [(i, i ^ (j * stride)) for i in range(count)]
            terms.append(lax.ppermute(block, axis, route))
        while len(terms) > 1:
            terms = [terms[k] + terms[k + 1] for k in range(0, len(terms), 2)]
        block = terms[0]
        stride *= width
    return block


def padded(block, sides, width):
    for axis, dim in sides:
        count = lax.axis_size(axis)
        forward = [(i, i + 1) for i in range(count - 1)]
        forward.append((count - 1, 0))
        backward = [(target, source) for source, target in forward]
        low = lax.ppermute(
            lax.slice_in_dim(block, block.shape[dim] - width, None, axis=dim), axis, forward
        )
        high = lax.ppermute(lax.slice_in_dim(block, 0, width, axis=dim), axis, backward)
        block = jnp.concatenate([low, block, high], axis=dim)
    return block


def lat_mask(field):
    rows = lax.broadcasted_iota(jnp.int32, field.shape, field.ndim - 1)
    return jnp.where(rows > 0, field, jnp.zeros_like(field))


def below(field):
    return jnp.concatenate([jnp.zeros_like(field[..., :1]), field[..., :-1]], axis=-1)


def above(field):
    return jnp.concatenate([field[..., 1:], jnp.zeros_like(field[..., :1])], axis=-1)


def forward_core(widened, east, north):
    a_pos = jnp.maximum(east, 0.0)
    b_neg = jnp.minimum(east, 0.0)
    c_pos = jnp.maximum(north[1:-1], 0.0)
    d_neg = jnp.minimum(north[1:-1], 0.0)
    flux_w = a_pos[1:] * widened[:, :-1] + b_neg[1:] * widened[:, 1:]
    inner = widened[:, 1:-1]
    flux_s = c_pos * below(inner) + d_neg * inner
    flux_n = above(flux_s)
    return inner - (flux_w[:, 1:] - flux_w[:, :-1]) - (flux_n - flux_s)


def adjoint_core(widened, east, north):
    a_pos = jnp.maximum(east, 0.0)
    b_neg = jnp.minimum(east, 0.0)[1:-1]
    c_pos = jnp.maximum(north[1:-1], 0.0)
    d_neg = jnp.minimum(north[1:-1], 0.0)
    a_east = a_pos[2:]
    c_north = above(c_pos)
    inner = widened[:, 1:-1]
    west_val = widened[:, :-2]
    east_val = widened[:, 2:]
    return (
        inner * (1.0 - a_east + b_neg - c_north + d_neg)
        - b_neg * west_val
        + a_east * east_val
        - d_neg * below(inner)
        + c_north * above(inner)
    )


def body(increments, winds, obs_weight):
    east_local = winds[0]
    north_local = lat_mask(winds[1])
    next_first = from_behind(east_local[:1], "lon", -1)
    near_east = jnp.concatenate([jnp.zeros_like(next_first), east_local, next_first], axis=0)
    edge_zero = jnp.zeros_like(north_local[:1])
    near_north = jnp.concatenate([edge_zero, north_local, edge_zero], axis=0)

    def widen(field):
        return padded(field, (("lon", 1),), 1)

    state = increments
    for step in range(2):
        state = forward_core(widen(state), near_east, near_north)
    state = obs_weight * state
    for step in range(2):
        state = adjoint_core(widen(state), near_east, near_north)
    sketch = increments + state
    probe_count, lon_count, level_count, lat_count = sketch.shape
    coarse = jnp.mean(
        sketch.reshape(probe_count, lon_count // 4, 4, level_count, lat_count // 4, 4), axis=(2, 5)
    )
    coarse = coarse.reshape(probe_count, -1)
    all_probes = probe_count * lax.axis_size("probe")
    ident = jnp.eye(all_probes, dtype=jnp.float32)
    full_panel = lax.all_gather(coarse, "probe", axis=0, tiled=True)
    local_gram = jnp.dot(
        full_panel,
        full_panel.T,
        precision=lax.Precision.HIGHEST,
        preferred_element_type=jnp.float32,
    )
    gram = butterfly_sum(local_gram, "lon")
    lower = jnp.linalg.cholesky(gram)
    inverse = lax.linalg.triangular_solve(lower, ident, left_side=True, lower=True)
    own_rows = lax.dynamic_slice_in_dim(
        inverse, lax.axis_index("probe") * probe_count, probe_count, 0
    )
    basis = jnp.dot(
        own_rows, full_panel, precision=lax.Precision.HIGHEST, preferred_element_type=jnp.float32
    )
    return (basis.reshape(probe_count, lon_count // 4, -1), lower.T)


def solution(mesh):
    in_specs = (P("probe", "lon", None, None), P(None, "lon", None, None), P("lon", None, None))
    out_specs = (P("probe", "lon", None), P())
    return jax.shard_map(body, mesh=mesh, in_specs=in_specs, out_specs=out_specs, check_vma=False)
```

```python
import functools

import jax
import jax.numpy as jnp
from jax import lax
from jax.experimental import pallas as pl
from jax.experimental.pallas import tpu as pltpu
from jax.sharding import PartitionSpec as P

MESH = pl.DeviceIdType.MESH


def from_behind(block, axis, distance):
    devices = range(lax.axis_size(axis))
    route = [((i - distance) % len(devices), i) for i in devices]
    return lax.ppermute(block, axis, route)


def exchange_kernel(count, radix, block_ref, out_ref, held, current, send_sem, recv_sem):
    me = lax.axis_index("lon")
    rounds = []
    stride = 1
    while stride < count:
        width = min(radix, count // stride)
        rounds.append((stride, width))
        stride *= width
    partners = [me ^ (j * stride) for stride, width in rounds for j in range(1, width)]

    barrier = pltpu.get_barrier_semaphore()
    for partner in partners:
        pl.semaphore_signal(barrier, inc=1, device_id={"lon": partner}, device_id_type=MESH)
    pl.semaphore_wait(barrier, len(partners))

    current[0] = block_ref[...]
    slot = 0
    for step, (stride, width) in enumerate(rounds):
        copies = []
        for j in range(1, width):
            copy = pltpu.make_async_remote_copy(
                src_ref=current.at[step],
                dst_ref=held.at[slot + j - 1],
                send_sem=send_sem.at[slot + j - 1],
                recv_sem=recv_sem.at[slot + j - 1],
                device_id={"lon": me ^ (j * stride)},
                device_id_type=MESH,
            )
            copy.start()
            copies.append(copy)
        for copy in copies:
            copy.wait()
        terms = [current[step]] + [held[slot + j - 1] for j in range(1, width)]
        while len(terms) > 1:
            terms = [terms[k] + terms[k + 1] for k in range(0, len(terms), 2)]
        current[step + 1] = terms[0]
        slot += width - 1
    out_ref[...] = current[len(rounds)]


def butterfly_sum(block, axis, radix=4):
    count = lax.axis_size(axis)
    if count & (count - 1) or count < 2:
        return lax.psum(block, axis)
    rounds = 0
    slots = 0
    stride = 1
    while stride < count:
        width = min(radix, count // stride)
        rounds += 1
        slots += width - 1
        stride *= width
    return pl.pallas_call(
        functools.partial(exchange_kernel, count, radix),
        out_shape=jax.ShapeDtypeStruct(block.shape, block.dtype),
        in_specs=[pl.BlockSpec(memory_space=pltpu.VMEM)],
        out_specs=pl.BlockSpec(memory_space=pltpu.VMEM),
        scratch_shapes=[
            pltpu.VMEM((slots,) + block.shape, block.dtype),
            pltpu.VMEM((rounds + 1,) + block.shape, block.dtype),
            pltpu.SemaphoreType.DMA((slots,)),
            pltpu.SemaphoreType.DMA((slots,)),
        ],
        compiler_params=pltpu.CompilerParams(collective_id=0, has_side_effects=True),
    )(block)


def padded(block, sides, width):
    for axis, dim in sides:
        count = lax.axis_size(axis)
        forward = [(i, i + 1) for i in range(count - 1)]
        forward.append((count - 1, 0))
        backward = [(target, source) for source, target in forward]
        low = lax.ppermute(
            lax.slice_in_dim(block, block.shape[dim] - width, None, axis=dim), axis, forward
        )
        high = lax.ppermute(lax.slice_in_dim(block, 0, width, axis=dim), axis, backward)
        block = jnp.concatenate([low, block, high], axis=dim)
    return block


def lat_mask(field):
    rows = lax.broadcasted_iota(jnp.int32, field.shape, field.ndim - 1)
    return jnp.where(rows > 0, field, jnp.zeros_like(field))


def below(field):
    return jnp.concatenate([jnp.zeros_like(field[..., :1]), field[..., :-1]], axis=-1)


def above(field):
    return jnp.concatenate([field[..., 1:], jnp.zeros_like(field[..., :1])], axis=-1)


def forward_core(widened, east, north):
    a_pos = jnp.maximum(east, 0.0)
    b_neg = jnp.minimum(east, 0.0)
    c_pos = jnp.maximum(north[1:-1], 0.0)
    d_neg = jnp.minimum(north[1:-1], 0.0)
    flux_w = a_pos[1:] * widened[:, :-1] + b_neg[1:] * widened[:, 1:]
    inner = widened[:, 1:-1]
    flux_s = c_pos * below(inner) + d_neg * inner
    flux_n = above(flux_s)
    return inner - (flux_w[:, 1:] - flux_w[:, :-1]) - (flux_n - flux_s)


def adjoint_core(widened, east, north):
    a_pos = jnp.maximum(east, 0.0)
    b_neg = jnp.minimum(east, 0.0)[1:-1]
    c_pos = jnp.maximum(north[1:-1], 0.0)
    d_neg = jnp.minimum(north[1:-1], 0.0)
    a_east = a_pos[2:]
    c_north = above(c_pos)
    inner = widened[:, 1:-1]
    west_val = widened[:, :-2]
    east_val = widened[:, 2:]
    return (
        inner * (1.0 - a_east + b_neg - c_north + d_neg)
        - b_neg * west_val
        + a_east * east_val
        - d_neg * below(inner)
        + c_north * above(inner)
    )


def body(increments, winds, obs_weight):
    east_local = winds[0]
    north_local = lat_mask(winds[1])
    next_first = from_behind(east_local[:1], "lon", -1)
    near_east = jnp.concatenate([jnp.zeros_like(next_first), east_local, next_first], axis=0)
    edge_zero = jnp.zeros_like(north_local[:1])
    near_north = jnp.concatenate([edge_zero, north_local, edge_zero], axis=0)

    def widen(field):
        return padded(field, (("lon", 1),), 1)

    state = increments
    for step in range(2):
        state = forward_core(widen(state), near_east, near_north)
    state = obs_weight * state
    for step in range(2):
        state = adjoint_core(widen(state), near_east, near_north)
    sketch = increments + state
    probe_count, lon_count, level_count, lat_count = sketch.shape
    coarse = jnp.mean(
        sketch.reshape(probe_count, lon_count // 4, 4, level_count, lat_count // 4, 4), axis=(2, 5)
    )
    coarse = coarse.reshape(probe_count, -1)
    all_probes = probe_count * lax.axis_size("probe")
    ident = jnp.eye(all_probes, dtype=jnp.float32)
    full_panel = lax.all_gather(coarse, "probe", axis=0, tiled=True)
    local_gram = jnp.dot(
        full_panel,
        full_panel.T,
        precision=lax.Precision.HIGHEST,
        preferred_element_type=jnp.float32,
    )
    gram = butterfly_sum(local_gram, "lon")
    lower = jnp.linalg.cholesky(gram)
    inverse = lax.linalg.triangular_solve(lower, ident, left_side=True, lower=True)
    own_rows = lax.dynamic_slice_in_dim(
        inverse, lax.axis_index("probe") * probe_count, probe_count, 0
    )
    basis = jnp.dot(
        own_rows, full_panel, precision=lax.Precision.HIGHEST, preferred_element_type=jnp.float32
    )
    return (basis.reshape(probe_count, lon_count // 4, -1), lower.T)


def solution(mesh):
    in_specs = (P("probe", "lon", None, None), P(None, "lon", None, None), P("lon", None, None))
    out_specs = (P("probe", "lon", None), P())
    return jax.shard_map(body, mesh=mesh, in_specs=in_specs, out_specs=out_specs, check_vma=False)
```

```python
import functools

import jax
import jax.numpy as jnp
from jax import lax
from jax.experimental import pallas as pl
from jax.experimental.pallas import tpu as pltpu
from jax.sharding import PartitionSpec as P

MESH = pl.DeviceIdType.MESH


def from_behind(block, axis, distance):
    devices = range(lax.axis_size(axis))
    route = [((i - distance) % len(devices), i) for i in devices]
    return lax.ppermute(block, axis, route)


def exchange_kernel(count, radix, block_ref, out_ref, held, current, send_sem, recv_sem):
    me = lax.axis_index("lon")
    rounds = []
    stride = 1
    while stride < count:
        width = min(radix, count // stride)
        rounds.append((stride, width))
        stride *= width
    partners = [me ^ (j * stride) for stride, width in rounds for j in range(1, width)]

    barrier = pltpu.get_barrier_semaphore()
    for partner in partners:
        pl.semaphore_signal(barrier, inc=1, device_id={"lon": partner}, device_id_type=MESH)
    pl.semaphore_wait(barrier, len(partners))

    current[0] = block_ref[...]
    slot = 0
    for step, (stride, width) in enumerate(rounds):
        copies = []
        for j in range(1, width):
            copy = pltpu.make_async_remote_copy(
                src_ref=current.at[step],
                dst_ref=held.at[slot + j - 1],
                send_sem=send_sem.at[slot + j - 1],
                recv_sem=recv_sem.at[slot + j - 1],
                device_id={"lon": me ^ (j * stride)},
                device_id_type=MESH,
            )
            copy.start()
            copies.append(copy)
        for copy in copies:
            copy.wait()
        terms = [current[step]] + [held[slot + j - 1] for j in range(1, width)]
        while len(terms) > 1:
            terms = [terms[k] + terms[k + 1] for k in range(0, len(terms), 2)]
        current[step + 1] = terms[0]
        slot += width - 1
    out_ref[...] = current[len(rounds)]


def butterfly_sum(block, axis, radix=4):
    count = lax.axis_size(axis)
    if count & (count - 1) or count < 2:
        return lax.psum(block, axis)
    rounds = 0
    slots = 0
    stride = 1
    while stride < count:
        width = min(radix, count // stride)
        rounds += 1
        slots += width - 1
        stride *= width
    return pl.pallas_call(
        functools.partial(exchange_kernel, count, radix),
        out_shape=jax.ShapeDtypeStruct(block.shape, block.dtype),
        in_specs=[pl.BlockSpec(memory_space=pltpu.VMEM)],
        out_specs=pl.BlockSpec(memory_space=pltpu.VMEM),
        scratch_shapes=[
            pltpu.VMEM((slots,) + block.shape, block.dtype),
            pltpu.VMEM((rounds + 1,) + block.shape, block.dtype),
            pltpu.SemaphoreType.DMA((slots,)),
            pltpu.SemaphoreType.DMA((slots,)),
        ],
        compiler_params=pltpu.CompilerParams(collective_id=0, has_side_effects=True),
    )(block)


def padded(block, sides, width):
    for axis, dim in sides:
        count = lax.axis_size(axis)
        forward = [(i, i + 1) for i in range(count - 1)]
        forward.append((count - 1, 0))
        backward = [(target, source) for source, target in forward]
        low = lax.ppermute(
            lax.slice_in_dim(block, block.shape[dim] - width, None, axis=dim), axis, forward
        )
        high = lax.ppermute(lax.slice_in_dim(block, 0, width, axis=dim), axis, backward)
        block = jnp.concatenate([low, block, high], axis=dim)
    return block


def lat_mask(field):
    rows = lax.broadcasted_iota(jnp.int32, field.shape, field.ndim - 1)
    return jnp.where(rows > 0, field, jnp.zeros_like(field))


def below(field):
    return jnp.concatenate([jnp.zeros_like(field[..., :1]), field[..., :-1]], axis=-1)


def above(field):
    return jnp.concatenate([field[..., 1:], jnp.zeros_like(field[..., :1])], axis=-1)


def forward_core(widened, east, north):
    a_pos = jnp.maximum(east, 0.0)
    b_neg = jnp.minimum(east, 0.0)
    c_pos = jnp.maximum(north[1:-1], 0.0)
    d_neg = jnp.minimum(north[1:-1], 0.0)
    flux_w = a_pos[1:] * widened[:, :-1] + b_neg[1:] * widened[:, 1:]
    inner = widened[:, 1:-1]
    flux_s = c_pos * below(inner) + d_neg * inner
    flux_n = above(flux_s)
    return inner - (flux_w[:, 1:] - flux_w[:, :-1]) - (flux_n - flux_s)


def adjoint_core(widened, east, north):
    a_pos = jnp.maximum(east, 0.0)
    b_neg = jnp.minimum(east, 0.0)[1:-1]
    c_pos = jnp.maximum(north[1:-1], 0.0)
    d_neg = jnp.minimum(north[1:-1], 0.0)
    a_east = a_pos[2:]
    c_north = above(c_pos)
    inner = widened[:, 1:-1]
    west_val = widened[:, :-2]
    east_val = widened[:, 2:]
    return (
        inner * (1.0 - a_east + b_neg - c_north + d_neg)
        - b_neg * west_val
        + a_east * east_val
        - d_neg * below(inner)
        + c_north * above(inner)
    )


def body(increments, winds, obs_weight):
    probe_count, lon_count, level_count, lat_count = increments.shape
    halo = 4
    pack = (increments, winds[0][None], lat_mask(winds[1])[None], obs_weight[None])
    count = lax.axis_size("lon")
    forward = [(i, (i + 1) % count) for i in range(count)]
    backward = [((i + 1) % count, i) for i in range(count)]
    west_edge = jnp.concatenate([part[:, lon_count - halo:] for part in pack], axis=0)
    east_edge = jnp.concatenate([part[:, :halo] for part in pack], axis=0)
    from_west = lax.ppermute(west_edge, "lon", forward)
    from_east = lax.ppermute(east_edge, "lon", backward)
    wide = [
        jnp.concatenate([from_west[lo:hi], part, from_east[lo:hi]], axis=1)
        for part, (lo, hi) in zip(
            pack,
            ((0, probe_count), (probe_count, probe_count + 1),
             (probe_count + 1, probe_count + 2), (probe_count + 2, probe_count + 3)),
        )
    ]
    state, east, north, weight = wide[0], wide[1][0], wide[2][0], wide[3][0]
    span = lon_count + 2 * halo
    for step in range(2):
        state = forward_core(state, east[step:span - step], north[step:span - step])
    state = weight[2:span - 2] * state
    for step in range(2, 4):
        state = adjoint_core(state, east[step:span - step], north[step:span - step])
    sketch = increments + state
    coarse = sketch.reshape(probe_count, lon_count // 4, 4, level_count, lat_count).sum(axis=2)
    coarse = coarse.reshape(probe_count, lon_count // 4, level_count, lat_count // 4, 4).sum(axis=4)
    coarse = coarse * (1.0 / 16.0)
    coarse = coarse.reshape(probe_count, -1)
    all_probes = probe_count * lax.axis_size("probe")
    ident = jnp.eye(all_probes, dtype=jnp.float32)
    full_panel = lax.all_gather(coarse, "probe", axis=0, tiled=True)
    local_gram = jnp.dot(
        full_panel,
        full_panel.T,
        precision=lax.Precision.HIGHEST,
        preferred_element_type=jnp.float32,
    )
    gram = butterfly_sum(local_gram, "lon")
    lower = jnp.linalg.cholesky(gram)
    inverse = lax.linalg.triangular_solve(lower, ident, left_side=True, lower=True)
    own_rows = lax.dynamic_slice_in_dim(
        inverse, lax.axis_index("probe") * probe_count, probe_count, 0
    )
    basis = jnp.dot(
        own_rows, full_panel, precision=lax.Precision.HIGHEST, preferred_element_type=jnp.float32
    )
    return (basis.reshape(probe_count, lon_count // 4, -1), lower.T)


def solution(mesh):
    in_specs = (P("probe", "lon", None, None), P(None, "lon", None, None), P("lon", None, None))
    out_specs = (P("probe", "lon", None), P())
    return jax.shard_map(body, mesh=mesh, in_specs=in_specs, out_specs=out_specs, check_vma=False)
```

```python
import functools

import jax
import jax.numpy as jnp
from jax import lax
from jax.experimental import pallas as pl
from jax.experimental.pallas import tpu as pltpu
from jax.sharding import PartitionSpec as P

MESH = pl.DeviceIdType.MESH


def from_behind(block, axis, distance):
    devices = range(lax.axis_size(axis))
    route = [((i - distance) % len(devices), i) for i in devices]
    return lax.ppermute(block, axis, route)


def exchange_kernel(count, radix, block_ref, out_ref, held, current, send_sem, recv_sem):
    me = lax.axis_index("lon")
    rounds = []
    stride = 1
    while stride < count:
        width = min(radix, count // stride)
        rounds.append((stride, width))
        stride *= width
    partners = [me ^ (j * stride) for stride, width in rounds for j in range(1, width)]

    barrier = pltpu.get_barrier_semaphore()
    for partner in partners:
        pl.semaphore_signal(barrier, inc=1, device_id={"lon": partner}, device_id_type=MESH)
    pl.semaphore_wait(barrier, len(partners))

    current[0] = block_ref[...]
    slot = 0
    for step, (stride, width) in enumerate(rounds):
        copies = []
        for j in range(1, width):
            copy = pltpu.make_async_remote_copy(
                src_ref=current.at[step],
                dst_ref=held.at[slot + j - 1],
                send_sem=send_sem.at[slot + j - 1],
                recv_sem=recv_sem.at[slot + j - 1],
                device_id={"lon": me ^ (j * stride)},
                device_id_type=MESH,
            )
            copy.start()
            copies.append(copy)
        for copy in copies:
            copy.wait()
        terms = [current[step]] + [held[slot + j - 1] for j in range(1, width)]
        while len(terms) > 1:
            terms = [terms[k] + terms[k + 1] for k in range(0, len(terms), 2)]
        current[step + 1] = terms[0]
        slot += width - 1
    out_ref[...] = current[len(rounds)]


def butterfly_sum(block, axis, radix=4):
    count = lax.axis_size(axis)
    if count & (count - 1) or count < 2:
        return lax.psum(block, axis)
    rounds = 0
    slots = 0
    stride = 1
    while stride < count:
        width = min(radix, count // stride)
        rounds += 1
        slots += width - 1
        stride *= width
    return pl.pallas_call(
        functools.partial(exchange_kernel, count, radix),
        out_shape=jax.ShapeDtypeStruct(block.shape, block.dtype),
        in_specs=[pl.BlockSpec(memory_space=pltpu.VMEM)],
        out_specs=pl.BlockSpec(memory_space=pltpu.VMEM),
        scratch_shapes=[
            pltpu.VMEM((slots,) + block.shape, block.dtype),
            pltpu.VMEM((rounds + 1,) + block.shape, block.dtype),
            pltpu.SemaphoreType.DMA((slots,)),
            pltpu.SemaphoreType.DMA((slots,)),
        ],
        compiler_params=pltpu.CompilerParams(collective_id=0, has_side_effects=True),
    )(block)


def padded(block, sides, width):
    for axis, dim in sides:
        count = lax.axis_size(axis)
        forward = [(i, i + 1) for i in range(count - 1)]
        forward.append((count - 1, 0))
        backward = [(target, source) for source, target in forward]
        low = lax.ppermute(
            lax.slice_in_dim(block, block.shape[dim] - width, None, axis=dim), axis, forward
        )
        high = lax.ppermute(lax.slice_in_dim(block, 0, width, axis=dim), axis, backward)
        block = jnp.concatenate([low, block, high], axis=dim)
    return block


def lat_mask(field):
    rows = lax.broadcasted_iota(jnp.int32, field.shape, field.ndim - 1)
    return jnp.where(rows > 0, field, jnp.zeros_like(field))


def below(field):
    return jnp.concatenate([jnp.zeros_like(field[..., :1]), field[..., :-1]], axis=-1)


def above(field):
    return jnp.concatenate([field[..., 1:], jnp.zeros_like(field[..., :1])], axis=-1)


def forward_core(widened, east, north):
    a_pos = jnp.maximum(east, 0.0)
    b_neg = jnp.minimum(east, 0.0)
    c_pos = jnp.maximum(north[1:-1], 0.0)
    d_neg = jnp.minimum(north[1:-1], 0.0)
    flux_w = a_pos[1:] * widened[:, :-1] + b_neg[1:] * widened[:, 1:]
    inner = widened[:, 1:-1]
    flux_s = c_pos * below(inner) + d_neg * inner
    flux_n = above(flux_s)
    return inner - (flux_w[:, 1:] - flux_w[:, :-1]) - (flux_n - flux_s)


def adjoint_core(widened, east, north):
    a_pos = jnp.maximum(east, 0.0)
    b_neg = jnp.minimum(east, 0.0)[1:-1]
    c_pos = jnp.maximum(north[1:-1], 0.0)
    d_neg = jnp.minimum(north[1:-1], 0.0)
    a_east = a_pos[2:]
    c_north = above(c_pos)
    inner = widened[:, 1:-1]
    west_val = widened[:, :-2]
    east_val = widened[:, 2:]
    return (
        inner * (1.0 - a_east + b_neg - c_north + d_neg)
        - b_neg * west_val
        + a_east * east_val
        - d_neg * below(inner)
        + c_north * above(inner)
    )


def four_steps(state, east, north, weight):
    span = state.shape[1]
    for step in range(2):
        state = forward_core(state, east[step:span - step], north[step:span - step])
    state = weight[2:span - 2] * state
    for step in range(2, 4):
        state = adjoint_core(state, east[step:span - step], north[step:span - step])
    return state


def coarsen(sketch):
    probe_count, lon_count, level_count, lat_count = sketch.shape
    coarse = sketch.reshape(probe_count, lon_count // 4, 4, level_count, lat_count).sum(axis=2)
    coarse = coarse.reshape(probe_count, lon_count // 4, level_count, lat_count // 4, 4).sum(axis=4)
    return coarse * (1.0 / 16.0)


def body(increments, winds, obs_weight):
    probe_count, lon_count, level_count, lat_count = increments.shape
    halo = 4
    pack = (increments, winds[0][None], lat_mask(winds[1])[None], obs_weight[None])
    count = lax.axis_size("lon")
    forward = [(i, (i + 1) % count) for i in range(count)]
    backward = [((i + 1) % count, i) for i in range(count)]
    west_edge = jnp.concatenate([part[:, lon_count - halo:] for part in pack], axis=0)
    east_edge = jnp.concatenate([part[:, :halo] for part in pack], axis=0)
    from_west = lax.ppermute(west_edge, "lon", forward)
    from_east = lax.ppermute(east_edge, "lon", backward)
    bounds = ((0, probe_count), (probe_count, probe_count + 1),
              (probe_count + 1, probe_count + 2), (probe_count + 2, probe_count + 3))

    def fields(parts):
        return parts[0], parts[1][0], parts[2][0], parts[3][0]

    inner = four_steps(*fields(pack))
    inner = coarsen(increments[:, halo:lon_count - halo] + inner)
    west = [jnp.concatenate([from_west[lo:hi], part[:, :2 * halo]], axis=1)
            for part, (lo, hi) in zip(pack, bounds)]
    west = coarsen(increments[:, :halo] + four_steps(*fields(west)))
    east = [jnp.concatenate([part[:, lon_count - 2 * halo:], from_east[lo:hi]], axis=1)
            for part, (lo, hi) in zip(pack, bounds)]
    east = coarsen(increments[:, lon_count - halo:] + four_steps(*fields(east)))
    coarse = jnp.concatenate([west, inner, east], axis=1)
    coarse = coarse.reshape(probe_count, -1)
    all_probes = probe_count * lax.axis_size("probe")
    ident = jnp.eye(all_probes, dtype=jnp.float32)
    full_panel = lax.all_gather(coarse, "probe", axis=0, tiled=True)
    local_gram = jnp.dot(
        full_panel,
        full_panel.T,
        precision=lax.Precision.HIGHEST,
        preferred_element_type=jnp.float32,
    )
    gram = butterfly_sum(local_gram, "lon")
    lower = jnp.linalg.cholesky(gram)
    inverse = lax.linalg.triangular_solve(lower, ident, left_side=True, lower=True)
    own_rows = lax.dynamic_slice_in_dim(
        inverse, lax.axis_index("probe") * probe_count, probe_count, 0
    )
    basis = jnp.dot(
        own_rows, full_panel, precision=lax.Precision.HIGHEST, preferred_element_type=jnp.float32
    )
    return (basis.reshape(probe_count, lon_count // 4, -1), lower.T)


def solution(mesh):
    in_specs = (P("probe", "lon", None, None), P(None, "lon", None, None), P("lon", None, None))
    out_specs = (P("probe", "lon", None), P())
    return jax.shard_map(body, mesh=mesh, in_specs=in_specs, out_specs=out_specs, check_vma=False)
```

```python
import functools

import jax
import jax.numpy as jnp
from jax import lax
from jax.experimental import pallas as pl
from jax.experimental.pallas import tpu as pltpu
from jax.sharding import PartitionSpec as P

MESH = pl.DeviceIdType.MESH


def from_behind(block, axis, distance):
    devices = range(lax.axis_size(axis))
    route = [((i - distance) % len(devices), i) for i in devices]
    return lax.ppermute(block, axis, route)


def exchange_kernel(count, radix, block_ref, out_ref, held, current, send_sem, recv_sem):
    me = lax.axis_index("lon")
    rounds = []
    stride = 1
    while stride < count:
        width = min(radix, count // stride)
        rounds.append((stride, width))
        stride *= width
    partners = [me ^ (j * stride) for stride, width in rounds for j in range(1, width)]

    barrier = pltpu.get_barrier_semaphore()
    for partner in partners:
        pl.semaphore_signal(barrier, inc=1, device_id={"lon": partner}, device_id_type=MESH)
    pl.semaphore_wait(barrier, len(partners))

    current[0] = block_ref[...]
    slot = 0
    for step, (stride, width) in enumerate(rounds):
        copies = []
        for j in range(1, width):
            copy = pltpu.make_async_remote_copy(
                src_ref=current.at[step],
                dst_ref=held.at[slot + j - 1],
                send_sem=send_sem.at[slot + j - 1],
                recv_sem=recv_sem.at[slot + j - 1],
                device_id={"lon": me ^ (j * stride)},
                device_id_type=MESH,
            )
            copy.start()
            copies.append(copy)
        for copy in copies:
            copy.wait()
        terms = [current[step]] + [held[slot + j - 1] for j in range(1, width)]
        while len(terms) > 1:
            terms = [terms[k] + terms[k + 1] for k in range(0, len(terms), 2)]
        current[step + 1] = terms[0]
        slot += width - 1
    out_ref[...] = current[len(rounds)]


def butterfly_sum(block, axis, radix=4):
    count = lax.axis_size(axis)
    if count & (count - 1) or count < 2:
        return lax.psum(block, axis)
    rounds = 0
    slots = 0
    stride = 1
    while stride < count:
        width = min(radix, count // stride)
        rounds += 1
        slots += width - 1
        stride *= width
    return pl.pallas_call(
        functools.partial(exchange_kernel, count, radix),
        out_shape=jax.ShapeDtypeStruct(block.shape, block.dtype),
        in_specs=[pl.BlockSpec(memory_space=pltpu.VMEM)],
        out_specs=pl.BlockSpec(memory_space=pltpu.VMEM),
        scratch_shapes=[
            pltpu.VMEM((slots,) + block.shape, block.dtype),
            pltpu.VMEM((rounds + 1,) + block.shape, block.dtype),
            pltpu.SemaphoreType.DMA((slots,)),
            pltpu.SemaphoreType.DMA((slots,)),
        ],
        compiler_params=pltpu.CompilerParams(collective_id=0, has_side_effects=True),
    )(block)


def padded(block, sides, width):
    for axis, dim in sides:
        count = lax.axis_size(axis)
        forward = [(i, i + 1) for i in range(count - 1)]
        forward.append((count - 1, 0))
        backward = [(target, source) for source, target in forward]
        low = lax.ppermute(
            lax.slice_in_dim(block, block.shape[dim] - width, None, axis=dim), axis, forward
        )
        high = lax.ppermute(lax.slice_in_dim(block, 0, width, axis=dim), axis, backward)
        block = jnp.concatenate([low, block, high], axis=dim)
    return block


def lat_mask(field):
    rows = lax.broadcasted_iota(jnp.int32, field.shape, field.ndim - 1)
    return jnp.where(rows > 0, field, jnp.zeros_like(field))


def below(field):
    return jnp.concatenate([jnp.zeros_like(field[..., :1]), field[..., :-1]], axis=-1)


def above(field):
    return jnp.concatenate([field[..., 1:], jnp.zeros_like(field[..., :1])], axis=-1)


def forward_core(widened, east, north):
    a_pos = jnp.maximum(east, 0.0)
    b_neg = jnp.minimum(east, 0.0)
    c_pos = jnp.maximum(north[1:-1], 0.0)
    d_neg = jnp.minimum(north[1:-1], 0.0)
    flux_w = a_pos[1:] * widened[:, :-1] + b_neg[1:] * widened[:, 1:]
    inner = widened[:, 1:-1]
    flux_s = c_pos * below(inner) + d_neg * inner
    flux_n = above(flux_s)
    return inner - (flux_w[:, 1:] - flux_w[:, :-1]) - (flux_n - flux_s)


def adjoint_core(widened, east, north):
    a_pos = jnp.maximum(east, 0.0)
    b_neg = jnp.minimum(east, 0.0)[1:-1]
    c_pos = jnp.maximum(north[1:-1], 0.0)
    d_neg = jnp.minimum(north[1:-1], 0.0)
    a_east = a_pos[2:]
    c_north = above(c_pos)
    inner = widened[:, 1:-1]
    west_val = widened[:, :-2]
    east_val = widened[:, 2:]
    return (
        inner * (1.0 - a_east + b_neg - c_north + d_neg)
        - b_neg * west_val
        + a_east * east_val
        - d_neg * below(inner)
        + c_north * above(inner)
    )


def four_steps(state, east, north, weight):
    span = state.shape[1]
    for step in range(2):
        state = forward_core(state, east[step:span - step], north[step:span - step])
    state = weight[2:span - 2] * state
    for step in range(2, 4):
        state = adjoint_core(state, east[step:span - step], north[step:span - step])
    return state


def coarsen(sketch):
    probe_count, lon_count, level_count, lat_count = sketch.shape
    coarse = sketch.reshape(probe_count, lon_count // 4, 4, level_count, lat_count).sum(axis=2)
    coarse = coarse.reshape(probe_count, lon_count // 4, level_count, lat_count // 4, 4).sum(axis=4)
    return coarse * (1.0 / 16.0)


def body(increments, winds, obs_weight):
    probe_count, lon_count, level_count, lat_count = increments.shape
    halo = 4
    pack = (increments, winds[0][None], lat_mask(winds[1])[None], obs_weight[None])
    count = lax.axis_size("lon")
    forward = [(i, (i + 1) % count) for i in range(count)]
    backward = [((i + 1) % count, i) for i in range(count)]
    west_edge = jnp.concatenate([part[:, lon_count - halo:] for part in pack], axis=0)
    east_edge = jnp.concatenate([part[:, :halo] for part in pack], axis=0)
    from_west = lax.ppermute(west_edge, "lon", forward)
    from_east = lax.ppermute(east_edge, "lon", backward)
    bounds = ((0, probe_count), (probe_count, probe_count + 1),
              (probe_count + 1, probe_count + 2), (probe_count + 2, probe_count + 3))

    def fields(parts):
        return parts[0], parts[1][0], parts[2][0], parts[3][0]

    inner = four_steps(*fields(pack))
    inner = coarsen(increments[:, halo:lon_count - halo] + inner)
    rim = [
        jnp.concatenate(
            [from_west[lo:hi], part[:, :2 * halo], part[:, lon_count - 2 * halo:], from_east[lo:hi]],
            axis=1,
        )
        for part, (lo, hi) in zip(pack, bounds)
    ]
    rim = four_steps(*fields(rim))
    west = coarsen(increments[:, :halo] + rim[:, :halo])
    east = coarsen(increments[:, lon_count - halo:] + rim[:, rim.shape[1] - halo:])
    coarse = jnp.concatenate([west, inner, east], axis=1)
    coarse = coarse.reshape(probe_count, -1)
    all_probes = probe_count * lax.axis_size("probe")
    ident = jnp.eye(all_probes, dtype=jnp.float32)
    full_panel = lax.all_gather(coarse, "probe", axis=0, tiled=True)
    local_gram = jnp.dot(
        full_panel,
        full_panel.T,
        precision=lax.Precision.HIGHEST,
        preferred_element_type=jnp.float32,
    )
    gram = butterfly_sum(local_gram, "lon")
    lower = jnp.linalg.cholesky(gram)
    inverse = lax.linalg.triangular_solve(lower, ident, left_side=True, lower=True)
    own_rows = lax.dynamic_slice_in_dim(
        inverse, lax.axis_index("probe") * probe_count, probe_count, 0
    )
    basis = jnp.dot(
        own_rows, full_panel, precision=lax.Precision.HIGHEST, preferred_element_type=jnp.float32
    )
    return (basis.reshape(probe_count, lon_count // 4, -1), lower.T)


def solution(mesh):
    in_specs = (P("probe", "lon", None, None), P(None, "lon", None, None), P("lon", None, None))
    out_specs = (P("probe", "lon", None), P())
    return jax.shard_map(body, mesh=mesh, in_specs=in_specs, out_specs=out_specs, check_vma=False)
```

```python
import functools

import jax
import jax.numpy as jnp
from jax import lax
from jax.experimental import pallas as pl
from jax.experimental.pallas import tpu as pltpu
from jax.sharding import PartitionSpec as P

MESH = pl.DeviceIdType.MESH


def from_behind(block, axis, distance):
    devices = range(lax.axis_size(axis))
    route = [((i - distance) % len(devices), i) for i in devices]
    return lax.ppermute(block, axis, route)


def exchange_kernel(count, radix, block_ref, out_ref, held, current, send_sem, recv_sem):
    me = lax.axis_index("lon")
    rounds = []
    stride = 1
    while stride < count:
        width = min(radix, count // stride)
        rounds.append((stride, width))
        stride *= width
    partners = [me ^ (j * stride) for stride, width in rounds for j in range(1, width)]

    barrier = pltpu.get_barrier_semaphore()
    for partner in partners:
        pl.semaphore_signal(barrier, inc=1, device_id={"lon": partner}, device_id_type=MESH)
    pl.semaphore_wait(barrier, len(partners))

    current[0] = block_ref[...]
    slot = 0
    for step, (stride, width) in enumerate(rounds):
        copies = []
        for j in range(1, width):
            copy = pltpu.make_async_remote_copy(
                src_ref=current.at[step],
                dst_ref=held.at[slot + j - 1],
                send_sem=send_sem.at[slot + j - 1],
                recv_sem=recv_sem.at[slot + j - 1],
                device_id={"lon": me ^ (j * stride)},
                device_id_type=MESH,
            )
            copy.start()
            copies.append(copy)
        for copy in copies:
            copy.wait()
        terms = [current[step]] + [held[slot + j - 1] for j in range(1, width)]
        while len(terms) > 1:
            terms = [terms[k] + terms[k + 1] for k in range(0, len(terms), 2)]
        current[step + 1] = terms[0]
        slot += width - 1
    out_ref[...] = current[len(rounds)]


def butterfly_sum(block, axis, radix=4):
    count = lax.axis_size(axis)
    if count & (count - 1) or count < 2:
        return lax.psum(block, axis)
    rounds = 0
    slots = 0
    stride = 1
    while stride < count:
        width = min(radix, count // stride)
        rounds += 1
        slots += width - 1
        stride *= width
    return pl.pallas_call(
        functools.partial(exchange_kernel, count, radix),
        out_shape=jax.ShapeDtypeStruct(block.shape, block.dtype),
        in_specs=[pl.BlockSpec(memory_space=pltpu.VMEM)],
        out_specs=pl.BlockSpec(memory_space=pltpu.VMEM),
        scratch_shapes=[
            pltpu.VMEM((slots,) + block.shape, block.dtype),
            pltpu.VMEM((rounds + 1,) + block.shape, block.dtype),
            pltpu.SemaphoreType.DMA((slots,)),
            pltpu.SemaphoreType.DMA((slots,)),
        ],
        compiler_params=pltpu.CompilerParams(collective_id=0, has_side_effects=True),
    )(block)


def padded(block, sides, width):
    for axis, dim in sides:
        count = lax.axis_size(axis)
        forward = [(i, i + 1) for i in range(count - 1)]
        forward.append((count - 1, 0))
        backward = [(target, source) for source, target in forward]
        low = lax.ppermute(
            lax.slice_in_dim(block, block.shape[dim] - width, None, axis=dim), axis, forward
        )
        high = lax.ppermute(lax.slice_in_dim(block, 0, width, axis=dim), axis, backward)
        block = jnp.concatenate([low, block, high], axis=dim)
    return block


def lat_mask(field):
    rows = lax.broadcasted_iota(jnp.int32, field.shape, field.ndim - 1)
    return jnp.where(rows > 0, field, jnp.zeros_like(field))


def below(field):
    return jnp.concatenate([jnp.zeros_like(field[..., :1]), field[..., :-1]], axis=-1)


def above(field):
    return jnp.concatenate([field[..., 1:], jnp.zeros_like(field[..., :1])], axis=-1)


def forward_core(widened, east, north):
    a_pos = jnp.maximum(east, 0.0)
    b_neg = jnp.minimum(east, 0.0)
    c_pos = jnp.maximum(north[1:-1], 0.0)
    d_neg = jnp.minimum(north[1:-1], 0.0)
    flux_w = a_pos[1:] * widened[:, :-1] + b_neg[1:] * widened[:, 1:]
    inner = widened[:, 1:-1]
    flux_s = c_pos * below(inner) + d_neg * inner
    flux_n = above(flux_s)
    return inner - (flux_w[:, 1:] - flux_w[:, :-1]) - (flux_n - flux_s)


def adjoint_core(widened, east, north):
    a_pos = jnp.maximum(east, 0.0)
    b_neg = jnp.minimum(east, 0.0)[1:-1]
    c_pos = jnp.maximum(north[1:-1], 0.0)
    d_neg = jnp.minimum(north[1:-1], 0.0)
    a_east = a_pos[2:]
    c_north = above(c_pos)
    inner = widened[:, 1:-1]
    west_val = widened[:, :-2]
    east_val = widened[:, 2:]
    return (
        inner * (1.0 - a_east + b_neg - c_north + d_neg)
        - b_neg * west_val
        + a_east * east_val
        - d_neg * below(inner)
        + c_north * above(inner)
    )


def four_steps(state, east, north, weight):
    span = state.shape[1]
    for step in range(2):
        state = forward_core(state, east[step:span - step], north[step:span - step])
    state = weight[2:span - 2] * state
    for step in range(2, 4):
        state = adjoint_core(state, east[step:span - step], north[step:span - step])
    return state


def coarsen(sketch):
    probe_count, lon_count, level_count, lat_count = sketch.shape
    summed = sketch.reshape(probe_count, lon_count // 4, 4, level_count, lat_count).sum(axis=2)
    rows = lax.broadcasted_iota(jnp.int32, (lat_count, lat_count // 4), 0) // 4
    cols = lax.broadcasted_iota(jnp.int32, (lat_count, lat_count // 4), 1)
    average = jnp.where(rows == cols, 1.0 / 16.0, 0.0).astype(jnp.float32)
    coarse = jnp.dot(
        summed.reshape(-1, lat_count),
        average,
        precision=lax.Precision.HIGHEST,
        preferred_element_type=jnp.float32,
    )
    return coarse.reshape(probe_count, lon_count // 4, level_count, lat_count // 4)


def body(increments, winds, obs_weight):
    probe_count, lon_count, level_count, lat_count = increments.shape
    halo = 4
    pack = (increments, winds[0][None], lat_mask(winds[1])[None], obs_weight[None])
    count = lax.axis_size("lon")
    forward = [(i, (i + 1) % count) for i in range(count)]
    backward = [((i + 1) % count, i) for i in range(count)]
    west_edge = jnp.concatenate([part[:, lon_count - halo:] for part in pack], axis=0)
    east_edge = jnp.concatenate([part[:, :halo] for part in pack], axis=0)
    from_west = lax.ppermute(west_edge, "lon", forward)
    from_east = lax.ppermute(east_edge, "lon", backward)
    bounds = ((0, probe_count), (probe_count, probe_count + 1),
              (probe_count + 1, probe_count + 2), (probe_count + 2, probe_count + 3))

    def fields(parts):
        return parts[0], parts[1][0], parts[2][0], parts[3][0]

    inner = four_steps(*fields(pack))
    inner = coarsen(increments[:, halo:lon_count - halo] + inner)
    rim = [
        jnp.concatenate(
            [from_west[lo:hi], part[:, :2 * halo], part[:, lon_count - 2 * halo:], from_east[lo:hi]],
            axis=1,
        )
        for part, (lo, hi) in zip(pack, bounds)
    ]
    rim = four_steps(*fields(rim))
    west = coarsen(increments[:, :halo] + rim[:, :halo])
    east = coarsen(increments[:, lon_count - halo:] + rim[:, rim.shape[1] - halo:])
    coarse = jnp.concatenate([west, inner, east], axis=1)
    coarse = coarse.reshape(probe_count, -1)
    all_probes = probe_count * lax.axis_size("probe")
    ident = jnp.eye(all_probes, dtype=jnp.float32)
    full_panel = lax.all_gather(coarse, "probe", axis=0, tiled=True)
    local_gram = jnp.dot(
        full_panel,
        full_panel.T,
        precision=lax.Precision.HIGHEST,
        preferred_element_type=jnp.float32,
    )
    gram = butterfly_sum(local_gram, "lon")
    lower = jnp.linalg.cholesky(gram)
    inverse = lax.linalg.triangular_solve(lower, ident, left_side=True, lower=True)
    own_rows = lax.dynamic_slice_in_dim(
        inverse, lax.axis_index("probe") * probe_count, probe_count, 0
    )
    basis = jnp.dot(
        own_rows, full_panel, precision=lax.Precision.HIGHEST, preferred_element_type=jnp.float32
    )
    return (basis.reshape(probe_count, lon_count // 4, -1), lower.T)


def solution(mesh):
    in_specs = (P("probe", "lon", None, None), P(None, "lon", None, None), P("lon", None, None))
    out_specs = (P("probe", "lon", None), P())
    return jax.shard_map(body, mesh=mesh, in_specs=in_specs, out_specs=out_specs, check_vma=False)
```

```python
import functools

import jax
import jax.numpy as jnp
from jax import lax
from jax.experimental import pallas as pl
from jax.experimental.pallas import tpu as pltpu
from jax.sharding import PartitionSpec as P

MESH = pl.DeviceIdType.MESH


def from_behind(block, axis, distance):
    devices = range(lax.axis_size(axis))
    route = [((i - distance) % len(devices), i) for i in devices]
    return lax.ppermute(block, axis, route)


def exchange_kernel(count, radix, block_ref, out_ref, held, current, send_sem, recv_sem):
    me = lax.axis_index("lon")
    rounds = []
    stride = 1
    while stride < count:
        width = min(radix, count // stride)
        rounds.append((stride, width))
        stride *= width
    partners = [me ^ (j * stride) for stride, width in rounds for j in range(1, width)]

    barrier = pltpu.get_barrier_semaphore()
    for partner in partners:
        pl.semaphore_signal(barrier, inc=1, device_id={"lon": partner}, device_id_type=MESH)
    pl.semaphore_wait(barrier, len(partners))

    current[0] = block_ref[...]
    slot = 0
    for step, (stride, width) in enumerate(rounds):
        copies = []
        for j in range(1, width):
            copy = pltpu.make_async_remote_copy(
                src_ref=current.at[step],
                dst_ref=held.at[slot + j - 1],
                send_sem=send_sem.at[slot + j - 1],
                recv_sem=recv_sem.at[slot + j - 1],
                device_id={"lon": me ^ (j * stride)},
                device_id_type=MESH,
            )
            copy.start()
            copies.append(copy)
        for copy in copies:
            copy.wait()
        terms = [current[step]] + [held[slot + j - 1] for j in range(1, width)]
        while len(terms) > 1:
            terms = [terms[k] + terms[k + 1] for k in range(0, len(terms), 2)]
        current[step + 1] = terms[0]
        slot += width - 1
    out_ref[...] = current[len(rounds)]


def butterfly_sum(block, axis, radix=4):
    count = lax.axis_size(axis)
    if count & (count - 1) or count < 2:
        return lax.psum(block, axis)
    rounds = 0
    slots = 0
    stride = 1
    while stride < count:
        width = min(radix, count // stride)
        rounds += 1
        slots += width - 1
        stride *= width
    return pl.pallas_call(
        functools.partial(exchange_kernel, count, radix),
        out_shape=jax.ShapeDtypeStruct(block.shape, block.dtype),
        in_specs=[pl.BlockSpec(memory_space=pltpu.VMEM)],
        out_specs=pl.BlockSpec(memory_space=pltpu.VMEM),
        scratch_shapes=[
            pltpu.VMEM((slots,) + block.shape, block.dtype),
            pltpu.VMEM((rounds + 1,) + block.shape, block.dtype),
            pltpu.SemaphoreType.DMA((slots,)),
            pltpu.SemaphoreType.DMA((slots,)),
        ],
        compiler_params=pltpu.CompilerParams(collective_id=0, has_side_effects=True),
    )(block)


def padded(block, sides, width):
    for axis, dim in sides:
        count = lax.axis_size(axis)
        forward = [(i, i + 1) for i in range(count - 1)]
        forward.append((count - 1, 0))
        backward = [(target, source) for source, target in forward]
        low = lax.ppermute(
            lax.slice_in_dim(block, block.shape[dim] - width, None, axis=dim), axis, forward
        )
        high = lax.ppermute(lax.slice_in_dim(block, 0, width, axis=dim), axis, backward)
        block = jnp.concatenate([low, block, high], axis=dim)
    return block


def lat_mask(field):
    rows = lax.broadcasted_iota(jnp.int32, field.shape, field.ndim - 1)
    return jnp.where(rows > 0, field, jnp.zeros_like(field))


def below(field):
    return jnp.concatenate([jnp.zeros_like(field[..., :1]), field[..., :-1]], axis=-1)


def above(field):
    return jnp.concatenate([field[..., 1:], jnp.zeros_like(field[..., :1])], axis=-1)


def forward_core(widened, east, north):
    a_pos = jnp.maximum(east, 0.0)
    b_neg = jnp.minimum(east, 0.0)
    c_pos = jnp.maximum(north[1:-1], 0.0)
    d_neg = jnp.minimum(north[1:-1], 0.0)
    flux_w = a_pos[1:] * widened[:, :-1] + b_neg[1:] * widened[:, 1:]
    inner = widened[:, 1:-1]
    flux_s = c_pos * below(inner) + d_neg * inner
    flux_n = above(flux_s)
    return inner - (flux_w[:, 1:] - flux_w[:, :-1]) - (flux_n - flux_s)


def adjoint_core(widened, east, north):
    a_pos = jnp.maximum(east, 0.0)
    b_neg = jnp.minimum(east, 0.0)[1:-1]
    c_pos = jnp.maximum(north[1:-1], 0.0)
    d_neg = jnp.minimum(north[1:-1], 0.0)
    a_east = a_pos[2:]
    c_north = above(c_pos)
    inner = widened[:, 1:-1]
    west_val = widened[:, :-2]
    east_val = widened[:, 2:]
    return (
        inner * (1.0 - a_east + b_neg - c_north + d_neg)
        - b_neg * west_val
        + a_east * east_val
        - d_neg * below(inner)
        + c_north * above(inner)
    )


def four_steps(state, east, north, weight):
    span = state.shape[1]
    for step in range(2):
        state = forward_core(state, east[step:span - step], north[step:span - step])
    state = weight[2:span - 2] * state
    for step in range(2, 4):
        state = adjoint_core(state, east[step:span - step], north[step:span - step])
    return state


def coarsen(sketch):
    probe_count, lon_count, level_count, lat_count = sketch.shape
    summed = sketch.reshape(probe_count, lon_count // 4, 4, level_count, lat_count).sum(axis=2)
    rows = lax.broadcasted_iota(jnp.int32, (lat_count, lat_count // 4), 0) // 4
    cols = lax.broadcasted_iota(jnp.int32, (lat_count, lat_count // 4), 1)
    average = jnp.where(rows == cols, 1.0 / 16.0, 0.0).astype(jnp.float32)
    coarse = jnp.dot(
        summed.reshape(-1, lat_count),
        average,
        precision=lax.Precision.HIGHEST,
        preferred_element_type=jnp.float32,
    )
    return coarse.reshape(probe_count, lon_count // 4, level_count, lat_count // 4)


def lat_below(x, lanes):
    rolled = pltpu.roll(x, 1, x.ndim - 1)
    return jnp.where(lanes > 0, rolled, 0.0)


def lat_above(x, lanes):
    rolled = pltpu.roll(x, x.shape[-1] - 1, x.ndim - 1)
    return jnp.where(lanes < x.shape[-1] - 1, rolled, 0.0)


def stencil_kernel(q_ref, a_ref, b_ref, c_ref, d_ref, w_ref, o_ref):
    span = q_ref.shape[1]
    field = q_ref[0]
    lanes = lax.broadcasted_iota(jnp.int32, field.shape[1:], 1)[None]
    state = field
    for step in range(2):
        lo, hi = step, span - step
        east_a = a_ref[lo:hi]
        east_b = b_ref[lo:hi]
        north_c = c_ref[lo + 1:hi - 1]
        north_d = d_ref[lo + 1:hi - 1]
        flux_w = east_a[1:] * state[:-1] + east_b[1:] * state[1:]
        inner = state[1:-1]
        flux_s = north_c * lat_below(inner, lanes) + north_d * inner
        flux_n = lat_above(flux_s, lanes)
        state = inner - (flux_w[1:] - flux_w[:-1]) - (flux_n - flux_s)
    state = w_ref[2:span - 2] * state
    for step in range(2, 4):
        lo, hi = step, span - step
        west_b = b_ref[lo + 1:hi - 1]
        east_a = a_ref[lo + 2:hi]
        north_c = c_ref[lo + 1:hi - 1]
        north_d = d_ref[lo + 1:hi - 1]
        north_up = lat_above(north_c, lanes)
        inner = state[1:-1]
        state = (
            inner * (1.0 - east_a + west_b - north_up + north_d)
            - west_b * state[:-2]
            + east_a * state[2:]
            - north_d * lat_below(inner, lanes)
            + north_up * lat_above(inner, lanes)
        )
    sketch = field[4:span - 4] + state
    groups = sketch.shape[0] // 4
    for g in range(groups):
        o_ref[0, g] = ((sketch[4 * g] + sketch[4 * g + 1]) + sketch[4 * g + 2]) + sketch[4 * g + 3]


def stencil_sums(slab, east, north, weight):
    probe_count, span, level_count, lat_count = slab.shape
    groups = (span - 8) // 4
    winds = (
        jnp.maximum(east, 0.0),
        jnp.minimum(east, 0.0),
        jnp.maximum(north, 0.0),
        jnp.minimum(north, 0.0),
        weight,
    )
    full = pl.BlockSpec((span, level_count, lat_count), lambda i: (0, 0, 0))
    elements = probe_count * span * level_count * lat_count
    return pl.pallas_call(
        stencil_kernel,
        out_shape=jax.ShapeDtypeStruct((probe_count, groups, level_count, lat_count), slab.dtype),
        grid=(probe_count,),
        in_specs=[pl.BlockSpec((1, span, level_count, lat_count), lambda i: (i, 0, 0, 0))] + [full] * 5,
        out_specs=pl.BlockSpec((1, groups, level_count, lat_count), lambda i: (i, 0, 0, 0)),
        cost_estimate=pl.CostEstimate(
            flops=80 * elements, transcendentals=0, bytes_accessed=4 * elements + 20 * span * level_count * lat_count
        ),
    )(slab, *winds)


def lat_average(summed):
    probe_count, groups, level_count, lat_count = summed.shape
    rows = lax.broadcasted_iota(jnp.int32, (lat_count, lat_count // 4), 0) // 4
    cols = lax.broadcasted_iota(jnp.int32, (lat_count, lat_count // 4), 1)
    average = jnp.where(rows == cols, 1.0 / 16.0, 0.0).astype(jnp.float32)
    coarse = jnp.dot(
        summed.reshape(-1, lat_count),
        average,
        precision=lax.Precision.HIGHEST,
        preferred_element_type=jnp.float32,
    )
    return coarse.reshape(probe_count, groups, level_count, lat_count // 4)


def body(increments, winds, obs_weight):
    probe_count, lon_count, level_count, lat_count = increments.shape
    halo = 4
    pack = (increments, winds[0][None], lat_mask(winds[1])[None], obs_weight[None])
    count = lax.axis_size("lon")
    forward = [(i, (i + 1) % count) for i in range(count)]
    backward = [((i + 1) % count, i) for i in range(count)]
    west_edge = jnp.concatenate([part[:, lon_count - halo:] for part in pack], axis=0)
    east_edge = jnp.concatenate([part[:, :halo] for part in pack], axis=0)
    from_west = lax.ppermute(west_edge, "lon", forward)
    from_east = lax.ppermute(east_edge, "lon", backward)
    bounds = ((0, probe_count), (probe_count, probe_count + 1),
              (probe_count + 1, probe_count + 2), (probe_count + 2, probe_count + 3))

    def fields(parts):
        return parts[0], parts[1][0], parts[2][0], parts[3][0]

    inner = stencil_sums(*fields(pack))
    rim = [
        jnp.concatenate(
            [from_west[lo:hi], part[:, :2 * halo], part[:, lon_count - 2 * halo:], from_east[lo:hi]],
            axis=1,
        )
        for part, (lo, hi) in zip(pack, bounds)
    ]
    rim = stencil_sums(*fields(rim))
    summed = jnp.concatenate([rim[:, :1], inner, rim[:, rim.shape[1] - 1:]], axis=1)
    coarse = lat_average(summed)
    coarse = coarse.reshape(probe_count, -1)
    all_probes = probe_count * lax.axis_size("probe")
    ident = jnp.eye(all_probes, dtype=jnp.float32)
    full_panel = lax.all_gather(coarse, "probe", axis=0, tiled=True)
    local_gram = jnp.dot(
        full_panel,
        full_panel.T,
        precision=lax.Precision.HIGHEST,
        preferred_element_type=jnp.float32,
    )
    gram = butterfly_sum(local_gram, "lon")
    lower = jnp.linalg.cholesky(gram)
    inverse = lax.linalg.triangular_solve(lower, ident, left_side=True, lower=True)
    own_rows = lax.dynamic_slice_in_dim(
        inverse, lax.axis_index("probe") * probe_count, probe_count, 0
    )
    basis = jnp.dot(
        own_rows, full_panel, precision=lax.Precision.HIGHEST, preferred_element_type=jnp.float32
    )
    return (basis.reshape(probe_count, lon_count // 4, -1), lower.T)


def solution(mesh):
    in_specs = (P("probe", "lon", None, None), P(None, "lon", None, None), P("lon", None, None))
    out_specs = (P("probe", "lon", None), P())
    return jax.shard_map(body, mesh=mesh, in_specs=in_specs, out_specs=out_specs, check_vma=False)
```

```python
import functools

import jax
import jax.numpy as jnp
from jax import lax
from jax.experimental import pallas as pl
from jax.experimental.pallas import tpu as pltpu
from jax.sharding import PartitionSpec as P

MESH = pl.DeviceIdType.MESH


def from_behind(block, axis, distance):
    devices = range(lax.axis_size(axis))
    route = [((i - distance) % len(devices), i) for i in devices]
    return lax.ppermute(block, axis, route)


def exchange_kernel(count, radix, block_ref, out_ref, held, current, send_sem, recv_sem):
    me = lax.axis_index("lon")
    rounds = []
    stride = 1
    while stride < count:
        width = min(radix, count // stride)
        rounds.append((stride, width))
        stride *= width
    partners = [me ^ (j * stride) for stride, width in rounds for j in range(1, width)]

    barrier = pltpu.get_barrier_semaphore()
    for partner in partners:
        pl.semaphore_signal(barrier, inc=1, device_id={"lon": partner}, device_id_type=MESH)
    pl.semaphore_wait(barrier, len(partners))

    current[0] = block_ref[...]
    slot = 0
    for step, (stride, width) in enumerate(rounds):
        copies = []
        for j in range(1, width):
            copy = pltpu.make_async_remote_copy(
                src_ref=current.at[step],
                dst_ref=held.at[slot + j - 1],
                send_sem=send_sem.at[slot + j - 1],
                recv_sem=recv_sem.at[slot + j - 1],
                device_id={"lon": me ^ (j * stride)},
                device_id_type=MESH,
            )
            copy.start()
            copies.append(copy)
        for copy in copies:
            copy.wait()
        terms = [current[step]] + [held[slot + j - 1] for j in range(1, width)]
        while len(terms) > 1:
            terms = [terms[k] + terms[k + 1] for k in range(0, len(terms), 2)]
        current[step + 1] = terms[0]
        slot += width - 1
    out_ref[...] = current[len(rounds)]


def butterfly_sum(block, axis, radix=4):
    count = lax.axis_size(axis)
    if count & (count - 1) or count < 2:
        return lax.psum(block, axis)
    rounds = 0
    slots = 0
    stride = 1
    while stride < count:
        width = min(radix, count // stride)
        rounds += 1
        slots += width - 1
        stride *= width
    return pl.pallas_call(
        functools.partial(exchange_kernel, count, radix),
        out_shape=jax.ShapeDtypeStruct(block.shape, block.dtype),
        in_specs=[pl.BlockSpec(memory_space=pltpu.VMEM)],
        out_specs=pl.BlockSpec(memory_space=pltpu.VMEM),
        scratch_shapes=[
            pltpu.VMEM((slots,) + block.shape, block.dtype),
            pltpu.VMEM((rounds + 1,) + block.shape, block.dtype),
            pltpu.SemaphoreType.DMA((slots,)),
            pltpu.SemaphoreType.DMA((slots,)),
        ],
        compiler_params=pltpu.CompilerParams(collective_id=0, has_side_effects=True),
    )(block)


def padded(block, sides, width):
    for axis, dim in sides:
        count = lax.axis_size(axis)
        forward = [(i, i + 1) for i in range(count - 1)]
        forward.append((count - 1, 0))
        backward = [(target, source) for source, target in forward]
        low = lax.ppermute(
            lax.slice_in_dim(block, block.shape[dim] - width, None, axis=dim), axis, forward
        )
        high = lax.ppermute(lax.slice_in_dim(block, 0, width, axis=dim), axis, backward)
        block = jnp.concatenate([low, block, high], axis=dim)
    return block


def lat_mask(field):
    rows = lax.broadcasted_iota(jnp.int32, field.shape, field.ndim - 1)
    return jnp.where(rows > 0, field, jnp.zeros_like(field))


def below(field):
    return jnp.concatenate([jnp.zeros_like(field[..., :1]), field[..., :-1]], axis=-1)


def above(field):
    return jnp.concatenate([field[..., 1:], jnp.zeros_like(field[..., :1])], axis=-1)


def forward_core(widened, east, north):
    a_pos = jnp.maximum(east, 0.0)
    b_neg = jnp.minimum(east, 0.0)
    c_pos = jnp.maximum(north[1:-1], 0.0)
    d_neg = jnp.minimum(north[1:-1], 0.0)
    flux_w = a_pos[1:] * widened[:, :-1] + b_neg[1:] * widened[:, 1:]
    inner = widened[:, 1:-1]
    flux_s = c_pos * below(inner) + d_neg * inner
    flux_n = above(flux_s)
    return inner - (flux_w[:, 1:] - flux_w[:, :-1]) - (flux_n - flux_s)


def adjoint_core(widened, east, north):
    a_pos = jnp.maximum(east, 0.0)
    b_neg = jnp.minimum(east, 0.0)[1:-1]
    c_pos = jnp.maximum(north[1:-1], 0.0)
    d_neg = jnp.minimum(north[1:-1], 0.0)
    a_east = a_pos[2:]
    c_north = above(c_pos)
    inner = widened[:, 1:-1]
    west_val = widened[:, :-2]
    east_val = widened[:, 2:]
    return (
        inner * (1.0 - a_east + b_neg - c_north + d_neg)
        - b_neg * west_val
        + a_east * east_val
        - d_neg * below(inner)
        + c_north * above(inner)
    )


def four_steps(state, east, north, weight):
    span = state.shape[1]
    for step in range(2):
        state = forward_core(state, east[step:span - step], north[step:span - step])
    state = weight[2:span - 2] * state
    for step in range(2, 4):
        state = adjoint_core(state, east[step:span - step], north[step:span - step])
    return state


def coarsen(sketch):
    probe_count, lon_count, level_count, lat_count = sketch.shape
    summed = sketch.reshape(probe_count, lon_count // 4, 4, level_count, lat_count).sum(axis=2)
    rows = lax.broadcasted_iota(jnp.int32, (lat_count, lat_count // 4), 0) // 4
    cols = lax.broadcasted_iota(jnp.int32, (lat_count, lat_count // 4), 1)
    average = jnp.where(rows == cols, 1.0 / 16.0, 0.0).astype(jnp.float32)
    coarse = jnp.dot(
        summed.reshape(-1, lat_count),
        average,
        precision=lax.Precision.HIGHEST,
        preferred_element_type=jnp.float32,
    )
    return coarse.reshape(probe_count, lon_count // 4, level_count, lat_count // 4)


def stencil_kernel(q_ref, a_ref, b_ref, c_ref, d_ref, w_ref, n_ref, k_ref, o_ref):
    span = q_ref.shape[1]
    lat = q_ref.shape[-1]
    field = q_ref[0]
    state = field
    for step in range(2):
        lo, hi = step, span - step
        east_a = a_ref[lo:hi]
        east_b = b_ref[lo:hi]
        north_c = c_ref[lo + 1:hi - 1]
        north_d = d_ref[lo + 1:hi - 1]
        flux_w = east_a[1:] * state[:-1] + east_b[1:] * state[1:]
        inner = state[1:-1]
        flux_s = north_c * pltpu.roll(inner, 1, 2) + north_d * inner
        flux_n = pltpu.roll(flux_s, lat - 1, 2)
        state = inner - (flux_w[1:] - flux_w[:-1]) - (flux_n - flux_s)
    state = w_ref[2:span - 2] * state
    for step in range(2, 4):
        lo, hi = step, span - step
        west_b = b_ref[lo + 1:hi - 1]
        east_a = a_ref[lo + 2:hi]
        north_d = d_ref[lo + 1:hi - 1]
        north_up = n_ref[lo + 1:hi - 1]
        inner = state[1:-1]
        state = (
            inner * k_ref[lo + 1:hi - 1]
            - west_b * state[:-2]
            + east_a * state[2:]
            - north_d * pltpu.roll(inner, 1, 2)
            + north_up * pltpu.roll(inner, lat - 1, 2)
        )
    sketch = field[4:span - 4] + state
    groups = sketch.shape[0] // 4
    for g in range(groups):
        o_ref[0, g] = ((sketch[4 * g] + sketch[4 * g + 1]) + sketch[4 * g + 2]) + sketch[4 * g + 3]


def stencil_sums(slab, east, north, weight):
    probe_count, span, level_count, lat_count = slab.shape
    groups = (span - 8) // 4
    east_a = jnp.maximum(east, 0.0)
    east_b = jnp.minimum(east, 0.0)
    north_c = jnp.maximum(north, 0.0)
    north_d = jnp.minimum(north, 0.0)
    north_up = above(north_c)
    next_a = jnp.concatenate([east_a[1:], jnp.zeros_like(east_a[:1])], axis=0)
    centre = 1.0 - next_a + east_b - north_up + north_d
    winds = (east_a, east_b, north_c, north_d, weight, north_up, centre)
    full = pl.BlockSpec((span, level_count, lat_count), lambda i: (0, 0, 0))
    elements = probe_count * span * level_count * lat_count
    return pl.pallas_call(
        stencil_kernel,
        out_shape=jax.ShapeDtypeStruct((probe_count, groups, level_count, lat_count), slab.dtype),
        grid=(probe_count,),
        in_specs=[pl.BlockSpec((1, span, level_count, lat_count), lambda i: (i, 0, 0, 0))] + [full] * 7,
        out_specs=pl.BlockSpec((1, groups, level_count, lat_count), lambda i: (i, 0, 0, 0)),
        cost_estimate=pl.CostEstimate(
            flops=50 * elements, transcendentals=0, bytes_accessed=4 * elements + 28 * span * level_count * lat_count
        ),
    )(slab, *winds)


def lat_average(summed):
    probe_count, groups, level_count, lat_count = summed.shape
    rows = lax.broadcasted_iota(jnp.int32, (lat_count, lat_count // 4), 0) // 4
    cols = lax.broadcasted_iota(jnp.int32, (lat_count, lat_count // 4), 1)
    average = jnp.where(rows == cols, 1.0 / 16.0, 0.0).astype(jnp.float32)
    coarse = jnp.dot(
        summed.reshape(-1, lat_count),
        average,
        precision=lax.Precision.HIGHEST,
        preferred_element_type=jnp.float32,
    )
    return coarse.reshape(probe_count, groups, level_count, lat_count // 4)


def body(increments, winds, obs_weight):
    probe_count, lon_count, level_count, lat_count = increments.shape
    halo = 4
    pack = (increments, winds[0][None], lat_mask(winds[1])[None], obs_weight[None])
    count = lax.axis_size("lon")
    forward = [(i, (i + 1) % count) for i in range(count)]
    backward = [((i + 1) % count, i) for i in range(count)]
    west_edge = jnp.concatenate([part[:, lon_count - halo:] for part in pack], axis=0)
    east_edge = jnp.concatenate([part[:, :halo] for part in pack], axis=0)
    from_west = lax.ppermute(west_edge, "lon", forward)
    from_east = lax.ppermute(east_edge, "lon", backward)
    bounds = ((0, probe_count), (probe_count, probe_count + 1),
              (probe_count + 1, probe_count + 2), (probe_count + 2, probe_count + 3))

    def fields(parts):
        return parts[0], parts[1][0], parts[2][0], parts[3][0]

    inner = stencil_sums(*fields(pack))
    rim = [
        jnp.concatenate(
            [from_west[lo:hi], part[:, :2 * halo], part[:, lon_count - 2 * halo:], from_east[lo:hi]],
            axis=1,
        )
        for part, (lo, hi) in zip(pack, bounds)
    ]
    rim = stencil_sums(*fields(rim))
    summed = jnp.concatenate([rim[:, :1], inner, rim[:, rim.shape[1] - 1:]], axis=1)
    coarse = lat_average(summed)
    coarse = coarse.reshape(probe_count, -1)
    all_probes = probe_count * lax.axis_size("probe")
    ident = jnp.eye(all_probes, dtype=jnp.float32)
    full_panel = lax.all_gather(coarse, "probe", axis=0, tiled=True)
    local_gram = jnp.dot(
        full_panel,
        full_panel.T,
        precision=lax.Precision.HIGHEST,
        preferred_element_type=jnp.float32,
    )
    gram = butterfly_sum(local_gram, "lon")
    lower = jnp.linalg.cholesky(gram)
    inverse = lax.linalg.triangular_solve(lower, ident, left_side=True, lower=True)
    own_rows = lax.dynamic_slice_in_dim(
        inverse, lax.axis_index("probe") * probe_count, probe_count, 0
    )
    basis = jnp.dot(
        own_rows, full_panel, precision=lax.Precision.HIGHEST, preferred_element_type=jnp.float32
    )
    return (basis.reshape(probe_count, lon_count // 4, -1), lower.T)


def solution(mesh):
    in_specs = (P("probe", "lon", None, None), P(None, "lon", None, None), P("lon", None, None))
    out_specs = (P("probe", "lon", None), P())
    return jax.shard_map(body, mesh=mesh, in_specs=in_specs, out_specs=out_specs, check_vma=False)
```

```python
import functools

import jax
import jax.numpy as jnp
from jax import lax
from jax.experimental import pallas as pl
from jax.experimental.pallas import tpu as pltpu
from jax.sharding import PartitionSpec as P

MESH = pl.DeviceIdType.MESH


def from_behind(block, axis, distance):
    devices = range(lax.axis_size(axis))
    route = [((i - distance) % len(devices), i) for i in devices]
    return lax.ppermute(block, axis, route)


def exchange_kernel(count, radix, block_ref, out_ref, held, current, send_sem, recv_sem):
    me = lax.axis_index("lon")
    rounds = []
    stride = 1
    while stride < count:
        width = min(radix, count // stride)
        rounds.append((stride, width))
        stride *= width
    partners = [me ^ (j * stride) for stride, width in rounds for j in range(1, width)]

    barrier = pltpu.get_barrier_semaphore()
    for partner in partners:
        pl.semaphore_signal(barrier, inc=1, device_id={"lon": partner}, device_id_type=MESH)
    pl.semaphore_wait(barrier, len(partners))

    current[0] = block_ref[...]
    slot = 0
    for step, (stride, width) in enumerate(rounds):
        copies = []
        for j in range(1, width):
            copy = pltpu.make_async_remote_copy(
                src_ref=current.at[step],
                dst_ref=held.at[slot + j - 1],
                send_sem=send_sem.at[slot + j - 1],
                recv_sem=recv_sem.at[slot + j - 1],
                device_id={"lon": me ^ (j * stride)},
                device_id_type=MESH,
            )
            copy.start()
            copies.append(copy)
        for copy in copies:
            copy.wait()
        terms = [current[step]] + [held[slot + j - 1] for j in range(1, width)]
        while len(terms) > 1:
            terms = [terms[k] + terms[k + 1] for k in range(0, len(terms), 2)]
        current[step + 1] = terms[0]
        slot += width - 1
    out_ref[...] = current[len(rounds)]


def butterfly_sum(block, axis, radix=8):
    count = lax.axis_size(axis)
    if count & (count - 1) or count < 2:
        return lax.psum(block, axis)
    rounds = 0
    slots = 0
    stride = 1
    while stride < count:
        width = min(radix, count // stride)
        rounds += 1
        slots += width - 1
        stride *= width
    return pl.pallas_call(
        functools.partial(exchange_kernel, count, radix),
        out_shape=jax.ShapeDtypeStruct(block.shape, block.dtype),
        in_specs=[pl.BlockSpec(memory_space=pltpu.VMEM)],
        out_specs=pl.BlockSpec(memory_space=pltpu.VMEM),
        scratch_shapes=[
            pltpu.VMEM((slots,) + block.shape, block.dtype),
            pltpu.VMEM((rounds + 1,) + block.shape, block.dtype),
            pltpu.SemaphoreType.DMA((slots,)),
            pltpu.SemaphoreType.DMA((slots,)),
        ],
        compiler_params=pltpu.CompilerParams(collective_id=0, has_side_effects=True),
    )(block)


def padded(block, sides, width):
    for axis, dim in sides:
        count = lax.axis_size(axis)
        forward = [(i, i + 1) for i in range(count - 1)]
        forward.append((count - 1, 0))
        backward = [(target, source) for source, target in forward]
        low = lax.ppermute(
            lax.slice_in_dim(block, block.shape[dim] - width, None, axis=dim), axis, forward
        )
        high = lax.ppermute(lax.slice_in_dim(block, 0, width, axis=dim), axis, backward)
        block = jnp.concatenate([low, block, high], axis=dim)
    return block


def lat_mask(field):
    rows = lax.broadcasted_iota(jnp.int32, field.shape, field.ndim - 1)
    return jnp.where(rows > 0, field, jnp.zeros_like(field))


def below(field):
    return jnp.concatenate([jnp.zeros_like(field[..., :1]), field[..., :-1]], axis=-1)


def above(field):
    return jnp.concatenate([field[..., 1:], jnp.zeros_like(field[..., :1])], axis=-1)


def forward_core(widened, east, north):
    a_pos = jnp.maximum(east, 0.0)
    b_neg = jnp.minimum(east, 0.0)
    c_pos = jnp.maximum(north[1:-1], 0.0)
    d_neg = jnp.minimum(north[1:-1], 0.0)
    flux_w = a_pos[1:] * widened[:, :-1] + b_neg[1:] * widened[:, 1:]
    inner = widened[:, 1:-1]
    flux_s = c_pos * below(inner) + d_neg * inner
    flux_n = above(flux_s)
    return inner - (flux_w[:, 1:] - flux_w[:, :-1]) - (flux_n - flux_s)


def adjoint_core(widened, east, north):
    a_pos = jnp.maximum(east, 0.0)
    b_neg = jnp.minimum(east, 0.0)[1:-1]
    c_pos = jnp.maximum(north[1:-1], 0.0)
    d_neg = jnp.minimum(north[1:-1], 0.0)
    a_east = a_pos[2:]
    c_north = above(c_pos)
    inner = widened[:, 1:-1]
    west_val = widened[:, :-2]
    east_val = widened[:, 2:]
    return (
        inner * (1.0 - a_east + b_neg - c_north + d_neg)
        - b_neg * west_val
        + a_east * east_val
        - d_neg * below(inner)
        + c_north * above(inner)
    )


def four_steps(state, east, north, weight):
    span = state.shape[1]
    for step in range(2):
        state = forward_core(state, east[step:span - step], north[step:span - step])
    state = weight[2:span - 2] * state
    for step in range(2, 4):
        state = adjoint_core(state, east[step:span - step], north[step:span - step])
    return state


def coarsen(sketch):
    probe_count, lon_count, level_count, lat_count = sketch.shape
    summed = sketch.reshape(probe_count, lon_count // 4, 4, level_count, lat_count).sum(axis=2)
    rows = lax.broadcasted_iota(jnp.int32, (lat_count, lat_count // 4), 0) // 4
    cols = lax.broadcasted_iota(jnp.int32, (lat_count, lat_count // 4), 1)
    average = jnp.where(rows == cols, 1.0 / 16.0, 0.0).astype(jnp.float32)
    coarse = jnp.dot(
        summed.reshape(-1, lat_count),
        average,
        precision=lax.Precision.HIGHEST,
        preferred_element_type=jnp.float32,
    )
    return coarse.reshape(probe_count, lon_count // 4, level_count, lat_count // 4)


def body(increments, winds, obs_weight):
    probe_count, lon_count, level_count, lat_count = increments.shape
    halo = 4
    pack = (increments, winds[0][None], lat_mask(winds[1])[None], obs_weight[None])
    count = lax.axis_size("lon")
    forward = [(i, (i + 1) % count) for i in range(count)]
    backward = [((i + 1) % count, i) for i in range(count)]
    west_edge = jnp.concatenate([part[:, lon_count - halo:] for part in pack], axis=0)
    east_edge = jnp.concatenate([part[:, :halo] for part in pack], axis=0)
    from_west = lax.ppermute(west_edge, "lon", forward)
    from_east = lax.ppermute(east_edge, "lon", backward)
    bounds = ((0, probe_count), (probe_count, probe_count + 1),
              (probe_count + 1, probe_count + 2), (probe_count + 2, probe_count + 3))

    def fields(parts):
        return parts[0], parts[1][0], parts[2][0], parts[3][0]

    inner = four_steps(*fields(pack))
    inner = coarsen(increments[:, halo:lon_count - halo] + inner)
    rim = [
        jnp.concatenate(
            [from_west[lo:hi], part[:, :2 * halo], part[:, lon_count - 2 * halo:], from_east[lo:hi]],
            axis=1,
        )
        for part, (lo, hi) in zip(pack, bounds)
    ]
    rim = four_steps(*fields(rim))
    west = coarsen(increments[:, :halo] + rim[:, :halo])
    east = coarsen(increments[:, lon_count - halo:] + rim[:, rim.shape[1] - halo:])
    coarse = jnp.concatenate([west, inner, east], axis=1)
    coarse = coarse.reshape(probe_count, -1)
    all_probes = probe_count * lax.axis_size("probe")
    ident = jnp.eye(all_probes, dtype=jnp.float32)
    full_panel = lax.all_gather(coarse, "probe", axis=0, tiled=True)
    local_gram = jnp.dot(
        full_panel,
        full_panel.T,
        precision=lax.Precision.HIGHEST,
        preferred_element_type=jnp.float32,
    )
    gram = butterfly_sum(local_gram, "lon")
    lower = jnp.linalg.cholesky(gram)
    inverse = lax.linalg.triangular_solve(lower, ident, left_side=True, lower=True)
    own_rows = lax.dynamic_slice_in_dim(
        inverse, lax.axis_index("probe") * probe_count, probe_count, 0
    )
    basis = jnp.dot(
        own_rows, full_panel, precision=lax.Precision.HIGHEST, preferred_element_type=jnp.float32
    )
    return (basis.reshape(probe_count, lon_count // 4, -1), lower.T)


def solution(mesh):
    in_specs = (P("probe", "lon", None, None), P(None, "lon", None, None), P("lon", None, None))
    out_specs = (P("probe", "lon", None), P())
    return jax.shard_map(body, mesh=mesh, in_specs=in_specs, out_specs=out_specs, check_vma=False)
```

```python
import functools

import jax
import jax.numpy as jnp
from jax import lax
from jax.experimental import pallas as pl
from jax.experimental.pallas import tpu as pltpu
from jax.sharding import PartitionSpec as P

MESH = pl.DeviceIdType.MESH


def from_behind(block, axis, distance):
    devices = range(lax.axis_size(axis))
    route = [((i - distance) % len(devices), i) for i in devices]
    return lax.ppermute(block, axis, route)


def exchange_kernel(count, radix, block_ref, out_ref, held, current, send_sem, recv_sem):
    me = lax.axis_index("lon")
    rounds = []
    stride = 1
    while stride < count:
        width = min(radix, count // stride)
        rounds.append((stride, width))
        stride *= width
    partners = [me ^ (j * stride) for stride, width in rounds for j in range(1, width)]

    barrier = pltpu.get_barrier_semaphore()
    for partner in partners:
        pl.semaphore_signal(barrier, inc=1, device_id={"lon": partner}, device_id_type=MESH)
    pl.semaphore_wait(barrier, len(partners))

    current[0] = block_ref[...]
    slot = 0
    for step, (stride, width) in enumerate(rounds):
        copies = []
        for j in range(1, width):
            copy = pltpu.make_async_remote_copy(
                src_ref=current.at[step],
                dst_ref=held.at[slot + j - 1],
                send_sem=send_sem.at[slot + j - 1],
                recv_sem=recv_sem.at[slot + j - 1],
                device_id={"lon": me ^ (j * stride)},
                device_id_type=MESH,
            )
            copy.start()
            copies.append(copy)
        for copy in copies:
            copy.wait()
        terms = [current[step]] + [held[slot + j - 1] for j in range(1, width)]
        while len(terms) > 1:
            terms = [terms[k] + terms[k + 1] for k in range(0, len(terms), 2)]
        current[step + 1] = terms[0]
        slot += width - 1
    out_ref[...] = current[len(rounds)]


def butterfly_sum(block, axis, radix=4):
    count = lax.axis_size(axis)
    if count & (count - 1) or count < 2:
        return lax.psum(block, axis)
    rounds = 0
    slots = 0
    stride = 1
    while stride < count:
        width = min(radix, count // stride)
        rounds += 1
        slots += width - 1
        stride *= width
    return pl.pallas_call(
        functools.partial(exchange_kernel, count, radix),
        out_shape=jax.ShapeDtypeStruct(block.shape, block.dtype),
        in_specs=[pl.BlockSpec(memory_space=pltpu.VMEM)],
        out_specs=pl.BlockSpec(memory_space=pltpu.VMEM),
        scratch_shapes=[
            pltpu.VMEM((slots,) + block.shape, block.dtype),
            pltpu.VMEM((rounds + 1,) + block.shape, block.dtype),
            pltpu.SemaphoreType.DMA((slots,)),
            pltpu.SemaphoreType.DMA((slots,)),
        ],
        compiler_params=pltpu.CompilerParams(collective_id=0, has_side_effects=True),
    )(block)


def padded(block, sides, width):
    for axis, dim in sides:
        count = lax.axis_size(axis)
        forward = [(i, i + 1) for i in range(count - 1)]
        forward.append((count - 1, 0))
        backward = [(target, source) for source, target in forward]
        low = lax.ppermute(
            lax.slice_in_dim(block, block.shape[dim] - width, None, axis=dim), axis, forward
        )
        high = lax.ppermute(lax.slice_in_dim(block, 0, width, axis=dim), axis, backward)
        block = jnp.concatenate([low, block, high], axis=dim)
    return block


def lat_mask(field):
    rows = lax.broadcasted_iota(jnp.int32, field.shape, field.ndim - 1)
    return jnp.where(rows > 0, field, jnp.zeros_like(field))


def below(field):
    return jnp.concatenate([jnp.zeros_like(field[..., :1]), field[..., :-1]], axis=-1)


def above(field):
    return jnp.concatenate([field[..., 1:], jnp.zeros_like(field[..., :1])], axis=-1)


def forward_core(widened, east, north):
    a_pos = jnp.maximum(east, 0.0)
    b_neg = jnp.minimum(east, 0.0)
    c_pos = jnp.maximum(north[1:-1], 0.0)
    d_neg = jnp.minimum(north[1:-1], 0.0)
    flux_w = a_pos[1:] * widened[:, :-1] + b_neg[1:] * widened[:, 1:]
    inner = widened[:, 1:-1]
    flux_s = c_pos * below(inner) + d_neg * inner
    flux_n = above(flux_s)
    return inner - (flux_w[:, 1:] - flux_w[:, :-1]) - (flux_n - flux_s)


def adjoint_core(widened, east, north):
    a_pos = jnp.maximum(east, 0.0)
    b_neg = jnp.minimum(east, 0.0)[1:-1]
    c_pos = jnp.maximum(north[1:-1], 0.0)
    d_neg = jnp.minimum(north[1:-1], 0.0)
    a_east = a_pos[2:]
    c_north = above(c_pos)
    inner = widened[:, 1:-1]
    west_val = widened[:, :-2]
    east_val = widened[:, 2:]
    return (
        inner * (1.0 - a_east + b_neg - c_north + d_neg)
        - b_neg * west_val
        + a_east * east_val
        - d_neg * below(inner)
        + c_north * above(inner)
    )


def four_steps(state, east, north, weight):
    a = jnp.maximum(east, 0.0)
    b = jnp.minimum(east, 0.0)
    c = jnp.maximum(north, 0.0)
    d = jnp.minimum(north, 0.0)
    a_east = jnp.roll(a, -1, axis=0)
    b_east = jnp.roll(b, -1, axis=0)
    c_north = above(c)
    d_north = above(d)
    centre = 1.0 - a_east + b - c_north + d
    for step in range(2):
        west_val = jnp.roll(state, 1, axis=1)
        east_val = jnp.roll(state, -1, axis=1)
        flux_w = a * west_val + b * state
        flux_e = a_east * state + b_east * east_val
        flux_s = c * below(state) + d * state
        flux_n = c_north * state + d_north * above(state)
        state = state - (flux_e - flux_w) - (flux_n - flux_s)
    state = weight * state
    for step in range(2):
        west_val = jnp.roll(state, 1, axis=1)
        east_val = jnp.roll(state, -1, axis=1)
        state = (
            state * centre
            - b * west_val
            + a_east * east_val
            - d * below(state)
            + c_north * above(state)
        )
    return state


def coarsen(sketch):
    probe_count, lon_count, level_count, lat_count = sketch.shape
    summed = sketch.reshape(probe_count, lon_count // 4, 4, level_count, lat_count).sum(axis=2)
    rows = lax.broadcasted_iota(jnp.int32, (lat_count, lat_count // 4), 0) // 4
    cols = lax.broadcasted_iota(jnp.int32, (lat_count, lat_count // 4), 1)
    average = jnp.where(rows == cols, 1.0 / 16.0, 0.0).astype(jnp.float32)
    coarse = jnp.dot(
        summed.reshape(-1, lat_count),
        average,
        precision=lax.Precision.HIGHEST,
        preferred_element_type=jnp.float32,
    )
    return coarse.reshape(probe_count, lon_count // 4, level_count, lat_count // 4)


def body(increments, winds, obs_weight):
    probe_count, lon_count, level_count, lat_count = increments.shape
    halo = 4
    pack = (increments, winds[0][None], lat_mask(winds[1])[None], obs_weight[None])
    count = lax.axis_size("lon")
    forward = [(i, (i + 1) % count) for i in range(count)]
    backward = [((i + 1) % count, i) for i in range(count)]
    west_edge = jnp.concatenate([part[:, lon_count - halo:] for part in pack], axis=0)
    east_edge = jnp.concatenate([part[:, :halo] for part in pack], axis=0)
    from_west = lax.ppermute(west_edge, "lon", forward)
    from_east = lax.ppermute(east_edge, "lon", backward)
    bounds = ((0, probe_count), (probe_count, probe_count + 1),
              (probe_count + 1, probe_count + 2), (probe_count + 2, probe_count + 3))

    def fields(parts):
        return parts[0], parts[1][0], parts[2][0], parts[3][0]

    inner = four_steps(*fields(pack))
    inner = coarsen(increments[:, halo:lon_count - halo] + inner[:, halo:lon_count - halo])
    rim = [
        jnp.concatenate(
            [from_west[lo:hi], part[:, :2 * halo], part[:, lon_count - 2 * halo:], from_east[lo:hi]],
            axis=1,
        )
        for part, (lo, hi) in zip(pack, bounds)
    ]
    rim = four_steps(*fields(rim))
    west = coarsen(increments[:, :halo] + rim[:, halo:2 * halo])
    east = coarsen(increments[:, lon_count - halo:] + rim[:, 4 * halo:5 * halo])
    coarse = jnp.concatenate([west, inner, east], axis=1)
    coarse = coarse.reshape(probe_count, -1)
    all_probes = probe_count * lax.axis_size("probe")
    ident = jnp.eye(all_probes, dtype=jnp.float32)
    full_panel = lax.all_gather(coarse, "probe", axis=0, tiled=True)
    local_gram = jnp.dot(
        full_panel,
        full_panel.T,
        precision=lax.Precision.HIGHEST,
        preferred_element_type=jnp.float32,
    )
    gram = butterfly_sum(local_gram, "lon")
    lower = jnp.linalg.cholesky(gram)
    inverse = lax.linalg.triangular_solve(lower, ident, left_side=True, lower=True)
    own_rows = lax.dynamic_slice_in_dim(
        inverse, lax.axis_index("probe") * probe_count, probe_count, 0
    )
    basis = jnp.dot(
        own_rows, full_panel, precision=lax.Precision.HIGHEST, preferred_element_type=jnp.float32
    )
    return (basis.reshape(probe_count, lon_count // 4, -1), lower.T)


def solution(mesh):
    in_specs = (P("probe", "lon", None, None), P(None, "lon", None, None), P("lon", None, None))
    out_specs = (P("probe", "lon", None), P())
    return jax.shard_map(body, mesh=mesh, in_specs=in_specs, out_specs=out_specs, check_vma=False)
```

```python
import functools

import jax
import jax.numpy as jnp
from jax import lax
from jax.experimental import pallas as pl
from jax.experimental.pallas import tpu as pltpu
from jax.sharding import PartitionSpec as P

MESH = pl.DeviceIdType.MESH


def from_behind(block, axis, distance):
    devices = range(lax.axis_size(axis))
    route = [((i - distance) % len(devices), i) for i in devices]
    return lax.ppermute(block, axis, route)


def exchange_kernel(count, radix, block_ref, out_ref, held, current, send_sem, recv_sem):
    me = lax.axis_index("lon")
    rounds = []
    stride = 1
    while stride < count:
        width = min(radix, count // stride)
        rounds.append((stride, width))
        stride *= width
    partners = [me ^ (j * stride) for stride, width in rounds for j in range(1, width)]

    barrier = pltpu.get_barrier_semaphore()
    for partner in partners:
        pl.semaphore_signal(barrier, inc=1, device_id={"lon": partner}, device_id_type=MESH)
    pl.semaphore_wait(barrier, len(partners))

    current[0] = block_ref[...]
    slot = 0
    for step, (stride, width) in enumerate(rounds):
        copies = []
        for j in range(1, width):
            copy = pltpu.make_async_remote_copy(
                src_ref=current.at[step],
                dst_ref=held.at[slot + j - 1],
                send_sem=send_sem.at[slot + j - 1],
                recv_sem=recv_sem.at[slot + j - 1],
                device_id={"lon": me ^ (j * stride)},
                device_id_type=MESH,
            )
            copy.start()
            copies.append(copy)
        for copy in copies:
            copy.wait()
        terms = [current[step]] + [held[slot + j - 1] for j in range(1, width)]
        while len(terms) > 1:
            terms = [terms[k] + terms[k + 1] for k in range(0, len(terms), 2)]
        current[step + 1] = terms[0]
        slot += width - 1
    out_ref[...] = current[len(rounds)]


def halo_kernel(west_ref, east_ref, from_west_ref, from_east_ref, held, send_sem, recv_sem):
    count = lax.axis_size("lon")
    me = lax.axis_index("lon")
    right = lax.rem(me + 1, count)
    left = lax.rem(me + count - 1, count)

    barrier = pltpu.get_barrier_semaphore()
    for neighbour in (left, right):
        pl.semaphore_signal(barrier, inc=1, device_id={"lon": neighbour}, device_id_type=MESH)
    pl.semaphore_wait(barrier, 2)

    copies = []
    for slot, (source, target) in enumerate(((west_ref, right), (east_ref, left))):
        copy = pltpu.make_async_remote_copy(
            src_ref=source,
            dst_ref=held.at[slot],
            send_sem=send_sem.at[slot],
            recv_sem=recv_sem.at[slot],
            device_id={"lon": target},
            device_id_type=MESH,
        )
        copy.start()
        copies.append(copy)
    for copy in copies:
        copy.wait()
    from_west_ref[...] = held[0]
    from_east_ref[...] = held[1]


def exchange_halos(west_edge, east_edge):
    vmem = pl.BlockSpec(memory_space=pltpu.VMEM)
    edge = jax.ShapeDtypeStruct(west_edge.shape, west_edge.dtype)
    return pl.pallas_call(
        halo_kernel,
        out_shape=(edge, edge),
        in_specs=[vmem, vmem],
        out_specs=(vmem, vmem),
        scratch_shapes=[
            pltpu.VMEM((2,) + west_edge.shape, west_edge.dtype),
            pltpu.SemaphoreType.DMA((2,)),
            pltpu.SemaphoreType.DMA((2,)),
        ],
        compiler_params=pltpu.CompilerParams(collective_id=1, has_side_effects=True),
    )(west_edge, east_edge)


def butterfly_sum(block, axis, radix=4):
    count = lax.axis_size(axis)
    if count & (count - 1) or count < 2:
        return lax.psum(block, axis)
    rounds = 0
    slots = 0
    stride = 1
    while stride < count:
        width = min(radix, count // stride)
        rounds += 1
        slots += width - 1
        stride *= width
    return pl.pallas_call(
        functools.partial(exchange_kernel, count, radix),
        out_shape=jax.ShapeDtypeStruct(block.shape, block.dtype),
        in_specs=[pl.BlockSpec(memory_space=pltpu.VMEM)],
        out_specs=pl.BlockSpec(memory_space=pltpu.VMEM),
        scratch_shapes=[
            pltpu.VMEM((slots,) + block.shape, block.dtype),
            pltpu.VMEM((rounds + 1,) + block.shape, block.dtype),
            pltpu.SemaphoreType.DMA((slots,)),
            pltpu.SemaphoreType.DMA((slots,)),
        ],
        compiler_params=pltpu.CompilerParams(collective_id=0, has_side_effects=True),
    )(block)


def padded(block, sides, width):
    for axis, dim in sides:
        count = lax.axis_size(axis)
        forward = [(i, i + 1) for i in range(count - 1)]
        forward.append((count - 1, 0))
        backward = [(target, source) for source, target in forward]
        low = lax.ppermute(
            lax.slice_in_dim(block, block.shape[dim] - width, None, axis=dim), axis, forward
        )
        high = lax.ppermute(lax.slice_in_dim(block, 0, width, axis=dim), axis, backward)
        block = jnp.concatenate([low, block, high], axis=dim)
    return block


def lat_mask(field):
    rows = lax.broadcasted_iota(jnp.int32, field.shape, field.ndim - 1)
    return jnp.where(rows > 0, field, jnp.zeros_like(field))


def below(field):
    return jnp.concatenate([jnp.zeros_like(field[..., :1]), field[..., :-1]], axis=-1)


def above(field):
    return jnp.concatenate([field[..., 1:], jnp.zeros_like(field[..., :1])], axis=-1)


def forward_core(widened, east, north):
    a_pos = jnp.maximum(east, 0.0)
    b_neg = jnp.minimum(east, 0.0)
    c_pos = jnp.maximum(north[1:-1], 0.0)
    d_neg = jnp.minimum(north[1:-1], 0.0)
    flux_w = a_pos[1:] * widened[:, :-1] + b_neg[1:] * widened[:, 1:]
    inner = widened[:, 1:-1]
    flux_s = c_pos * below(inner) + d_neg * inner
    flux_n = above(flux_s)
    return inner - (flux_w[:, 1:] - flux_w[:, :-1]) - (flux_n - flux_s)


def adjoint_core(widened, east, north):
    a_pos = jnp.maximum(east, 0.0)
    b_neg = jnp.minimum(east, 0.0)[1:-1]
    c_pos = jnp.maximum(north[1:-1], 0.0)
    d_neg = jnp.minimum(north[1:-1], 0.0)
    a_east = a_pos[2:]
    c_north = above(c_pos)
    inner = widened[:, 1:-1]
    west_val = widened[:, :-2]
    east_val = widened[:, 2:]
    return (
        inner * (1.0 - a_east + b_neg - c_north + d_neg)
        - b_neg * west_val
        + a_east * east_val
        - d_neg * below(inner)
        + c_north * above(inner)
    )


def four_steps(state, east, north, weight):
    a = jnp.maximum(east, 0.0)
    b = jnp.minimum(east, 0.0)
    c = jnp.maximum(north, 0.0)
    d = jnp.minimum(north, 0.0)
    a_east = jnp.roll(a, -1, axis=0)
    b_east = jnp.roll(b, -1, axis=0)
    c_north = above(c)
    d_north = above(d)
    centre = 1.0 - a_east + b - c_north + d
    for step in range(2):
        west_val = jnp.roll(state, 1, axis=1)
        east_val = jnp.roll(state, -1, axis=1)
        flux_w = a * west_val + b * state
        flux_e = a_east * state + b_east * east_val
        flux_s = c * below(state) + d * state
        flux_n = c_north * state + d_north * above(state)
        state = state - (flux_e - flux_w) - (flux_n - flux_s)
    state = weight * state
    for step in range(2):
        west_val = jnp.roll(state, 1, axis=1)
        east_val = jnp.roll(state, -1, axis=1)
        state = (
            state * centre
            - b * west_val
            + a_east * east_val
            - d * below(state)
            + c_north * above(state)
        )
    return state


def coarsen(sketch):
    probe_count, lon_count, level_count, lat_count = sketch.shape
    summed = sketch.reshape(probe_count, lon_count // 4, 4, level_count, lat_count).sum(axis=2)
    rows = lax.broadcasted_iota(jnp.int32, (lat_count, lat_count // 4), 0) // 4
    cols = lax.broadcasted_iota(jnp.int32, (lat_count, lat_count // 4), 1)
    average = jnp.where(rows == cols, 1.0 / 16.0, 0.0).astype(jnp.float32)
    coarse = jnp.dot(
        summed.reshape(-1, lat_count),
        average,
        precision=lax.Precision.HIGHEST,
        preferred_element_type=jnp.float32,
    )
    return coarse.reshape(probe_count, lon_count // 4, level_count, lat_count // 4)


def body(increments, winds, obs_weight):
    probe_count, lon_count, level_count, lat_count = increments.shape
    halo = 4
    pack = (increments, winds[0][None], lat_mask(winds[1])[None], obs_weight[None])
    west_edge = jnp.concatenate([part[:, lon_count - halo:] for part in pack], axis=0)
    east_edge = jnp.concatenate([part[:, :halo] for part in pack], axis=0)
    from_west, from_east = exchange_halos(west_edge, east_edge)
    bounds = ((0, probe_count), (probe_count, probe_count + 1),
              (probe_count + 1, probe_count + 2), (probe_count + 2, probe_count + 3))
    wide = [
        jnp.concatenate([from_west[lo:hi], part, from_east[lo:hi]], axis=1)
        for part, (lo, hi) in zip(pack, bounds)
    ]
    state = four_steps(wide[0], wide[1][0], wide[2][0], wide[3][0])
    coarse = coarsen(increments + state[:, halo:halo + lon_count])
    coarse = coarse.reshape(probe_count, -1)
    all_probes = probe_count * lax.axis_size("probe")
    ident = jnp.eye(all_probes, dtype=jnp.float32)
    full_panel = lax.all_gather(coarse, "probe", axis=0, tiled=True)
    local_gram = jnp.dot(
        full_panel,
        full_panel.T,
        precision=lax.Precision.HIGHEST,
        preferred_element_type=jnp.float32,
    )
    gram = butterfly_sum(local_gram, "lon")
    lower = jnp.linalg.cholesky(gram)
    inverse = lax.linalg.triangular_solve(lower, ident, left_side=True, lower=True)
    own_rows = lax.dynamic_slice_in_dim(
        inverse, lax.axis_index("probe") * probe_count, probe_count, 0
    )
    basis = jnp.dot(
        own_rows, full_panel, precision=lax.Precision.HIGHEST, preferred_element_type=jnp.float32
    )
    return (basis.reshape(probe_count, lon_count // 4, -1), lower.T)


def solution(mesh):
    in_specs = (P("probe", "lon", None, None), P(None, "lon", None, None), P("lon", None, None))
    out_specs = (P("probe", "lon", None), P())
    return jax.shard_map(body, mesh=mesh, in_specs=in_specs, out_specs=out_specs, check_vma=False)
```

```python
import functools

import jax
import jax.numpy as jnp
from jax import lax
from jax.experimental import pallas as pl
from jax.experimental.pallas import tpu as pltpu
from jax.sharding import PartitionSpec as P

MESH = pl.DeviceIdType.MESH


def from_behind(block, axis, distance):
    devices = range(lax.axis_size(axis))
    route = [((i - distance) % len(devices), i) for i in devices]
    return lax.ppermute(block, axis, route)


def exchange_kernel(count, radix, block_ref, out_ref, held, current, send_sem, recv_sem):
    me = lax.axis_index("lon")
    rounds = []
    stride = 1
    while stride < count:
        width = min(radix, count // stride)
        rounds.append((stride, width))
        stride *= width
    partners = [me ^ (j * stride) for stride, width in rounds for j in range(1, width)]

    barrier = pltpu.get_barrier_semaphore()
    for partner in partners:
        pl.semaphore_signal(barrier, inc=1, device_id={"lon": partner}, device_id_type=MESH)
    pl.semaphore_wait(barrier, len(partners))

    current[0] = block_ref[...]
    slot = 0
    for step, (stride, width) in enumerate(rounds):
        copies = []
        for j in range(1, width):
            copy = pltpu.make_async_remote_copy(
                src_ref=current.at[step],
                dst_ref=held.at[slot + j - 1],
                send_sem=send_sem.at[slot + j - 1],
                recv_sem=recv_sem.at[slot + j - 1],
                device_id={"lon": me ^ (j * stride)},
                device_id_type=MESH,
            )
            copy.start()
            copies.append(copy)
        for copy in copies:
            copy.wait()
        terms = [current[step]] + [held[slot + j - 1] for j in range(1, width)]
        while len(terms) > 1:
            terms = [terms[k] + terms[k + 1] for k in range(0, len(terms), 2)]
        current[step + 1] = terms[0]
        slot += width - 1
    out_ref[...] = current[len(rounds)]


def butterfly_sum(block, axis, radix=4):
    count = lax.axis_size(axis)
    if count & (count - 1) or count < 2:
        return lax.psum(block, axis)
    rounds = 0
    slots = 0
    stride = 1
    while stride < count:
        width = min(radix, count // stride)
        rounds += 1
        slots += width - 1
        stride *= width
    return pl.pallas_call(
        functools.partial(exchange_kernel, count, radix),
        out_shape=jax.ShapeDtypeStruct(block.shape, block.dtype),
        in_specs=[pl.BlockSpec(memory_space=pltpu.VMEM)],
        out_specs=pl.BlockSpec(memory_space=pltpu.VMEM),
        scratch_shapes=[
            pltpu.VMEM((slots,) + block.shape, block.dtype),
            pltpu.VMEM((rounds + 1,) + block.shape, block.dtype),
            pltpu.SemaphoreType.DMA((slots,)),
            pltpu.SemaphoreType.DMA((slots,)),
        ],
        compiler_params=pltpu.CompilerParams(collective_id=0, has_side_effects=True),
    )(block)


def padded(block, sides, width):
    for axis, dim in sides:
        count = lax.axis_size(axis)
        forward = [(i, i + 1) for i in range(count - 1)]
        forward.append((count - 1, 0))
        backward = [(target, source) for source, target in forward]
        low = lax.ppermute(
            lax.slice_in_dim(block, block.shape[dim] - width, None, axis=dim), axis, forward
        )
        high = lax.ppermute(lax.slice_in_dim(block, 0, width, axis=dim), axis, backward)
        block = jnp.concatenate([low, block, high], axis=dim)
    return block


def lat_mask(field):
    rows = lax.broadcasted_iota(jnp.int32, field.shape, field.ndim - 1)
    return jnp.where(rows > 0, field, jnp.zeros_like(field))


def below(field):
    return jnp.concatenate([jnp.zeros_like(field[..., :1]), field[..., :-1]], axis=-1)


def above(field):
    return jnp.concatenate([field[..., 1:], jnp.zeros_like(field[..., :1])], axis=-1)


def lon(x, start, stop):
    first, last, _ = slice(start, stop).indices(x.shape[-3])
    return lax.slice_in_dim(x, first, last, axis=x.ndim - 3)


def forward_core(widened, east, north):
    a_pos = jnp.maximum(east, 0.0)
    b_neg = jnp.minimum(east, 0.0)
    c_pos = jnp.maximum(lon(north, 1, -1), 0.0)
    d_neg = jnp.minimum(lon(north, 1, -1), 0.0)
    flux_w = lon(a_pos, 1, None) * lon(widened, 0, -1) + lon(b_neg, 1, None) * lon(widened, 1, None)
    inner = lon(widened, 1, -1)
    flux_s = c_pos * below(inner) + d_neg * inner
    flux_n = above(flux_s)
    return inner - (lon(flux_w, 1, None) - lon(flux_w, 0, -1)) - (flux_n - flux_s)


def adjoint_core(widened, east, north):
    a_pos = jnp.maximum(east, 0.0)
    b_neg = lon(jnp.minimum(east, 0.0), 1, -1)
    c_pos = jnp.maximum(lon(north, 1, -1), 0.0)
    d_neg = jnp.minimum(lon(north, 1, -1), 0.0)
    a_east = lon(a_pos, 2, None)
    c_north = above(c_pos)
    inner = lon(widened, 1, -1)
    west_val = lon(widened, 0, -2)
    east_val = lon(widened, 2, None)
    return (
        inner * (1.0 - a_east + b_neg - c_north + d_neg)
        - b_neg * west_val
        + a_east * east_val
        - d_neg * below(inner)
        + c_north * above(inner)
    )


def four_steps(state, east, north, weight):
    span = state.shape[-3]
    for step in range(2):
        state = forward_core(state, lon(east, step, span - step), lon(north, step, span - step))
    state = lon(weight, 2, span - 2) * state
    for step in range(2, 4):
        state = adjoint_core(state, lon(east, step, span - step), lon(north, step, span - step))
    return state


def coarsen(sketch):
    probe_count, lon_count, level_count, lat_count = sketch.shape
    summed = sketch.reshape(probe_count, lon_count // 4, 4, level_count, lat_count).sum(axis=2)
    rows = lax.broadcasted_iota(jnp.int32, (lat_count, lat_count // 4), 0) // 4
    cols = lax.broadcasted_iota(jnp.int32, (lat_count, lat_count // 4), 1)
    average = jnp.where(rows == cols, 1.0 / 16.0, 0.0).astype(jnp.float32)
    coarse = jnp.dot(
        summed.reshape(-1, lat_count),
        average,
        precision=lax.Precision.HIGHEST,
        preferred_element_type=jnp.float32,
    )
    return coarse.reshape(probe_count, lon_count // 4, level_count, lat_count // 4)


def body(increments, winds, obs_weight):
    probe_count, lon_count, level_count, lat_count = increments.shape
    halo = 4
    pack = (increments, winds[0][None], lat_mask(winds[1])[None], obs_weight[None])
    count = lax.axis_size("lon")
    forward = [(i, (i + 1) % count) for i in range(count)]
    backward = [((i + 1) % count, i) for i in range(count)]
    west_edge = jnp.concatenate([part[:, lon_count - halo:] for part in pack], axis=0)
    east_edge = jnp.concatenate([part[:, :halo] for part in pack], axis=0)
    from_west = lax.ppermute(west_edge, "lon", forward)
    from_east = lax.ppermute(east_edge, "lon", backward)
    bounds = ((0, probe_count), (probe_count, probe_count + 1),
              (probe_count + 1, probe_count + 2), (probe_count + 2, probe_count + 3))

    def fields(parts):
        return parts[0], parts[1][0], parts[2][0], parts[3][0]

    inner = four_steps(*fields(pack))
    inner = coarsen(increments[:, halo:lon_count - halo] + inner)
    sides = [
        jnp.stack([
            jnp.concatenate([from_west[lo:hi], part[:, :2 * halo]], axis=1),
            jnp.concatenate([part[:, lon_count - 2 * halo:], from_east[lo:hi]], axis=1),
        ])
        for part, (lo, hi) in zip(pack, bounds)
    ]
    rim = four_steps(sides[0], sides[1], sides[2], sides[3])
    west = coarsen(increments[:, :halo] + rim[0])
    east = coarsen(increments[:, lon_count - halo:] + rim[1])
    coarse = jnp.concatenate([west, inner, east], axis=1)
    coarse = coarse.reshape(probe_count, -1)
    all_probes = probe_count * lax.axis_size("probe")
    ident = jnp.eye(all_probes, dtype=jnp.float32)
    full_panel = lax.all_gather(coarse, "probe", axis=0, tiled=True)
    local_gram = jnp.dot(
        full_panel,
        full_panel.T,
        precision=lax.Precision.HIGHEST,
        preferred_element_type=jnp.float32,
    )
    gram = butterfly_sum(local_gram, "lon")
    lower = jnp.linalg.cholesky(gram)
    inverse = lax.linalg.triangular_solve(lower, ident, left_side=True, lower=True)
    own_rows = lax.dynamic_slice_in_dim(
        inverse, lax.axis_index("probe") * probe_count, probe_count, 0
    )
    basis = jnp.dot(
        own_rows, full_panel, precision=lax.Precision.HIGHEST, preferred_element_type=jnp.float32
    )
    return (basis.reshape(probe_count, lon_count // 4, -1), lower.T)


def solution(mesh):
    in_specs = (P("probe", "lon", None, None), P(None, "lon", None, None), P("lon", None, None))
    out_specs = (P("probe", "lon", None), P())
    return jax.shard_map(body, mesh=mesh, in_specs=in_specs, out_specs=out_specs, check_vma=False)
```

```python
import functools

import jax
import jax.numpy as jnp
from jax import lax
from jax.experimental import pallas as pl
from jax.experimental.pallas import tpu as pltpu
from jax.sharding import PartitionSpec as P

MESH = pl.DeviceIdType.MESH


def from_behind(block, axis, distance):
    devices = range(lax.axis_size(axis))
    route = [((i - distance) % len(devices), i) for i in devices]
    return lax.ppermute(block, axis, route)


def exchange_kernel(count, radix, block_ref, out_ref, held, current, send_sem, recv_sem):
    me = lax.axis_index("lon")
    rounds = []
    stride = 1
    while stride < count:
        width = min(radix, count // stride)
        rounds.append((stride, width))
        stride *= width
    partners = [me ^ (j * stride) for stride, width in rounds for j in range(1, width)]

    barrier = pltpu.get_barrier_semaphore()
    for partner in partners:
        pl.semaphore_signal(barrier, inc=1, device_id={"lon": partner}, device_id_type=MESH)
    pl.semaphore_wait(barrier, len(partners))

    current[0] = block_ref[...]
    slot = 0
    for step, (stride, width) in enumerate(rounds):
        copies = []
        for j in range(1, width):
            copy = pltpu.make_async_remote_copy(
                src_ref=current.at[step],
                dst_ref=held.at[slot + j - 1],
                send_sem=send_sem.at[slot + j - 1],
                recv_sem=recv_sem.at[slot + j - 1],
                device_id={"lon": me ^ (j * stride)},
                device_id_type=MESH,
            )
            copy.start()
            copies.append(copy)
        for copy in copies:
            copy.wait()
        terms = [current[step]] + [held[slot + j - 1] for j in range(1, width)]
        while len(terms) > 1:
            terms = [terms[k] + terms[k + 1] for k in range(0, len(terms), 2)]
        current[step + 1] = terms[0]
        slot += width - 1
    out_ref[...] = current[len(rounds)]


def butterfly_sum(block, axis, radix=4):
    count = lax.axis_size(axis)
    if count & (count - 1) or count < 2:
        return lax.psum(block, axis)
    rounds = 0
    slots = 0
    stride = 1
    while stride < count:
        width = min(radix, count // stride)
        rounds += 1
        slots += width - 1
        stride *= width
    return pl.pallas_call(
        functools.partial(exchange_kernel, count, radix),
        out_shape=jax.ShapeDtypeStruct(block.shape, block.dtype),
        in_specs=[pl.BlockSpec(memory_space=pltpu.VMEM)],
        out_specs=pl.BlockSpec(memory_space=pltpu.VMEM),
        scratch_shapes=[
            pltpu.VMEM((slots,) + block.shape, block.dtype),
            pltpu.VMEM((rounds + 1,) + block.shape, block.dtype),
            pltpu.SemaphoreType.DMA((slots,)),
            pltpu.SemaphoreType.DMA((slots,)),
        ],
        compiler_params=pltpu.CompilerParams(collective_id=0, has_side_effects=True),
    )(block)


def padded(block, sides, width):
    for axis, dim in sides:
        count = lax.axis_size(axis)
        forward = [(i, i + 1) for i in range(count - 1)]
        forward.append((count - 1, 0))
        backward = [(target, source) for source, target in forward]
        low = lax.ppermute(
            lax.slice_in_dim(block, block.shape[dim] - width, None, axis=dim), axis, forward
        )
        high = lax.ppermute(lax.slice_in_dim(block, 0, width, axis=dim), axis, backward)
        block = jnp.concatenate([low, block, high], axis=dim)
    return block


def lat_mask(field):
    rows = lax.broadcasted_iota(jnp.int32, field.shape, field.ndim - 1)
    return jnp.where(rows > 0, field, jnp.zeros_like(field))


def below(field):
    return jnp.concatenate([jnp.zeros_like(field[..., :1]), field[..., :-1]], axis=-1)


def above(field):
    return jnp.concatenate([field[..., 1:], jnp.zeros_like(field[..., :1])], axis=-1)


def lon(x, start, stop):
    first, last, _ = slice(start, stop).indices(x.shape[-3])
    return lax.slice_in_dim(x, first, last, axis=x.ndim - 3)


def forward_core(widened, east, north):
    a_pos = jnp.maximum(east, 0.0)
    b_neg = jnp.minimum(east, 0.0)
    c_pos = jnp.maximum(lon(north, 1, -1), 0.0)
    d_neg = jnp.minimum(lon(north, 1, -1), 0.0)
    flux_w = lon(a_pos, 1, None) * lon(widened, 0, -1) + lon(b_neg, 1, None) * lon(widened, 1, None)
    inner = lon(widened, 1, -1)
    flux_s = c_pos * below(inner) + d_neg * inner
    flux_n = above(flux_s)
    return inner - (lon(flux_w, 1, None) - lon(flux_w, 0, -1)) - (flux_n - flux_s)


def adjoint_core(widened, east, north):
    a_pos = jnp.maximum(east, 0.0)
    b_neg = lon(jnp.minimum(east, 0.0), 1, -1)
    c_pos = jnp.maximum(lon(north, 1, -1), 0.0)
    d_neg = jnp.minimum(lon(north, 1, -1), 0.0)
    a_east = lon(a_pos, 2, None)
    c_north = above(c_pos)
    inner = lon(widened, 1, -1)
    west_val = lon(widened, 0, -2)
    east_val = lon(widened, 2, None)
    return (
        inner * (1.0 - a_east + b_neg - c_north + d_neg)
        - b_neg * west_val
        + a_east * east_val
        - d_neg * below(inner)
        + c_north * above(inner)
    )


def four_steps(state, east, north, weight):
    span = state.shape[-3]
    for step in range(2):
        state = forward_core(state, lon(east, step, span - step), lon(north, step, span - step))
    state = lon(weight, 2, span - 2) * state
    for step in range(2, 4):
        state = adjoint_core(state, lon(east, step, span - step), lon(north, step, span - step))
    return state


def coarsen(sketch):
    probe_count, lon_count, level_count, lat_count = sketch.shape
    summed = sketch.reshape(probe_count, lon_count // 4, 4, level_count, lat_count).sum(axis=2)
    rows = lax.broadcasted_iota(jnp.int32, (lat_count, lat_count // 4), 0) // 4
    cols = lax.broadcasted_iota(jnp.int32, (lat_count, lat_count // 4), 1)
    average = jnp.where(rows == cols, 1.0 / 16.0, 0.0).astype(jnp.float32)
    coarse = jnp.dot(
        summed.reshape(-1, lat_count),
        average,
        precision=lax.Precision.HIGHEST,
        preferred_element_type=jnp.float32,
    )
    return coarse.reshape(probe_count, lon_count // 4, level_count, lat_count // 4)


def stencil_kernel(q_ref, a_ref, b_ref, c_ref, d_ref, w_ref, n_ref, k_ref, o_ref):
    span = q_ref.shape[1]
    lat = q_ref.shape[-1]
    field = q_ref[0]
    state = field
    for step in range(2):
        lo, hi = step, span - step
        east_a = a_ref[lo:hi]
        east_b = b_ref[lo:hi]
        north_c = c_ref[lo + 1:hi - 1]
        north_d = d_ref[lo + 1:hi - 1]
        flux_w = east_a[1:] * state[:-1] + east_b[1:] * state[1:]
        inner = state[1:-1]
        flux_s = north_c * pltpu.roll(inner, 1, 2) + north_d * inner
        flux_n = pltpu.roll(flux_s, lat - 1, 2)
        state = inner - (flux_w[1:] - flux_w[:-1]) - (flux_n - flux_s)
    state = w_ref[2:span - 2] * state
    for step in range(2, 4):
        lo, hi = step, span - step
        west_b = b_ref[lo + 1:hi - 1]
        east_a = a_ref[lo + 2:hi]
        north_d = d_ref[lo + 1:hi - 1]
        north_up = n_ref[lo + 1:hi - 1]
        inner = state[1:-1]
        state = (
            inner * k_ref[lo + 1:hi - 1]
            - west_b * state[:-2]
            + east_a * state[2:]
            - north_d * pltpu.roll(inner, 1, 2)
            + north_up * pltpu.roll(inner, lat - 1, 2)
        )
    sketch = field[4:span - 4] + state
    groups = sketch.shape[0] // 4
    for g in range(groups):
        o_ref[0, g] = ((sketch[4 * g] + sketch[4 * g + 1]) + sketch[4 * g + 2]) + sketch[4 * g + 3]


def stencil_sums(slab, east, north, weight):
    probe_count, span, level_count, lat_count = slab.shape
    groups = (span - 8) // 4
    east_a = jnp.maximum(east, 0.0)
    east_b = jnp.minimum(east, 0.0)
    north_c = jnp.maximum(north, 0.0)
    north_d = jnp.minimum(north, 0.0)
    north_up = above(north_c)
    next_a = jnp.concatenate([east_a[1:], jnp.zeros_like(east_a[:1])], axis=0)
    centre = 1.0 - next_a + east_b - north_up + north_d
    winds = (east_a, east_b, north_c, north_d, weight, north_up, centre)
    full = pl.BlockSpec((span, level_count, lat_count), lambda i: (0, 0, 0))
    elements = probe_count * span * level_count * lat_count
    return pl.pallas_call(
        stencil_kernel,
        out_shape=jax.ShapeDtypeStruct((probe_count, groups, level_count, lat_count), slab.dtype),
        grid=(probe_count,),
        in_specs=[pl.BlockSpec((1, span, level_count, lat_count), lambda i: (i, 0, 0, 0))] + [full] * 7,
        out_specs=pl.BlockSpec((1, groups, level_count, lat_count), lambda i: (i, 0, 0, 0)),
        cost_estimate=pl.CostEstimate(
            flops=50 * elements, transcendentals=0, bytes_accessed=4 * elements + 28 * span * level_count * lat_count
        ),
    )(slab, *winds)


def lat_average(summed):
    probe_count, groups, level_count, lat_count = summed.shape
    rows = lax.broadcasted_iota(jnp.int32, (lat_count, lat_count // 4), 0) // 4
    cols = lax.broadcasted_iota(jnp.int32, (lat_count, lat_count // 4), 1)
    average = jnp.where(rows == cols, 1.0 / 16.0, 0.0).astype(jnp.float32)
    coarse = jnp.dot(
        summed.reshape(-1, lat_count),
        average,
        precision=lax.Precision.HIGHEST,
        preferred_element_type=jnp.float32,
    )
    return coarse.reshape(probe_count, groups, level_count, lat_count // 4)


def body(increments, winds, obs_weight):
    probe_count, lon_count, level_count, lat_count = increments.shape
    halo = 4
    pack = (increments, winds[0][None], lat_mask(winds[1])[None], obs_weight[None])
    count = lax.axis_size("lon")
    forward = [(i, (i + 1) % count) for i in range(count)]
    backward = [((i + 1) % count, i) for i in range(count)]
    west_edge = jnp.concatenate([part[:, lon_count - halo:] for part in pack], axis=0)
    east_edge = jnp.concatenate([part[:, :halo] for part in pack], axis=0)
    from_west = lax.ppermute(west_edge, "lon", forward)
    from_east = lax.ppermute(east_edge, "lon", backward)
    bounds = ((0, probe_count), (probe_count, probe_count + 1),
              (probe_count + 1, probe_count + 2), (probe_count + 2, probe_count + 3))

    def fields(parts):
        return parts[0], parts[1][0], parts[2][0], parts[3][0]

    inner = lat_average(stencil_sums(*fields(pack)))
    sides = [
        jnp.stack([
            jnp.concatenate([from_west[lo:hi], part[:, :2 * halo]], axis=1),
            jnp.concatenate([part[:, lon_count - 2 * halo:], from_east[lo:hi]], axis=1),
        ])
        for part, (lo, hi) in zip(pack, bounds)
    ]
    rim = four_steps(sides[0], sides[1], sides[2], sides[3])
    west = coarsen(increments[:, :halo] + rim[0])
    east = coarsen(increments[:, lon_count - halo:] + rim[1])
    coarse = jnp.concatenate([west, inner, east], axis=1)
    coarse = coarse.reshape(probe_count, -1)
    all_probes = probe_count * lax.axis_size("probe")
    ident = jnp.eye(all_probes, dtype=jnp.float32)
    full_panel = lax.all_gather(coarse, "probe", axis=0, tiled=True)
    local_gram = jnp.dot(
        full_panel,
        full_panel.T,
        precision=lax.Precision.HIGHEST,
        preferred_element_type=jnp.float32,
    )
    gram = butterfly_sum(local_gram, "lon")
    lower = jnp.linalg.cholesky(gram)
    inverse = lax.linalg.triangular_solve(lower, ident, left_side=True, lower=True)
    own_rows = lax.dynamic_slice_in_dim(
        inverse, lax.axis_index("probe") * probe_count, probe_count, 0
    )
    basis = jnp.dot(
        own_rows, full_panel, precision=lax.Precision.HIGHEST, preferred_element_type=jnp.float32
    )
    return (basis.reshape(probe_count, lon_count // 4, -1), lower.T)


def solution(mesh):
    in_specs = (P("probe", "lon", None, None), P(None, "lon", None, None), P("lon", None, None))
    out_specs = (P("probe", "lon", None), P())
    return jax.shard_map(body, mesh=mesh, in_specs=in_specs, out_specs=out_specs, check_vma=False)
```

```python
import functools

import jax
import jax.numpy as jnp
from jax import lax
from jax.experimental import pallas as pl
from jax.experimental.pallas import tpu as pltpu
from jax.sharding import PartitionSpec as P

MESH = pl.DeviceIdType.MESH


def from_behind(block, axis, distance):
    devices = range(lax.axis_size(axis))
    route = [((i - distance) % len(devices), i) for i in devices]
    return lax.ppermute(block, axis, route)


def exchange_kernel(count, radix, block_ref, out_ref, held, current, send_sem, recv_sem):
    me = lax.axis_index("lon")
    rounds = []
    stride = 1
    while stride < count:
        width = min(radix, count // stride)
        rounds.append((stride, width))
        stride *= width
    partners = [me ^ (j * stride) for stride, width in rounds for j in range(1, width)]

    barrier = pltpu.get_barrier_semaphore()
    for partner in partners:
        pl.semaphore_signal(barrier, inc=1, device_id={"lon": partner}, device_id_type=MESH)
    pl.semaphore_wait(barrier, len(partners))

    current[0] = block_ref[...]
    slot = 0
    for step, (stride, width) in enumerate(rounds):
        copies = []
        for j in range(1, width):
            copy = pltpu.make_async_remote_copy(
                src_ref=current.at[step],
                dst_ref=held.at[slot + j - 1],
                send_sem=send_sem.at[slot + j - 1],
                recv_sem=recv_sem.at[slot + j - 1],
                device_id={"lon": me ^ (j * stride)},
                device_id_type=MESH,
            )
            copy.start()
            copies.append(copy)
        for copy in copies:
            copy.wait()
        terms = [current[step]] + [held[slot + j - 1] for j in range(1, width)]
        while len(terms) > 1:
            terms = [terms[k] + terms[k + 1] for k in range(0, len(terms), 2)]
        current[step + 1] = terms[0]
        slot += width - 1
    out_ref[...] = current[len(rounds)]


def butterfly_sum(block, axis, radix=4):
    count = lax.axis_size(axis)
    if count & (count - 1) or count < 2:
        return lax.psum(block, axis)
    rounds = 0
    slots = 0
    stride = 1
    while stride < count:
        width = min(radix, count // stride)
        rounds += 1
        slots += width - 1
        stride *= width
    return pl.pallas_call(
        functools.partial(exchange_kernel, count, radix),
        out_shape=jax.ShapeDtypeStruct(block.shape, block.dtype),
        in_specs=[pl.BlockSpec(memory_space=pltpu.VMEM)],
        out_specs=pl.BlockSpec(memory_space=pltpu.VMEM),
        scratch_shapes=[
            pltpu.VMEM((slots,) + block.shape, block.dtype),
            pltpu.VMEM((rounds + 1,) + block.shape, block.dtype),
            pltpu.SemaphoreType.DMA((slots,)),
            pltpu.SemaphoreType.DMA((slots,)),
        ],
        compiler_params=pltpu.CompilerParams(collective_id=0, has_side_effects=True),
    )(block)


def padded(block, sides, width):
    for axis, dim in sides:
        count = lax.axis_size(axis)
        forward = [(i, i + 1) for i in range(count - 1)]
        forward.append((count - 1, 0))
        backward = [(target, source) for source, target in forward]
        low = lax.ppermute(
            lax.slice_in_dim(block, block.shape[dim] - width, None, axis=dim), axis, forward
        )
        high = lax.ppermute(lax.slice_in_dim(block, 0, width, axis=dim), axis, backward)
        block = jnp.concatenate([low, block, high], axis=dim)
    return block


def lat_mask(field):
    rows = lax.broadcasted_iota(jnp.int32, field.shape, field.ndim - 1)
    return jnp.where(rows > 0, field, jnp.zeros_like(field))


def below(field):
    return jnp.concatenate([jnp.zeros_like(field[..., :1]), field[..., :-1]], axis=-1)


def above(field):
    return jnp.concatenate([field[..., 1:], jnp.zeros_like(field[..., :1])], axis=-1)


def lon(x, start, stop):
    first, last, _ = slice(start, stop).indices(x.shape[-3])
    return lax.slice_in_dim(x, first, last, axis=x.ndim - 3)


def forward_core(widened, east, north):
    a_pos = jnp.maximum(east, 0.0)
    b_neg = jnp.minimum(east, 0.0)
    c_pos = jnp.maximum(lon(north, 1, -1), 0.0)
    d_neg = jnp.minimum(lon(north, 1, -1), 0.0)
    flux_w = lon(a_pos, 1, None) * lon(widened, 0, -1) + lon(b_neg, 1, None) * lon(widened, 1, None)
    inner = lon(widened, 1, -1)
    flux_s = c_pos * below(inner) + d_neg * inner
    flux_n = above(flux_s)
    return inner - (lon(flux_w, 1, None) - lon(flux_w, 0, -1)) - (flux_n - flux_s)


def adjoint_core(widened, east, north):
    a_pos = jnp.maximum(east, 0.0)
    b_neg = lon(jnp.minimum(east, 0.0), 1, -1)
    c_pos = jnp.maximum(lon(north, 1, -1), 0.0)
    d_neg = jnp.minimum(lon(north, 1, -1), 0.0)
    a_east = lon(a_pos, 2, None)
    c_north = above(c_pos)
    inner = lon(widened, 1, -1)
    west_val = lon(widened, 0, -2)
    east_val = lon(widened, 2, None)
    return (
        inner * (1.0 - a_east + b_neg - c_north + d_neg)
        - b_neg * west_val
        + a_east * east_val
        - d_neg * below(inner)
        + c_north * above(inner)
    )


def four_steps(state, east, north, weight):
    span = state.shape[-3]
    for step in range(2):
        state = forward_core(state, lon(east, step, span - step), lon(north, step, span - step))
    state = lon(weight, 2, span - 2) * state
    for step in range(2, 4):
        state = adjoint_core(state, lon(east, step, span - step), lon(north, step, span - step))
    return state


def coarsen(sketch):
    probe_count, lon_count, level_count, lat_count = sketch.shape
    summed = sketch.reshape(probe_count, lon_count // 4, 4, level_count, lat_count).sum(axis=2)
    rows = lax.broadcasted_iota(jnp.int32, (lat_count, lat_count // 4), 0) // 4
    cols = lax.broadcasted_iota(jnp.int32, (lat_count, lat_count // 4), 1)
    average = jnp.where(rows == cols, 1.0 / 16.0, 0.0).astype(jnp.float32)
    coarse = jnp.dot(
        summed.reshape(-1, lat_count),
        average,
        precision=lax.Precision.HIGHEST,
        preferred_element_type=jnp.float32,
    )
    return coarse.reshape(probe_count, lon_count // 4, level_count, lat_count // 4)


def stencil_kernel(q_ref, a_ref, b_ref, c_ref, d_ref, w_ref, n_ref, k_ref, o_ref):
    span = q_ref.shape[1]
    lat = q_ref.shape[-1]
    field = q_ref[0]
    state = field
    for step in range(2):
        lo, hi = step, span - step
        east_a = a_ref[lo:hi]
        east_b = b_ref[lo:hi]
        north_c = c_ref[lo + 1:hi - 1]
        north_d = d_ref[lo + 1:hi - 1]
        flux_w = east_a[1:] * state[:-1] + east_b[1:] * state[1:]
        inner = state[1:-1]
        flux_s = north_c * pltpu.roll(inner, 1, 2) + north_d * inner
        flux_n = pltpu.roll(flux_s, lat - 1, 2)
        state = inner - (flux_w[1:] - flux_w[:-1]) - (flux_n - flux_s)
    state = w_ref[2:span - 2] * state
    for step in range(2, 4):
        lo, hi = step, span - step
        west_b = b_ref[lo + 1:hi - 1]
        east_a = a_ref[lo + 2:hi]
        north_d = d_ref[lo + 1:hi - 1]
        north_up = n_ref[lo + 1:hi - 1]
        inner = state[1:-1]
        state = (
            inner * k_ref[lo + 1:hi - 1]
            - west_b * state[:-2]
            + east_a * state[2:]
            - north_d * pltpu.roll(inner, 1, 2)
            + north_up * pltpu.roll(inner, lat - 1, 2)
        )
    sketch = field[4:span - 4] + state
    groups = sketch.shape[0] // 4
    for g in range(groups):
        o_ref[0, g] = ((sketch[4 * g] + sketch[4 * g + 1]) + sketch[4 * g + 2]) + sketch[4 * g + 3]


def stencil_sums(slab, east, north, weight):
    probe_count, span, level_count, lat_count = slab.shape
    groups = (span - 8) // 4
    east_a = jnp.maximum(east, 0.0)
    east_b = jnp.minimum(east, 0.0)
    north_c = jnp.maximum(north, 0.0)
    north_d = jnp.minimum(north, 0.0)
    north_up = above(north_c)
    next_a = jnp.concatenate([east_a[1:], jnp.zeros_like(east_a[:1])], axis=0)
    centre = 1.0 - next_a + east_b - north_up + north_d
    winds = (east_a, east_b, north_c, north_d, weight, north_up, centre)
    full = pl.BlockSpec((span, level_count, lat_count), lambda i: (0, 0, 0))
    elements = probe_count * span * level_count * lat_count
    return pl.pallas_call(
        stencil_kernel,
        out_shape=jax.ShapeDtypeStruct((probe_count, groups, level_count, lat_count), slab.dtype),
        grid=(probe_count,),
        in_specs=[pl.BlockSpec((1, span, level_count, lat_count), lambda i: (i, 0, 0, 0))] + [full] * 7,
        out_specs=pl.BlockSpec((1, groups, level_count, lat_count), lambda i: (i, 0, 0, 0)),
        cost_estimate=pl.CostEstimate(
            flops=50 * elements, transcendentals=0, bytes_accessed=4 * elements + 28 * span * level_count * lat_count
        ),
    )(slab, *winds)


def lat_average(summed):
    probe_count, groups, level_count, lat_count = summed.shape
    rows = lax.broadcasted_iota(jnp.int32, (lat_count, lat_count // 4), 0) // 4
    cols = lax.broadcasted_iota(jnp.int32, (lat_count, lat_count // 4), 1)
    average = jnp.where(rows == cols, 1.0 / 16.0, 0.0).astype(jnp.float32)
    coarse = jnp.dot(
        summed.reshape(-1, lat_count),
        average,
        precision=lax.Precision.HIGHEST,
        preferred_element_type=jnp.float32,
    )
    return coarse.reshape(probe_count, groups, level_count, lat_count // 4)


def body(increments, winds, obs_weight):
    probe_count, lon_count, level_count, lat_count = increments.shape
    halo = 4
    pack = (increments, winds[0][None], winds[1][None], obs_weight[None])
    count = lax.axis_size("lon")
    forward = [(i, (i + 1) % count) for i in range(count)]
    backward = [((i + 1) % count, i) for i in range(count)]
    west_edge = jnp.concatenate([part[:, lon_count - halo:] for part in pack], axis=0)
    east_edge = jnp.concatenate([part[:, :halo] for part in pack], axis=0)
    from_west = lax.ppermute(west_edge, "lon", forward)
    from_east = lax.ppermute(east_edge, "lon", backward)
    bounds = ((0, probe_count), (probe_count, probe_count + 1),
              (probe_count + 1, probe_count + 2), (probe_count + 2, probe_count + 3))

    def fields(parts):
        return parts[0], parts[1][0], lat_mask(parts[2][0]), parts[3][0]

    inner = lat_average(stencil_sums(*fields(pack)))
    sides = [
        jnp.stack([
            jnp.concatenate([from_west[lo:hi], part[:, :2 * halo]], axis=1),
            jnp.concatenate([part[:, lon_count - 2 * halo:], from_east[lo:hi]], axis=1),
        ])
        for part, (lo, hi) in zip(pack, bounds)
    ]
    rim = four_steps(sides[0], sides[1], lat_mask(sides[2]), sides[3])
    west = coarsen(increments[:, :halo] + rim[0])
    east = coarsen(increments[:, lon_count - halo:] + rim[1])
    coarse = jnp.concatenate([west, inner, east], axis=1)
    coarse = coarse.reshape(probe_count, -1)
    all_probes = probe_count * lax.axis_size("probe")
    ident = jnp.eye(all_probes, dtype=jnp.float32)
    full_panel = lax.all_gather(coarse, "probe", axis=0, tiled=True)
    local_gram = jnp.dot(
        full_panel,
        full_panel.T,
        precision=lax.Precision.HIGHEST,
        preferred_element_type=jnp.float32,
    )
    gram = butterfly_sum(local_gram, "lon")
    lower = jnp.linalg.cholesky(gram)
    inverse = lax.linalg.triangular_solve(lower, ident, left_side=True, lower=True)
    own_rows = lax.dynamic_slice_in_dim(
        inverse, lax.axis_index("probe") * probe_count, probe_count, 0
    )
    basis = jnp.dot(
        own_rows, full_panel, precision=lax.Precision.HIGHEST, preferred_element_type=jnp.float32
    )
    return (basis.reshape(probe_count, lon_count // 4, -1), lower.T)


def solution(mesh):
    in_specs = (P("probe", "lon", None, None), P(None, "lon", None, None), P("lon", None, None))
    out_specs = (P("probe", "lon", None), P())
    return jax.shard_map(body, mesh=mesh, in_specs=in_specs, out_specs=out_specs, check_vma=False)
```

```python
import functools

import jax
import jax.numpy as jnp
from jax import lax
from jax.experimental import pallas as pl
from jax.experimental.pallas import tpu as pltpu
from jax.sharding import PartitionSpec as P

MESH = pl.DeviceIdType.MESH


def from_behind(block, axis, distance):
    devices = range(lax.axis_size(axis))
    route = [((i - distance) % len(devices), i) for i in devices]
    return lax.ppermute(block, axis, route)


def exchange_kernel(count, radix, block_ref, out_ref, held, current, send_sem, recv_sem):
    me = lax.axis_index("lon")
    rounds = []
    stride = 1
    while stride < count:
        width = min(radix, count // stride)
        rounds.append((stride, width))
        stride *= width
    partners = [me ^ (j * stride) for stride, width in rounds for j in range(1, width)]

    barrier = pltpu.get_barrier_semaphore()
    for partner in partners:
        pl.semaphore_signal(barrier, inc=1, device_id={"lon": partner}, device_id_type=MESH)
    pl.semaphore_wait(barrier, len(partners))

    current[0] = block_ref[...]
    slot = 0
    for step, (stride, width) in enumerate(rounds):
        copies = []
        for j in range(1, width):
            copy = pltpu.make_async_remote_copy(
                src_ref=current.at[step],
                dst_ref=held.at[slot + j - 1],
                send_sem=send_sem.at[slot + j - 1],
                recv_sem=recv_sem.at[slot + j - 1],
                device_id={"lon": me ^ (j * stride)},
                device_id_type=MESH,
            )
            copy.start()
            copies.append(copy)
        for copy in copies:
            copy.wait()
        terms = [current[step]] + [held[slot + j - 1] for j in range(1, width)]
        while len(terms) > 1:
            terms = [terms[k] + terms[k + 1] for k in range(0, len(terms), 2)]
        current[step + 1] = terms[0]
        slot += width - 1
    out_ref[...] = current[len(rounds)]


def butterfly_sum(block, axis, radix=4):
    count = lax.axis_size(axis)
    if count & (count - 1) or count < 2:
        return lax.psum(block, axis)
    rounds = 0
    slots = 0
    stride = 1
    while stride < count:
        width = min(radix, count // stride)
        rounds += 1
        slots += width - 1
        stride *= width
    return pl.pallas_call(
        functools.partial(exchange_kernel, count, radix),
        out_shape=jax.ShapeDtypeStruct(block.shape, block.dtype),
        in_specs=[pl.BlockSpec(memory_space=pltpu.VMEM)],
        out_specs=pl.BlockSpec(memory_space=pltpu.VMEM),
        scratch_shapes=[
            pltpu.VMEM((slots,) + block.shape, block.dtype),
            pltpu.VMEM((rounds + 1,) + block.shape, block.dtype),
            pltpu.SemaphoreType.DMA((slots,)),
            pltpu.SemaphoreType.DMA((slots,)),
        ],
        compiler_params=pltpu.CompilerParams(collective_id=0, has_side_effects=True),
    )(block)


def padded(block, sides, width):
    for axis, dim in sides:
        count = lax.axis_size(axis)
        forward = [(i, i + 1) for i in range(count - 1)]
        forward.append((count - 1, 0))
        backward = [(target, source) for source, target in forward]
        low = lax.ppermute(
            lax.slice_in_dim(block, block.shape[dim] - width, None, axis=dim), axis, forward
        )
        high = lax.ppermute(lax.slice_in_dim(block, 0, width, axis=dim), axis, backward)
        block = jnp.concatenate([low, block, high], axis=dim)
    return block


def lat_mask(field):
    rows = lax.broadcasted_iota(jnp.int32, field.shape, field.ndim - 1)
    return jnp.where(rows > 0, field, jnp.zeros_like(field))


def below(field):
    return jnp.concatenate([jnp.zeros_like(field[..., :1]), field[..., :-1]], axis=-1)


def above(field):
    return jnp.concatenate([field[..., 1:], jnp.zeros_like(field[..., :1])], axis=-1)


def lon(x, start, stop):
    first, last, _ = slice(start, stop).indices(x.shape[-3])
    return lax.slice_in_dim(x, first, last, axis=x.ndim - 3)


def forward_core(widened, east, north):
    a_pos = jnp.maximum(east, 0.0)
    b_neg = jnp.minimum(east, 0.0)
    c_pos = jnp.maximum(lon(north, 1, -1), 0.0)
    d_neg = jnp.minimum(lon(north, 1, -1), 0.0)
    flux_w = lon(a_pos, 1, None) * lon(widened, 0, -1) + lon(b_neg, 1, None) * lon(widened, 1, None)
    inner = lon(widened, 1, -1)
    flux_s = c_pos * below(inner) + d_neg * inner
    flux_n = above(flux_s)
    return inner - (lon(flux_w, 1, None) - lon(flux_w, 0, -1)) - (flux_n - flux_s)


def adjoint_core(widened, east, north):
    a_pos = jnp.maximum(east, 0.0)
    b_neg = lon(jnp.minimum(east, 0.0), 1, -1)
    c_pos = jnp.maximum(lon(north, 1, -1), 0.0)
    d_neg = jnp.minimum(lon(north, 1, -1), 0.0)
    a_east = lon(a_pos, 2, None)
    c_north = above(c_pos)
    inner = lon(widened, 1, -1)
    west_val = lon(widened, 0, -2)
    east_val = lon(widened, 2, None)
    return (
        inner * (1.0 - a_east + b_neg - c_north + d_neg)
        - b_neg * west_val
        + a_east * east_val
        - d_neg * below(inner)
        + c_north * above(inner)
    )


def four_steps(state, east, north, weight):
    span = state.shape[-3]
    for step in range(2):
        state = forward_core(state, lon(east, step, span - step), lon(north, step, span - step))
    state = lon(weight, 2, span - 2) * state
    for step in range(2, 4):
        state = adjoint_core(state, lon(east, step, span - step), lon(north, step, span - step))
    return state


def coarsen(sketch):
    probe_count, lon_count, level_count, lat_count = sketch.shape
    summed = sketch.reshape(probe_count, lon_count // 4, 4, level_count, lat_count).sum(axis=2)
    rows = lax.broadcasted_iota(jnp.int32, (lat_count, lat_count // 4), 0) // 4
    cols = lax.broadcasted_iota(jnp.int32, (lat_count, lat_count // 4), 1)
    average = jnp.where(rows == cols, 1.0 / 16.0, 0.0).astype(jnp.float32)
    coarse = jnp.dot(
        summed.reshape(-1, lat_count),
        average,
        precision=lax.Precision.HIGHEST,
        preferred_element_type=jnp.float32,
    )
    return coarse.reshape(probe_count, lon_count // 4, level_count, lat_count // 4)


def stencil_kernel(q_ref, a_ref, b_ref, c_ref, d_ref, w_ref, n_ref, k_ref, o_ref):
    span = q_ref.shape[1]
    lat = q_ref.shape[-1]
    field = q_ref[0]
    state = field
    for step in range(2):
        lo, hi = step, span - step
        east_a = a_ref[lo:hi]
        east_b = b_ref[lo:hi]
        north_c = c_ref[lo + 1:hi - 1]
        north_d = d_ref[lo + 1:hi - 1]
        flux_w = east_a[1:] * state[:-1] + east_b[1:] * state[1:]
        inner = state[1:-1]
        flux_s = north_c * pltpu.roll(inner, 1, 2) + north_d * inner
        flux_n = pltpu.roll(flux_s, lat - 1, 2)
        state = inner - (flux_w[1:] - flux_w[:-1]) - (flux_n - flux_s)
    state = w_ref[2:span - 2] * state
    for step in range(2, 4):
        lo, hi = step, span - step
        west_b = b_ref[lo + 1:hi - 1]
        east_a = a_ref[lo + 2:hi]
        north_d = d_ref[lo + 1:hi - 1]
        north_up = n_ref[lo + 1:hi - 1]
        inner = state[1:-1]
        state = (
            inner * k_ref[lo + 1:hi - 1]
            - west_b * state[:-2]
            + east_a * state[2:]
            - north_d * pltpu.roll(inner, 1, 2)
            + north_up * pltpu.roll(inner, lat - 1, 2)
        )
    sketch = field[4:span - 4] + state
    groups = sketch.shape[0] // 4
    for g in range(groups):
        o_ref[0, g] = ((sketch[4 * g] + sketch[4 * g + 1]) + sketch[4 * g + 2]) + sketch[4 * g + 3]


def stencil_sums(slab, east, north, weight):
    probe_count, span, level_count, lat_count = slab.shape
    groups = (span - 8) // 4
    east_a = jnp.maximum(east, 0.0)
    east_b = jnp.minimum(east, 0.0)
    north_c = jnp.maximum(north, 0.0)
    north_d = jnp.minimum(north, 0.0)
    north_up = above(north_c)
    next_a = jnp.concatenate([east_a[1:], jnp.zeros_like(east_a[:1])], axis=0)
    centre = 1.0 - next_a + east_b - north_up + north_d
    winds = (east_a, east_b, north_c, north_d, weight, north_up, centre)
    full = pl.BlockSpec((span, level_count, lat_count), lambda i: (0, 0, 0))
    elements = probe_count * span * level_count * lat_count
    return pl.pallas_call(
        stencil_kernel,
        out_shape=jax.ShapeDtypeStruct((probe_count, groups, level_count, lat_count), slab.dtype),
        grid=(probe_count,),
        in_specs=[pl.BlockSpec((1, span, level_count, lat_count), lambda i: (i, 0, 0, 0))] + [full] * 7,
        out_specs=pl.BlockSpec((1, groups, level_count, lat_count), lambda i: (i, 0, 0, 0)),
        cost_estimate=pl.CostEstimate(
            flops=50 * elements, transcendentals=0, bytes_accessed=4 * elements + 28 * span * level_count * lat_count
        ),
    )(slab, *winds)


def lat_average(summed):
    probe_count, groups, level_count, lat_count = summed.shape
    rows = lax.broadcasted_iota(jnp.int32, (lat_count, lat_count // 4), 0) // 4
    cols = lax.broadcasted_iota(jnp.int32, (lat_count, lat_count // 4), 1)
    average = jnp.where(rows == cols, 1.0 / 16.0, 0.0).astype(jnp.float32)
    coarse = jnp.dot(
        summed.reshape(-1, lat_count),
        average,
        precision=lax.Precision.HIGHEST,
        preferred_element_type=jnp.float32,
    )
    return coarse.reshape(probe_count, groups, level_count, lat_count // 4)


def body(increments, winds, obs_weight):
    probe_count, lon_count, level_count, lat_count = increments.shape
    halo = 4
    pack = (increments, winds[0][None], lat_mask(winds[1])[None], obs_weight[None])
    count = lax.axis_size("lon")
    forward = [(i, (i + 1) % count) for i in range(count)]
    backward = [((i + 1) % count, i) for i in range(count)]
    west_edge = jnp.concatenate([part[:, lon_count - halo:] for part in pack], axis=0)
    east_edge = jnp.concatenate([part[:, :halo] for part in pack], axis=0)
    from_west = lax.ppermute(west_edge, "lon", forward)
    from_east = lax.ppermute(east_edge, "lon", backward)
    bounds = ((0, probe_count), (probe_count, probe_count + 1),
              (probe_count + 1, probe_count + 2), (probe_count + 2, probe_count + 3))

    def fields(parts):
        return parts[0], parts[1][0], parts[2][0], parts[3][0]

    inner = lat_average(stencil_sums(*fields(pack)))
    sides = [
        jnp.stack([
            jnp.concatenate([from_west[lo:hi], part[:, :2 * halo]], axis=1),
            jnp.concatenate([part[:, lon_count - 2 * halo:], from_east[lo:hi]], axis=1),
        ])
        for part, (lo, hi) in zip(pack, bounds)
    ]
    rim = four_steps(sides[0], sides[1], sides[2], sides[3])
    west = coarsen(increments[:, :halo] + rim[0])
    east = coarsen(increments[:, lon_count - halo:] + rim[1])
    coarse = jnp.concatenate([west, inner, east], axis=1)
    coarse = coarse.reshape(probe_count, -1)
    all_probes = probe_count * lax.axis_size("probe")
    ident = jnp.eye(all_probes, dtype=jnp.float32)
    full_panel = lax.all_gather(coarse, "probe", axis=0, tiled=True)
    local_gram = jnp.dot(
        full_panel,
        full_panel.T,
        precision=lax.Precision.HIGHEST,
        preferred_element_type=jnp.float32,
    )
    gram = butterfly_sum(local_gram, "lon")
    lower = lax.linalg.cholesky(gram, symmetrize_input=False)
    inverse = lax.linalg.triangular_solve(lower, ident, left_side=True, lower=True)
    own_rows = lax.dynamic_slice_in_dim(
        inverse, lax.axis_index("probe") * probe_count, probe_count, 0
    )
    basis = jnp.dot(
        own_rows, full_panel, precision=lax.Precision.HIGHEST, preferred_element_type=jnp.float32
    )
    return (basis.reshape(probe_count, lon_count // 4, -1), lower.T)


def solution(mesh):
    in_specs = (P("probe", "lon", None, None), P(None, "lon", None, None), P("lon", None, None))
    out_specs = (P("probe", "lon", None), P())
    return jax.shard_map(body, mesh=mesh, in_specs=in_specs, out_specs=out_specs, check_vma=False)
```

```python
import functools

import jax
import jax.numpy as jnp
from jax import lax
from jax.experimental import pallas as pl
from jax.experimental.pallas import tpu as pltpu
from jax.sharding import PartitionSpec as P

MESH = pl.DeviceIdType.MESH


def from_behind(block, axis, distance):
    devices = range(lax.axis_size(axis))
    route = [((i - distance) % len(devices), i) for i in devices]
    return lax.ppermute(block, axis, route)


def exchange_kernel(count, radix, block_ref, out_ref, held, current, send_sem, recv_sem):
    me = lax.axis_index("lon")
    rounds = []
    stride = 1
    while stride < count:
        width = min(radix, count // stride)
        rounds.append((stride, width))
        stride *= width
    partners = [me ^ (j * stride) for stride, width in rounds for j in range(1, width)]

    barrier = pltpu.get_barrier_semaphore()
    for partner in partners:
        pl.semaphore_signal(barrier, inc=1, device_id={"lon": partner}, device_id_type=MESH)
    pl.semaphore_wait(barrier, len(partners))

    current[0] = block_ref[...]
    slot = 0
    for step, (stride, width) in enumerate(rounds):
        copies = []
        for j in range(1, width):
            copy = pltpu.make_async_remote_copy(
                src_ref=current.at[step],
                dst_ref=held.at[slot + j - 1],
                send_sem=send_sem.at[slot + j - 1],
                recv_sem=recv_sem.at[slot + j - 1],
                device_id={"lon": me ^ (j * stride)},
                device_id_type=MESH,
            )
            copy.start()
            copies.append(copy)
        for copy in copies:
            copy.wait()
        terms = [current[step]] + [held[slot + j - 1] for j in range(1, width)]
        while len(terms) > 1:
            terms = [terms[k] + terms[k + 1] for k in range(0, len(terms), 2)]
        current[step + 1] = terms[0]
        slot += width - 1
    out_ref[...] = current[len(rounds)]


def butterfly_sum(block, axis, radix=4):
    count = lax.axis_size(axis)
    if count & (count - 1) or count < 2:
        return lax.psum(block, axis)
    rounds = 0
    slots = 0
    stride = 1
    while stride < count:
        width = min(radix, count // stride)
        rounds += 1
        slots += width - 1
        stride *= width
    return pl.pallas_call(
        functools.partial(exchange_kernel, count, radix),
        out_shape=jax.ShapeDtypeStruct(block.shape, block.dtype),
        in_specs=[pl.BlockSpec(memory_space=pltpu.VMEM)],
        out_specs=pl.BlockSpec(memory_space=pltpu.VMEM),
        scratch_shapes=[
            pltpu.VMEM((slots,) + block.shape, block.dtype),
            pltpu.VMEM((rounds + 1,) + block.shape, block.dtype),
            pltpu.SemaphoreType.DMA((slots,)),
            pltpu.SemaphoreType.DMA((slots,)),
        ],
        compiler_params=pltpu.CompilerParams(collective_id=0, has_side_effects=True),
    )(block)


def padded(block, sides, width):
    for axis, dim in sides:
        count = lax.axis_size(axis)
        forward = [(i, i + 1) for i in range(count - 1)]
        forward.append((count - 1, 0))
        backward = [(target, source) for source, target in forward]
        low = lax.ppermute(
            lax.slice_in_dim(block, block.shape[dim] - width, None, axis=dim), axis, forward
        )
        high = lax.ppermute(lax.slice_in_dim(block, 0, width, axis=dim), axis, backward)
        block = jnp.concatenate([low, block, high], axis=dim)
    return block


def lat_mask(field):
    rows = lax.broadcasted_iota(jnp.int32, field.shape, field.ndim - 1)
    return jnp.where(rows > 0, field, jnp.zeros_like(field))


def below(field):
    return jnp.concatenate([jnp.zeros_like(field[..., :1]), field[..., :-1]], axis=-1)


def above(field):
    return jnp.concatenate([field[..., 1:], jnp.zeros_like(field[..., :1])], axis=-1)


def lon(x, start, stop):
    first, last, _ = slice(start, stop).indices(x.shape[-3])
    return lax.slice_in_dim(x, first, last, axis=x.ndim - 3)


def forward_core(widened, east, north):
    a_pos = jnp.maximum(east, 0.0)
    b_neg = jnp.minimum(east, 0.0)
    c_pos = jnp.maximum(lon(north, 1, -1), 0.0)
    d_neg = jnp.minimum(lon(north, 1, -1), 0.0)
    flux_w = lon(a_pos, 1, None) * lon(widened, 0, -1) + lon(b_neg, 1, None) * lon(widened, 1, None)
    inner = lon(widened, 1, -1)
    flux_s = c_pos * below(inner) + d_neg * inner
    flux_n = above(flux_s)
    return inner - (lon(flux_w, 1, None) - lon(flux_w, 0, -1)) - (flux_n - flux_s)


def adjoint_core(widened, east, north):
    a_pos = jnp.maximum(east, 0.0)
    b_neg = lon(jnp.minimum(east, 0.0), 1, -1)
    c_pos = jnp.maximum(lon(north, 1, -1), 0.0)
    d_neg = jnp.minimum(lon(north, 1, -1), 0.0)
    a_east = lon(a_pos, 2, None)
    c_north = above(c_pos)
    inner = lon(widened, 1, -1)
    west_val = lon(widened, 0, -2)
    east_val = lon(widened, 2, None)
    return (
        inner * (1.0 - a_east + b_neg - c_north + d_neg)
        - b_neg * west_val
        + a_east * east_val
        - d_neg * below(inner)
        + c_north * above(inner)
    )


def four_steps(state, east, north, weight):
    span = state.shape[-3]
    for step in range(2):
        state = forward_core(state, lon(east, step, span - step), lon(north, step, span - step))
    state = lon(weight, 2, span - 2) * state
    for step in range(2, 4):
        state = adjoint_core(state, lon(east, step, span - step), lon(north, step, span - step))
    return state


def coarsen(sketch):
    probe_count, lon_count, level_count, lat_count = sketch.shape
    summed = sketch.reshape(probe_count, lon_count // 4, 4, level_count, lat_count).sum(axis=2)
    rows = lax.broadcasted_iota(jnp.int32, (lat_count, lat_count // 4), 0) // 4
    cols = lax.broadcasted_iota(jnp.int32, (lat_count, lat_count // 4), 1)
    average = jnp.where(rows == cols, 1.0 / 16.0, 0.0).astype(jnp.float32)
    coarse = jnp.dot(
        summed.reshape(-1, lat_count),
        average,
        precision=lax.Precision.HIGHEST,
        preferred_element_type=jnp.float32,
    )
    return coarse.reshape(probe_count, lon_count // 4, level_count, lat_count // 4)


def stencil_kernel(q_ref, a_ref, b_ref, c_ref, d_ref, w_ref, n_ref, k_ref, o_ref):
    span = q_ref.shape[1]
    lat = q_ref.shape[-1]
    field = q_ref[0]
    state = field
    for step in range(2):
        lo, hi = step, span - step
        east_a = a_ref[lo:hi]
        east_b = b_ref[lo:hi]
        north_c = c_ref[lo + 1:hi - 1]
        north_d = d_ref[lo + 1:hi - 1]
        flux_w = east_a[1:] * state[:-1] + east_b[1:] * state[1:]
        inner = state[1:-1]
        flux_s = north_c * pltpu.roll(inner, 1, 2) + north_d * inner
        flux_n = pltpu.roll(flux_s, lat - 1, 2)
        state = inner - (flux_w[1:] - flux_w[:-1]) - (flux_n - flux_s)
    state = w_ref[2:span - 2] * state
    for step in range(2, 4):
        lo, hi = step, span - step
        west_b = b_ref[lo + 1:hi - 1]
        east_a = a_ref[lo + 2:hi]
        north_d = d_ref[lo + 1:hi - 1]
        north_up = n_ref[lo + 1:hi - 1]
        inner = state[1:-1]
        state = (
            inner * k_ref[lo + 1:hi - 1]
            - west_b * state[:-2]
            + east_a * state[2:]
            - north_d * pltpu.roll(inner, 1, 2)
            + north_up * pltpu.roll(inner, lat - 1, 2)
        )
    sketch = field[4:span - 4] + state
    groups = sketch.shape[0] // 4
    for g in range(groups):
        o_ref[0, g] = ((sketch[4 * g] + sketch[4 * g + 1]) + sketch[4 * g + 2]) + sketch[4 * g + 3]


def stencil_sums(slab, east, north, weight):
    probe_count, span, level_count, lat_count = slab.shape
    groups = (span - 8) // 4
    east_a = jnp.maximum(east, 0.0)
    east_b = jnp.minimum(east, 0.0)
    north_c = jnp.maximum(north, 0.0)
    north_d = jnp.minimum(north, 0.0)
    north_up = above(north_c)
    next_a = jnp.concatenate([east_a[1:], jnp.zeros_like(east_a[:1])], axis=0)
    centre = 1.0 - next_a + east_b - north_up + north_d
    winds = (east_a, east_b, north_c, north_d, weight, north_up, centre)
    full = pl.BlockSpec((span, level_count, lat_count), lambda i: (0, 0, 0))
    elements = probe_count * span * level_count * lat_count
    return pl.pallas_call(
        stencil_kernel,
        out_shape=jax.ShapeDtypeStruct((probe_count, groups, level_count, lat_count), slab.dtype),
        grid=(probe_count,),
        in_specs=[pl.BlockSpec((1, span, level_count, lat_count), lambda i: (i, 0, 0, 0))] + [full] * 7,
        out_specs=pl.BlockSpec((1, groups, level_count, lat_count), lambda i: (i, 0, 0, 0)),
        cost_estimate=pl.CostEstimate(
            flops=50 * elements, transcendentals=0, bytes_accessed=4 * elements + 28 * span * level_count * lat_count
        ),
    )(slab, *winds)


def lat_average(summed):
    probe_count, groups, level_count, lat_count = summed.shape
    rows = lax.broadcasted_iota(jnp.int32, (lat_count, lat_count // 4), 0) // 4
    cols = lax.broadcasted_iota(jnp.int32, (lat_count, lat_count // 4), 1)
    average = jnp.where(rows == cols, 1.0 / 16.0, 0.0).astype(jnp.float32)
    coarse = jnp.dot(
        summed.reshape(-1, lat_count),
        average,
        precision=lax.Precision.HIGHEST,
        preferred_element_type=jnp.float32,
    )
    return coarse.reshape(probe_count, groups, level_count, lat_count // 4)


def body(increments, winds, obs_weight):
    probe_count, lon_count, level_count, lat_count = increments.shape
    halo = 4
    pack = (increments, winds[0][None], lat_mask(winds[1])[None], obs_weight[None])
    count = lax.axis_size("lon")
    forward = [(i, (i + 1) % count) for i in range(count)]
    backward = [((i + 1) % count, i) for i in range(count)]
    west_edge = jnp.concatenate([part[:, lon_count - halo:] for part in pack], axis=0)
    east_edge = jnp.concatenate([part[:, :halo] for part in pack], axis=0)
    from_west = lax.ppermute(west_edge, "lon", forward)
    from_east = lax.ppermute(east_edge, "lon", backward)
    bounds = ((0, probe_count), (probe_count, probe_count + 1),
              (probe_count + 1, probe_count + 2), (probe_count + 2, probe_count + 3))

    def fields(parts):
        return parts[0], parts[1][0], parts[2][0], parts[3][0]

    inner = lat_average(stencil_sums(*fields(pack)))
    sides = [
        jnp.stack([
            jnp.concatenate([from_west[lo:hi], part[:, :2 * halo]], axis=1),
            jnp.concatenate([part[:, lon_count - 2 * halo:], from_east[lo:hi]], axis=1),
        ])
        for part, (lo, hi) in zip(pack, bounds)
    ]
    rim = four_steps(sides[0], sides[1], sides[2], sides[3])
    west = coarsen(increments[:, :halo] + rim[0])
    east = coarsen(increments[:, lon_count - halo:] + rim[1])
    coarse = jnp.concatenate([west, inner, east], axis=1)
    coarse = coarse.reshape(probe_count, -1)
    all_probes = probe_count * lax.axis_size("probe")
    ident = jnp.eye(all_probes, dtype=jnp.float32)
    full_panel = lax.all_gather(coarse, "probe", axis=0, tiled=True)
    local_gram = jnp.dot(
        full_panel,
        full_panel.T,
        precision=lax.Precision.HIGHEST,
        preferred_element_type=jnp.float32,
    )
    gram = butterfly_sum(local_gram, "lon")
    lower = lax.linalg.cholesky(gram, symmetrize_input=False)
    inverse = lax.linalg.triangular_solve(lower, ident, left_side=True, lower=True)
    own_rows = lax.dynamic_slice_in_dim(
        inverse, lax.axis_index("probe") * probe_count, probe_count, 0
    )
    basis = lax.dot_general(
        own_rows,
        full_panel.reshape(all_probes, lon_count // 4, -1),
        (((1,), (0,)), ((), ())),
        precision=lax.Precision.HIGHEST,
        preferred_element_type=jnp.float32,
    )
    return (basis, lower.T)


def solution(mesh):
    in_specs = (P("probe", "lon", None, None), P(None, "lon", None, None), P("lon", None, None))
    out_specs = (P("probe", "lon", None), P())
    return jax.shard_map(body, mesh=mesh, in_specs=in_specs, out_specs=out_specs, check_vma=False)
```

```python
import functools

import jax
import jax.numpy as jnp
from jax import lax
from jax.experimental import pallas as pl
from jax.experimental.pallas import tpu as pltpu
from jax.sharding import PartitionSpec as P

MESH = pl.DeviceIdType.MESH


def from_behind(block, axis, distance):
    devices = range(lax.axis_size(axis))
    route = [((i - distance) % len(devices), i) for i in devices]
    return lax.ppermute(block, axis, route)


def exchange_kernel(count, radix, block_ref, out_ref, held, current, send_sem, recv_sem):
    me = lax.axis_index("lon")
    rounds = []
    stride = 1
    while stride < count:
        width = min(radix, count // stride)
        rounds.append((stride, width))
        stride *= width
    partners = [me ^ (j * stride) for stride, width in rounds for j in range(1, width)]

    barrier = pltpu.get_barrier_semaphore()
    for partner in partners:
        pl.semaphore_signal(barrier, inc=1, device_id={"lon": partner}, device_id_type=MESH)
    pl.semaphore_wait(barrier, len(partners))

    current[0] = block_ref[...]
    slot = 0
    for step, (stride, width) in enumerate(rounds):
        copies = []
        for j in range(1, width):
            copy = pltpu.make_async_remote_copy(
                src_ref=current.at[step],
                dst_ref=held.at[slot + j - 1],
                send_sem=send_sem.at[slot + j - 1],
                recv_sem=recv_sem.at[slot + j - 1],
                device_id={"lon": me ^ (j * stride)},
                device_id_type=MESH,
            )
            copy.start()
            copies.append(copy)
        for copy in copies:
            copy.wait()
        terms = [current[step]] + [held[slot + j - 1] for j in range(1, width)]
        while len(terms) > 1:
            terms = [terms[k] + terms[k + 1] for k in range(0, len(terms), 2)]
        current[step + 1] = terms[0]
        slot += width - 1
    out_ref[...] = current[len(rounds)]


def butterfly_sum(block, axis, radix=4):
    count = lax.axis_size(axis)
    if count & (count - 1) or count < 2:
        return lax.psum(block, axis)
    rounds = 0
    slots = 0
    stride = 1
    while stride < count:
        width = min(radix, count // stride)
        rounds += 1
        slots += width - 1
        stride *= width
    return pl.pallas_call(
        functools.partial(exchange_kernel, count, radix),
        out_shape=jax.ShapeDtypeStruct(block.shape, block.dtype),
        in_specs=[pl.BlockSpec(memory_space=pltpu.VMEM)],
        out_specs=pl.BlockSpec(memory_space=pltpu.VMEM),
        scratch_shapes=[
            pltpu.VMEM((slots,) + block.shape, block.dtype),
            pltpu.VMEM((rounds + 1,) + block.shape, block.dtype),
            pltpu.SemaphoreType.DMA((slots,)),
            pltpu.SemaphoreType.DMA((slots,)),
        ],
        compiler_params=pltpu.CompilerParams(collective_id=0, has_side_effects=True),
    )(block)


def padded(block, sides, width):
    for axis, dim in sides:
        count = lax.axis_size(axis)
        forward = [(i, i + 1) for i in range(count - 1)]
        forward.append((count - 1, 0))
        backward = [(target, source) for source, target in forward]
        low = lax.ppermute(
            lax.slice_in_dim(block, block.shape[dim] - width, None, axis=dim), axis, forward
        )
        high = lax.ppermute(lax.slice_in_dim(block, 0, width, axis=dim), axis, backward)
        block = jnp.concatenate([low, block, high], axis=dim)
    return block


def lat_mask(field):
    rows = lax.broadcasted_iota(jnp.int32, field.shape, field.ndim - 1)
    return jnp.where(rows > 0, field, jnp.zeros_like(field))


def below(field):
    return jnp.concatenate([jnp.zeros_like(field[..., :1]), field[..., :-1]], axis=-1)


def above(field):
    return jnp.concatenate([field[..., 1:], jnp.zeros_like(field[..., :1])], axis=-1)


def lon(x, start, stop):
    first, last, _ = slice(start, stop).indices(x.shape[-3])
    return lax.slice_in_dim(x, first, last, axis=x.ndim - 3)


def forward_core(widened, east, north):
    a_pos = jnp.maximum(east, 0.0)
    b_neg = jnp.minimum(east, 0.0)
    c_pos = jnp.maximum(lon(north, 1, -1), 0.0)
    d_neg = jnp.minimum(lon(north, 1, -1), 0.0)
    flux_w = lon(a_pos, 1, None) * lon(widened, 0, -1) + lon(b_neg, 1, None) * lon(widened, 1, None)
    inner = lon(widened, 1, -1)
    flux_s = c_pos * below(inner) + d_neg * inner
    flux_n = above(flux_s)
    return inner - (lon(flux_w, 1, None) - lon(flux_w, 0, -1)) - (flux_n - flux_s)


def adjoint_core(widened, east, north):
    a_pos = jnp.maximum(east, 0.0)
    b_neg = lon(jnp.minimum(east, 0.0), 1, -1)
    c_pos = jnp.maximum(lon(north, 1, -1), 0.0)
    d_neg = jnp.minimum(lon(north, 1, -1), 0.0)
    a_east = lon(a_pos, 2, None)
    c_north = above(c_pos)
    inner = lon(widened, 1, -1)
    west_val = lon(widened, 0, -2)
    east_val = lon(widened, 2, None)
    return (
        inner * (1.0 - a_east + b_neg - c_north + d_neg)
        - b_neg * west_val
        + a_east * east_val
        - d_neg * below(inner)
        + c_north * above(inner)
    )


def four_steps(state, east, north, weight):
    span = state.shape[-3]
    for step in range(2):
        state = forward_core(state, lon(east, step, span - step), lon(north, step, span - step))
    state = lon(weight, 2, span - 2) * state
    for step in range(2, 4):
        state = adjoint_core(state, lon(east, step, span - step), lon(north, step, span - step))
    return state


def coarsen(sketch):
    probe_count, lon_count, level_count, lat_count = sketch.shape
    summed = sketch.reshape(probe_count, lon_count // 4, 4, level_count, lat_count).sum(axis=2)
    rows = lax.broadcasted_iota(jnp.int32, (lat_count, lat_count // 4), 0) // 4
    cols = lax.broadcasted_iota(jnp.int32, (lat_count, lat_count // 4), 1)
    average = jnp.where(rows == cols, 1.0 / 16.0, 0.0).astype(jnp.float32)
    coarse = jnp.dot(
        summed.reshape(-1, lat_count),
        average,
        precision=lax.Precision.HIGHEST,
        preferred_element_type=jnp.float32,
    )
    return coarse.reshape(probe_count, lon_count // 4, level_count, lat_count // 4)


def stencil_kernel(q_ref, a_ref, b_ref, c_ref, d_ref, w_ref, n_ref, k_ref, o_ref):
    span = q_ref.shape[1]
    lat = q_ref.shape[-1]
    field = q_ref[0]
    state = field
    for step in range(2):
        lo, hi = step, span - step
        east_a = a_ref[lo:hi]
        east_b = b_ref[lo:hi]
        north_c = c_ref[lo + 1:hi - 1]
        north_d = d_ref[lo + 1:hi - 1]
        flux_w = east_a[1:] * state[:-1] + east_b[1:] * state[1:]
        inner = state[1:-1]
        flux_s = north_c * pltpu.roll(inner, 1, 2) + north_d * inner
        flux_n = pltpu.roll(flux_s, lat - 1, 2)
        state = inner - (flux_w[1:] - flux_w[:-1]) - (flux_n - flux_s)
    state = w_ref[2:span - 2] * state
    for step in range(2, 4):
        lo, hi = step, span - step
        west_b = b_ref[lo + 1:hi - 1]
        east_a = a_ref[lo + 2:hi]
        north_d = d_ref[lo + 1:hi - 1]
        north_up = n_ref[lo + 1:hi - 1]
        inner = state[1:-1]
        state = (
            inner * k_ref[lo + 1:hi - 1]
            - west_b * state[:-2]
            + east_a * state[2:]
            - north_d * pltpu.roll(inner, 1, 2)
            + north_up * pltpu.roll(inner, lat - 1, 2)
        )
    sketch = field[4:span - 4] + state
    groups = sketch.shape[0] // 4
    for g in range(groups):
        o_ref[0, g] = ((sketch[4 * g] + sketch[4 * g + 1]) + sketch[4 * g + 2]) + sketch[4 * g + 3]


def stencil_sums(slab, east, north, weight):
    probe_count, span, level_count, lat_count = slab.shape
    groups = (span - 8) // 4
    east_a = jnp.maximum(east, 0.0)
    east_b = jnp.minimum(east, 0.0)
    north_c = jnp.maximum(north, 0.0)
    north_d = jnp.minimum(north, 0.0)
    north_up = above(north_c)
    next_a = jnp.concatenate([east_a[1:], jnp.zeros_like(east_a[:1])], axis=0)
    centre = 1.0 - next_a + east_b - north_up + north_d
    winds = (east_a, east_b, north_c, north_d, weight, north_up, centre)
    full = pl.BlockSpec((span, level_count, lat_count), lambda i: (0, 0, 0))
    elements = probe_count * span * level_count * lat_count
    return pl.pallas_call(
        stencil_kernel,
        out_shape=jax.ShapeDtypeStruct((probe_count, groups, level_count, lat_count), slab.dtype),
        grid=(probe_count,),
        in_specs=[pl.BlockSpec((1, span, level_count, lat_count), lambda i: (i, 0, 0, 0))] + [full] * 7,
        out_specs=pl.BlockSpec((1, groups, level_count, lat_count), lambda i: (i, 0, 0, 0)),
        cost_estimate=pl.CostEstimate(
            flops=50 * elements, transcendentals=0, bytes_accessed=4 * elements + 28 * span * level_count * lat_count
        ),
    )(slab, *winds)


def lat_average(summed):
    probe_count, groups, level_count, lat_count = summed.shape
    rows = lax.broadcasted_iota(jnp.int32, (lat_count, lat_count // 4), 0) // 4
    cols = lax.broadcasted_iota(jnp.int32, (lat_count, lat_count // 4), 1)
    average = jnp.where(rows == cols, 1.0 / 16.0, 0.0).astype(jnp.float32)
    coarse = jnp.dot(
        summed.reshape(-1, lat_count),
        average,
        precision=lax.Precision.HIGHEST,
        preferred_element_type=jnp.float32,
    )
    return coarse.reshape(probe_count, groups, level_count, lat_count // 4)


def body(increments, winds, obs_weight):
    probe_count, lon_count, level_count, lat_count = increments.shape
    halo = 4
    pack = (increments, winds[0][None], lat_mask(winds[1])[None], obs_weight[None])
    count = lax.axis_size("lon")
    forward = [(i, (i + 1) % count) for i in range(count)]
    backward = [((i + 1) % count, i) for i in range(count)]
    west_width = (halo, halo - 1, halo - 1, halo - 2)
    east_width = (halo, halo, halo - 1, halo - 2)
    west_edge = jnp.concatenate(
        [part[:, lon_count - width:].reshape((-1,) + part.shape[2:])
         for part, width in zip(pack, west_width)], axis=0)
    east_edge = jnp.concatenate(
        [part[:, :width].reshape((-1,) + part.shape[2:])
         for part, width in zip(pack, east_width)], axis=0)
    from_west = lax.ppermute(west_edge, "lon", forward)
    from_east = lax.ppermute(east_edge, "lon", backward)

    def unpack(flat, widths, west_side):
        parts, row = [], 0
        for part, width in zip(pack, widths):
            rows = part.shape[0] * width
            piece = flat[row:row + rows].reshape((part.shape[0], width) + part.shape[2:])
            fill = jnp.zeros((part.shape[0], halo - width) + part.shape[2:], part.dtype)
            parts.append(jnp.concatenate([fill, piece] if west_side else [piece, fill], axis=1))
            row += rows
        return parts

    west_parts = unpack(from_west, west_width, True)
    east_parts = unpack(from_east, east_width, False)

    def fields(parts):
        return parts[0], parts[1][0], parts[2][0], parts[3][0]

    inner = lat_average(stencil_sums(*fields(pack)))
    sides = [
        jnp.stack([
            jnp.concatenate([west_part, part[:, :2 * halo]], axis=1),
            jnp.concatenate([part[:, lon_count - 2 * halo:], east_part], axis=1),
        ])
        for part, west_part, east_part in zip(pack, west_parts, east_parts)
    ]
    rim = four_steps(sides[0], sides[1], sides[2], sides[3])
    west = coarsen(increments[:, :halo] + rim[0])
    east = coarsen(increments[:, lon_count - halo:] + rim[1])
    coarse = jnp.concatenate([west, inner, east], axis=1)
    coarse = coarse.reshape(probe_count, -1)
    all_probes = probe_count * lax.axis_size("probe")
    ident = jnp.eye(all_probes, dtype=jnp.float32)
    full_panel = lax.all_gather(coarse, "probe", axis=0, tiled=True)
    local_gram = jnp.dot(
        full_panel,
        full_panel.T,
        precision=lax.Precision.HIGHEST,
        preferred_element_type=jnp.float32,
    )
    gram = butterfly_sum(local_gram, "lon")
    lower = lax.linalg.cholesky(gram, symmetrize_input=False)
    inverse = lax.linalg.triangular_solve(lower, ident, left_side=True, lower=True)
    own_rows = lax.dynamic_slice_in_dim(
        inverse, lax.axis_index("probe") * probe_count, probe_count, 0
    )
    basis = jnp.dot(
        own_rows, full_panel, precision=lax.Precision.HIGHEST, preferred_element_type=jnp.float32
    )
    return (basis.reshape(probe_count, lon_count // 4, -1), lower.T)


def solution(mesh):
    in_specs = (P("probe", "lon", None, None), P(None, "lon", None, None), P("lon", None, None))
    out_specs = (P("probe", "lon", None), P())
    return jax.shard_map(body, mesh=mesh, in_specs=in_specs, out_specs=out_specs, check_vma=False)
```

```python
import functools

import jax
import jax.numpy as jnp
from jax import lax
from jax.experimental import pallas as pl
from jax.experimental.pallas import tpu as pltpu
from jax.sharding import PartitionSpec as P

MESH = pl.DeviceIdType.MESH


def from_behind(block, axis, distance):
    devices = range(lax.axis_size(axis))
    route = [((i - distance) % len(devices), i) for i in devices]
    return lax.ppermute(block, axis, route)


def exchange_kernel(count, radix, block_ref, out_ref, held, current, send_sem, recv_sem):
    me = lax.axis_index("lon")
    rounds = []
    stride = 1
    while stride < count:
        width = min(radix, count // stride)
        rounds.append((stride, width))
        stride *= width
    partners = [me ^ (j * stride) for stride, width in rounds for j in range(1, width)]

    barrier = pltpu.get_barrier_semaphore()
    for partner in partners:
        pl.semaphore_signal(barrier, inc=1, device_id={"lon": partner}, device_id_type=MESH)
    pl.semaphore_wait(barrier, len(partners))

    current[0] = block_ref[...]
    slot = 0
    for step, (stride, width) in enumerate(rounds):
        copies = []
        for j in range(1, width):
            copy = pltpu.make_async_remote_copy(
                src_ref=current.at[step],
                dst_ref=held.at[slot + j - 1],
                send_sem=send_sem.at[slot + j - 1],
                recv_sem=recv_sem.at[slot + j - 1],
                device_id={"lon": me ^ (j * stride)},
                device_id_type=MESH,
            )
            copy.start()
            copies.append(copy)
        for copy in copies:
            copy.wait()
        terms = [current[step]] + [held[slot + j - 1] for j in range(1, width)]
        while len(terms) > 1:
            terms = [terms[k] + terms[k + 1] for k in range(0, len(terms), 2)]
        current[step + 1] = terms[0]
        slot += width - 1
    out_ref[...] = current[len(rounds)]


def butterfly_sum(block, axis, radix=4):
    count = lax.axis_size(axis)
    if count & (count - 1) or count < 2:
        return lax.psum(block, axis)
    rounds = 0
    slots = 0
    stride = 1
    while stride < count:
        width = min(radix, count // stride)
        rounds += 1
        slots += width - 1
        stride *= width
    return pl.pallas_call(
        functools.partial(exchange_kernel, count, radix),
        out_shape=jax.ShapeDtypeStruct(block.shape, block.dtype),
        in_specs=[pl.BlockSpec(memory_space=pltpu.VMEM)],
        out_specs=pl.BlockSpec(memory_space=pltpu.VMEM),
        scratch_shapes=[
            pltpu.VMEM((slots,) + block.shape, block.dtype),
            pltpu.VMEM((rounds + 1,) + block.shape, block.dtype),
            pltpu.SemaphoreType.DMA((slots,)),
            pltpu.SemaphoreType.DMA((slots,)),
        ],
        compiler_params=pltpu.CompilerParams(collective_id=0, has_side_effects=True),
    )(block)


def padded(block, sides, width):
    for axis, dim in sides:
        count = lax.axis_size(axis)
        forward = [(i, i + 1) for i in range(count - 1)]
        forward.append((count - 1, 0))
        backward = [(target, source) for source, target in forward]
        low = lax.ppermute(
            lax.slice_in_dim(block, block.shape[dim] - width, None, axis=dim), axis, forward
        )
        high = lax.ppermute(lax.slice_in_dim(block, 0, width, axis=dim), axis, backward)
        block = jnp.concatenate([low, block, high], axis=dim)
    return block


def lat_mask(field):
    rows = lax.broadcasted_iota(jnp.int32, field.shape, field.ndim - 1)
    return jnp.where(rows > 0, field, jnp.zeros_like(field))


def below(field):
    return jnp.concatenate([jnp.zeros_like(field[..., :1]), field[..., :-1]], axis=-1)


def above(field):
    return jnp.concatenate([field[..., 1:], jnp.zeros_like(field[..., :1])], axis=-1)


def lon(x, start, stop):
    first, last, _ = slice(start, stop).indices(x.shape[-3])
    return lax.slice_in_dim(x, first, last, axis=x.ndim - 3)


def forward_core(widened, east, north):
    a_pos = jnp.maximum(east, 0.0)
    b_neg = jnp.minimum(east, 0.0)
    c_pos = jnp.maximum(lon(north, 1, -1), 0.0)
    d_neg = jnp.minimum(lon(north, 1, -1), 0.0)
    flux_w = lon(a_pos, 1, None) * lon(widened, 0, -1) + lon(b_neg, 1, None) * lon(widened, 1, None)
    inner = lon(widened, 1, -1)
    flux_s = c_pos * below(inner) + d_neg * inner
    flux_n = above(flux_s)
    return inner - (lon(flux_w, 1, None) - lon(flux_w, 0, -1)) - (flux_n - flux_s)


def adjoint_core(widened, east, north):
    a_pos = jnp.maximum(east, 0.0)
    b_neg = lon(jnp.minimum(east, 0.0), 1, -1)
    c_pos = jnp.maximum(lon(north, 1, -1), 0.0)
    d_neg = jnp.minimum(lon(north, 1, -1), 0.0)
    a_east = lon(a_pos, 2, None)
    c_north = above(c_pos)
    inner = lon(widened, 1, -1)
    west_val = lon(widened, 0, -2)
    east_val = lon(widened, 2, None)
    return (
        inner * (1.0 - a_east + b_neg - c_north + d_neg)
        - b_neg * west_val
        + a_east * east_val
        - d_neg * below(inner)
        + c_north * above(inner)
    )


def four_steps(state, east, north, weight):
    span = state.shape[-3]
    for step in range(2):
        state = forward_core(state, lon(east, step, span - step), lon(north, step, span - step))
    state = lon(weight, 2, span - 2) * state
    for step in range(2, 4):
        state = adjoint_core(state, lon(east, step, span - step), lon(north, step, span - step))
    return state


def coarsen(sketch):
    probe_count, lon_count, level_count, lat_count = sketch.shape
    summed = sketch.reshape(probe_count, lon_count // 4, 4, level_count, lat_count).sum(axis=2)
    rows = lax.broadcasted_iota(jnp.int32, (lat_count, lat_count // 4), 0) // 4
    cols = lax.broadcasted_iota(jnp.int32, (lat_count, lat_count // 4), 1)
    average = jnp.where(rows == cols, 1.0 / 16.0, 0.0).astype(jnp.float32)
    coarse = jnp.dot(
        summed.reshape(-1, lat_count),
        average,
        precision=lax.Precision.HIGHEST,
        preferred_element_type=jnp.float32,
    )
    return coarse.reshape(probe_count, lon_count // 4, level_count, lat_count // 4)


def stencil_kernel(q_ref, a_ref, b_ref, c_ref, d_ref, w_ref, n_ref, k_ref, o_ref):
    span = q_ref.shape[1]
    lat = q_ref.shape[-1]
    field = q_ref[0]
    state = field
    for step in range(2):
        lo, hi = step, span - step
        east_a = a_ref[lo:hi]
        east_b = b_ref[lo:hi]
        north_c = c_ref[lo + 1:hi - 1]
        north_d = d_ref[lo + 1:hi - 1]
        flux_w = east_a[1:] * state[:-1] + east_b[1:] * state[1:]
        inner = state[1:-1]
        flux_s = north_c * pltpu.roll(inner, 1, 2) + north_d * inner
        flux_n = pltpu.roll(flux_s, lat - 1, 2)
        state = inner - (flux_w[1:] - flux_w[:-1]) - (flux_n - flux_s)
    state = w_ref[2:span - 2] * state
    for step in range(2, 4):
        lo, hi = step, span - step
        west_b = b_ref[lo + 1:hi - 1]
        east_a = a_ref[lo + 2:hi]
        north_d = d_ref[lo + 1:hi - 1]
        north_up = n_ref[lo + 1:hi - 1]
        inner = state[1:-1]
        state = (
            inner * k_ref[lo + 1:hi - 1]
            - west_b * state[:-2]
            + east_a * state[2:]
            - north_d * pltpu.roll(inner, 1, 2)
            + north_up * pltpu.roll(inner, lat - 1, 2)
        )
    sketch = field[4:span - 4] + state
    groups = sketch.shape[0] // 4
    for g in range(groups):
        o_ref[0, g] = ((sketch[4 * g] + sketch[4 * g + 1]) + sketch[4 * g + 2]) + sketch[4 * g + 3]


def stencil_sums(slab, east, north, weight):
    rows, span, level_count, lat_count = slab.shape
    per_run = rows // east.shape[0]
    groups = (span - 8) // 4
    east_a = jnp.maximum(east, 0.0)
    east_b = jnp.minimum(east, 0.0)
    north_c = jnp.maximum(north, 0.0)
    north_d = jnp.minimum(north, 0.0)
    north_up = above(north_c)
    next_a = jnp.concatenate([east_a[:, 1:], jnp.zeros_like(east_a[:, :1])], axis=1)
    centre = 1.0 - next_a + east_b - north_up + north_d
    winds = (east_a, east_b, north_c, north_d, weight, north_up, centre)
    full = pl.BlockSpec((None, span, level_count, lat_count), lambda i: (i // per_run, 0, 0, 0))
    elements = rows * span * level_count * lat_count
    return pl.pallas_call(
        stencil_kernel,
        out_shape=jax.ShapeDtypeStruct((rows, groups, level_count, lat_count), slab.dtype),
        grid=(rows,),
        in_specs=[pl.BlockSpec((1, span, level_count, lat_count), lambda i: (i, 0, 0, 0))] + [full] * 7,
        out_specs=pl.BlockSpec((1, groups, level_count, lat_count), lambda i: (i, 0, 0, 0)),
        cost_estimate=pl.CostEstimate(
            flops=50 * elements, transcendentals=0, bytes_accessed=4 * elements + 28 * east.size
        ),
    )(slab, *winds)


def lat_average(summed):
    probe_count, groups, level_count, lat_count = summed.shape
    rows = lax.broadcasted_iota(jnp.int32, (lat_count, lat_count // 4), 0) // 4
    cols = lax.broadcasted_iota(jnp.int32, (lat_count, lat_count // 4), 1)
    average = jnp.where(rows == cols, 1.0 / 16.0, 0.0).astype(jnp.float32)
    coarse = jnp.dot(
        summed.reshape(-1, lat_count),
        average,
        precision=lax.Precision.HIGHEST,
        preferred_element_type=jnp.float32,
    )
    return coarse.reshape(probe_count, groups, level_count, lat_count // 4)


def body(increments, winds, obs_weight):
    probe_count, lon_count, level_count, lat_count = increments.shape
    halo = 4
    pack = (increments, winds[0][None], lat_mask(winds[1])[None], obs_weight[None])
    count = lax.axis_size("lon")
    forward = [(i, (i + 1) % count) for i in range(count)]
    backward = [((i + 1) % count, i) for i in range(count)]
    west_edge = jnp.concatenate([part[:, lon_count - halo:] for part in pack], axis=0)
    east_edge = jnp.concatenate([part[:, :halo] for part in pack], axis=0)
    from_west = lax.ppermute(west_edge, "lon", forward)
    from_east = lax.ppermute(east_edge, "lon", backward)
    bounds = ((0, probe_count), (probe_count, probe_count + 1),
              (probe_count + 1, probe_count + 2), (probe_count + 2, probe_count + 3))

    def fields(parts):
        return parts[0], parts[1][0], parts[2][0], parts[3][0]

    inner = lat_average(stencil_sums(pack[0], pack[1], pack[2], pack[3]))
    sides = [
        jnp.stack([
            jnp.concatenate([from_west[lo:hi], part[:, :2 * halo]], axis=1),
            jnp.concatenate([part[:, lon_count - 2 * halo:], from_east[lo:hi]], axis=1),
        ])
        for part, (lo, hi) in zip(pack, bounds)
    ]
    rim = stencil_sums(
        sides[0].reshape((-1,) + sides[0].shape[2:]),
        sides[1][:, 0], sides[2][:, 0], sides[3][:, 0],
    )
    rim = lat_average(rim)
    west, east = rim[:probe_count], rim[probe_count:]
    coarse = jnp.concatenate([west, inner, east], axis=1)
    coarse = coarse.reshape(probe_count, -1)
    all_probes = probe_count * lax.axis_size("probe")
    ident = jnp.eye(all_probes, dtype=jnp.float32)
    full_panel = lax.all_gather(coarse, "probe", axis=0, tiled=True)
    local_gram = jnp.dot(
        full_panel,
        full_panel.T,
        precision=lax.Precision.HIGHEST,
        preferred_element_type=jnp.float32,
    )
    gram = butterfly_sum(local_gram, "lon")
    lower = lax.linalg.cholesky(gram, symmetrize_input=False)
    inverse = lax.linalg.triangular_solve(lower, ident, left_side=True, lower=True)
    own_rows = lax.dynamic_slice_in_dim(
        inverse, lax.axis_index("probe") * probe_count, probe_count, 0
    )
    basis = jnp.dot(
        own_rows, full_panel, precision=lax.Precision.HIGHEST, preferred_element_type=jnp.float32
    )
    return (basis.reshape(probe_count, lon_count // 4, -1), lower.T)


def solution(mesh):
    in_specs = (P("probe", "lon", None, None), P(None, "lon", None, None), P("lon", None, None))
    out_specs = (P("probe", "lon", None), P())
    return jax.shard_map(body, mesh=mesh, in_specs=in_specs, out_specs=out_specs, check_vma=False)
```

```python
import functools

import jax
import jax.numpy as jnp
from jax import lax
from jax.experimental import pallas as pl
from jax.experimental.pallas import tpu as pltpu
from jax.sharding import PartitionSpec as P

MESH = pl.DeviceIdType.MESH


def from_behind(block, axis, distance):
    devices = range(lax.axis_size(axis))
    route = [((i - distance) % len(devices), i) for i in devices]
    return lax.ppermute(block, axis, route)


def exchange_kernel(count, radix, block_ref, out_ref, held, current, send_sem, recv_sem):
    me = lax.axis_index("lon")
    rounds = []
    stride = 1
    while stride < count:
        width = min(radix, count // stride)
        rounds.append((stride, width))
        stride *= width
    partners = [me ^ (j * stride) for stride, width in rounds for j in range(1, width)]

    barrier = pltpu.get_barrier_semaphore()
    for partner in partners:
        pl.semaphore_signal(barrier, inc=1, device_id={"lon": partner}, device_id_type=MESH)
    pl.semaphore_wait(barrier, len(partners))

    current[0] = block_ref[...]
    slot = 0
    for step, (stride, width) in enumerate(rounds):
        copies = []
        for j in range(1, width):
            copy = pltpu.make_async_remote_copy(
                src_ref=current.at[step],
                dst_ref=held.at[slot + j - 1],
                send_sem=send_sem.at[slot + j - 1],
                recv_sem=recv_sem.at[slot + j - 1],
                device_id={"lon": me ^ (j * stride)},
                device_id_type=MESH,
            )
            copy.start()
            copies.append(copy)
        for copy in copies:
            copy.wait()
        terms = [current[step]] + [held[slot + j - 1] for j in range(1, width)]
        while len(terms) > 1:
            terms = [terms[k] + terms[k + 1] for k in range(0, len(terms), 2)]
        current[step + 1] = terms[0]
        slot += width - 1
    out_ref[...] = current[len(rounds)]


def butterfly_sum(block, axis, radix=4):
    count = lax.axis_size(axis)
    if count & (count - 1) or count < 2:
        return lax.psum(block, axis)
    rounds = 0
    slots = 0
    stride = 1
    while stride < count:
        width = min(radix, count // stride)
        rounds += 1
        slots += width - 1
        stride *= width
    return pl.pallas_call(
        functools.partial(exchange_kernel, count, radix),
        out_shape=jax.ShapeDtypeStruct(block.shape, block.dtype),
        in_specs=[pl.BlockSpec(memory_space=pltpu.VMEM)],
        out_specs=pl.BlockSpec(memory_space=pltpu.VMEM),
        scratch_shapes=[
            pltpu.VMEM((slots,) + block.shape, block.dtype),
            pltpu.VMEM((rounds + 1,) + block.shape, block.dtype),
            pltpu.SemaphoreType.DMA((slots,)),
            pltpu.SemaphoreType.DMA((slots,)),
        ],
        compiler_params=pltpu.CompilerParams(collective_id=0, has_side_effects=True),
    )(block)


def padded(block, sides, width):
    for axis, dim in sides:
        count = lax.axis_size(axis)
        forward = [(i, i + 1) for i in range(count - 1)]
        forward.append((count - 1, 0))
        backward = [(target, source) for source, target in forward]
        low = lax.ppermute(
            lax.slice_in_dim(block, block.shape[dim] - width, None, axis=dim), axis, forward
        )
        high = lax.ppermute(lax.slice_in_dim(block, 0, width, axis=dim), axis, backward)
        block = jnp.concatenate([low, block, high], axis=dim)
    return block


def lat_mask(field):
    rows = lax.broadcasted_iota(jnp.int32, field.shape, field.ndim - 1)
    return jnp.where(rows > 0, field, jnp.zeros_like(field))


def below(field):
    return jnp.concatenate([jnp.zeros_like(field[..., :1]), field[..., :-1]], axis=-1)


def above(field):
    return jnp.concatenate([field[..., 1:], jnp.zeros_like(field[..., :1])], axis=-1)


def lon(x, start, stop):
    first, last, _ = slice(start, stop).indices(x.shape[-3])
    return lax.slice_in_dim(x, first, last, axis=x.ndim - 3)


def forward_core(widened, east, north):
    a_pos = jnp.maximum(east, 0.0)
    b_neg = jnp.minimum(east, 0.0)
    c_pos = jnp.maximum(lon(north, 1, -1), 0.0)
    d_neg = jnp.minimum(lon(north, 1, -1), 0.0)
    flux_w = lon(a_pos, 1, None) * lon(widened, 0, -1) + lon(b_neg, 1, None) * lon(widened, 1, None)
    inner = lon(widened, 1, -1)
    flux_s = c_pos * below(inner) + d_neg * inner
    flux_n = above(flux_s)
    return inner - (lon(flux_w, 1, None) - lon(flux_w, 0, -1)) - (flux_n - flux_s)


def adjoint_core(widened, east, north):
    a_pos = jnp.maximum(east, 0.0)
    b_neg = lon(jnp.minimum(east, 0.0), 1, -1)
    c_pos = jnp.maximum(lon(north, 1, -1), 0.0)
    d_neg = jnp.minimum(lon(north, 1, -1), 0.0)
    a_east = lon(a_pos, 2, None)
    c_north = above(c_pos)
    inner = lon(widened, 1, -1)
    west_val = lon(widened, 0, -2)
    east_val = lon(widened, 2, None)
    return (
        inner * (1.0 - a_east + b_neg - c_north + d_neg)
        - b_neg * west_val
        + a_east * east_val
        - d_neg * below(inner)
        + c_north * above(inner)
    )


def four_steps(state, east, north, weight):
    span = state.shape[-3]
    for step in range(2):
        state = forward_core(state, lon(east, step, span - step), lon(north, step, span - step))
    state = lon(weight, 2, span - 2) * state
    for step in range(2, 4):
        state = adjoint_core(state, lon(east, step, span - step), lon(north, step, span - step))
    return state


def coarsen(sketch):
    probe_count, lon_count, level_count, lat_count = sketch.shape
    summed = sketch.reshape(probe_count, lon_count // 4, 4, level_count, lat_count).sum(axis=2)
    rows = lax.broadcasted_iota(jnp.int32, (lat_count, lat_count // 4), 0) // 4
    cols = lax.broadcasted_iota(jnp.int32, (lat_count, lat_count // 4), 1)
    average = jnp.where(rows == cols, 1.0 / 16.0, 0.0).astype(jnp.float32)
    coarse = jnp.dot(
        summed.reshape(-1, lat_count),
        average,
        precision=lax.Precision.HIGHEST,
        preferred_element_type=jnp.float32,
    )
    return coarse.reshape(probe_count, lon_count // 4, level_count, lat_count // 4)


def stencil_kernel(q_ref, a_ref, b_ref, c_ref, d_ref, w_ref, n_ref, k_ref, o_ref):
    for row in range(q_ref.shape[0]):
        stencil_row(row, q_ref, a_ref, b_ref, c_ref, d_ref, w_ref, n_ref, k_ref, o_ref)


def stencil_row(row, q_ref, a_ref, b_ref, c_ref, d_ref, w_ref, n_ref, k_ref, o_ref):
    span = q_ref.shape[1]
    lat = q_ref.shape[-1]
    field = q_ref[row]
    state = field
    for step in range(2):
        lo, hi = step, span - step
        east_a = a_ref[lo:hi]
        east_b = b_ref[lo:hi]
        north_c = c_ref[lo + 1:hi - 1]
        north_d = d_ref[lo + 1:hi - 1]
        flux_w = east_a[1:] * state[:-1] + east_b[1:] * state[1:]
        inner = state[1:-1]
        flux_s = north_c * pltpu.roll(inner, 1, 2) + north_d * inner
        flux_n = pltpu.roll(flux_s, lat - 1, 2)
        state = inner - (flux_w[1:] - flux_w[:-1]) - (flux_n - flux_s)
    state = w_ref[2:span - 2] * state
    for step in range(2, 4):
        lo, hi = step, span - step
        west_b = b_ref[lo + 1:hi - 1]
        east_a = a_ref[lo + 2:hi]
        north_d = d_ref[lo + 1:hi - 1]
        north_up = n_ref[lo + 1:hi - 1]
        inner = state[1:-1]
        state = (
            inner * k_ref[lo + 1:hi - 1]
            - west_b * state[:-2]
            + east_a * state[2:]
            - north_d * pltpu.roll(inner, 1, 2)
            + north_up * pltpu.roll(inner, lat - 1, 2)
        )
    sketch = field[4:span - 4] + state
    groups = sketch.shape[0] // 4
    for g in range(groups):
        o_ref[row, g] = ((sketch[4 * g] + sketch[4 * g + 1]) + sketch[4 * g + 2]) + sketch[4 * g + 3]


def stencil_sums(slab, east, north, weight):
    rows, span, level_count, lat_count = slab.shape
    per_run = rows // east.shape[0]
    groups = (span - 8) // 4
    east_a = jnp.maximum(east, 0.0)
    east_b = jnp.minimum(east, 0.0)
    north_c = jnp.maximum(north, 0.0)
    north_d = jnp.minimum(north, 0.0)
    north_up = above(north_c)
    next_a = jnp.concatenate([east_a[:, 1:], jnp.zeros_like(east_a[:, :1])], axis=1)
    centre = 1.0 - next_a + east_b - north_up + north_d
    winds = (east_a, east_b, north_c, north_d, weight, north_up, centre)
    block = 4 if per_run % 4 == 0 else 1
    full = pl.BlockSpec(
        (None, span, level_count, lat_count), lambda i: (i * block // per_run, 0, 0, 0)
    )
    elements = rows * span * level_count * lat_count
    return pl.pallas_call(
        stencil_kernel,
        out_shape=jax.ShapeDtypeStruct((rows, groups, level_count, lat_count), slab.dtype),
        grid=(rows // block,),
        in_specs=[pl.BlockSpec((block, span, level_count, lat_count), lambda i: (i, 0, 0, 0))]
        + [full] * 7,
        out_specs=pl.BlockSpec((block, groups, level_count, lat_count), lambda i: (i, 0, 0, 0)),
        cost_estimate=pl.CostEstimate(
            flops=50 * elements, transcendentals=0, bytes_accessed=4 * elements + 28 * east.size
        ),
    )(slab, *winds)


def lat_average(summed):
    probe_count, groups, level_count, lat_count = summed.shape
    rows = lax.broadcasted_iota(jnp.int32, (lat_count, lat_count // 4), 0) // 4
    cols = lax.broadcasted_iota(jnp.int32, (lat_count, lat_count // 4), 1)
    average = jnp.where(rows == cols, 1.0 / 16.0, 0.0).astype(jnp.float32)
    coarse = jnp.dot(
        summed.reshape(-1, lat_count),
        average,
        precision=lax.Precision.HIGHEST,
        preferred_element_type=jnp.float32,
    )
    return coarse.reshape(probe_count, groups, level_count, lat_count // 4)


def body(increments, winds, obs_weight):
    probe_count, lon_count, level_count, lat_count = increments.shape
    halo = 4
    pack = (increments, winds[0][None], lat_mask(winds[1])[None], obs_weight[None])
    count = lax.axis_size("lon")
    forward = [(i, (i + 1) % count) for i in range(count)]
    backward = [((i + 1) % count, i) for i in range(count)]
    west_edge = jnp.concatenate([part[:, lon_count - halo:] for part in pack], axis=0)
    east_edge = jnp.concatenate([part[:, :halo] for part in pack], axis=0)
    from_west = lax.ppermute(west_edge, "lon", forward)
    from_east = lax.ppermute(east_edge, "lon", backward)
    bounds = ((0, probe_count), (probe_count, probe_count + 1),
              (probe_count + 1, probe_count + 2), (probe_count + 2, probe_count + 3))

    def fields(parts):
        return parts[0], parts[1][0], parts[2][0], parts[3][0]

    inner = lat_average(stencil_sums(pack[0], pack[1], pack[2], pack[3]))
    sides = [
        jnp.stack([
            jnp.concatenate([from_west[lo:hi], part[:, :2 * halo]], axis=1),
            jnp.concatenate([part[:, lon_count - 2 * halo:], from_east[lo:hi]], axis=1),
        ])
        for part, (lo, hi) in zip(pack, bounds)
    ]
    rim = stencil_sums(
        sides[0].reshape((-1,) + sides[0].shape[2:]),
        sides[1][:, 0], sides[2][:, 0], sides[3][:, 0],
    )
    rim = lat_average(rim)
    west, east = rim[:probe_count], rim[probe_count:]
    coarse = jnp.concatenate([west, inner, east], axis=1)
    coarse = coarse.reshape(probe_count, -1)
    all_probes = probe_count * lax.axis_size("probe")
    ident = jnp.eye(all_probes, dtype=jnp.float32)
    full_panel = lax.all_gather(coarse, "probe", axis=0, tiled=True)
    local_gram = jnp.dot(
        full_panel,
        full_panel.T,
        precision=lax.Precision.HIGHEST,
        preferred_element_type=jnp.float32,
    )
    gram = butterfly_sum(local_gram, "lon")
    lower = lax.linalg.cholesky(gram, symmetrize_input=False)
    inverse = lax.linalg.triangular_solve(lower, ident, left_side=True, lower=True)
    own_rows = lax.dynamic_slice_in_dim(
        inverse, lax.axis_index("probe") * probe_count, probe_count, 0
    )
    basis = jnp.dot(
        own_rows, full_panel, precision=lax.Precision.HIGHEST, preferred_element_type=jnp.float32
    )
    return (basis.reshape(probe_count, lon_count // 4, -1), lower.T)


def solution(mesh):
    in_specs = (P("probe", "lon", None, None), P(None, "lon", None, None), P("lon", None, None))
    out_specs = (P("probe", "lon", None), P())
    return jax.shard_map(body, mesh=mesh, in_specs=in_specs, out_specs=out_specs, check_vma=False)
```

```python
import functools

import jax
import jax.numpy as jnp
from jax import lax
from jax.experimental import pallas as pl
from jax.experimental.pallas import tpu as pltpu
from jax.sharding import PartitionSpec as P

MESH = pl.DeviceIdType.MESH


def from_behind(block, axis, distance):
    devices = range(lax.axis_size(axis))
    route = [((i - distance) % len(devices), i) for i in devices]
    return lax.ppermute(block, axis, route)


def exchange_kernel(count, radix, block_ref, out_ref, held, current, send_sem, recv_sem):
    me = lax.axis_index("lon")
    rounds = []
    stride = 1
    while stride < count:
        width = min(radix, count // stride)
        rounds.append((stride, width))
        stride *= width
    partners = [me ^ (j * stride) for stride, width in rounds for j in range(1, width)]

    barrier = pltpu.get_barrier_semaphore()
    for partner in partners:
        pl.semaphore_signal(barrier, inc=1, device_id={"lon": partner}, device_id_type=MESH)
    pl.semaphore_wait(barrier, len(partners))

    current[0] = block_ref[...]
    slot = 0
    for step, (stride, width) in enumerate(rounds):
        copies = []
        for j in range(1, width):
            copy = pltpu.make_async_remote_copy(
                src_ref=current.at[step],
                dst_ref=held.at[slot + j - 1],
                send_sem=send_sem.at[slot + j - 1],
                recv_sem=recv_sem.at[slot + j - 1],
                device_id={"lon": me ^ (j * stride)},
                device_id_type=MESH,
            )
            copy.start()
            copies.append(copy)
        for copy in copies:
            copy.wait()
        terms = [current[step]] + [held[slot + j - 1] for j in range(1, width)]
        while len(terms) > 1:
            terms = [terms[k] + terms[k + 1] for k in range(0, len(terms), 2)]
        current[step + 1] = terms[0]
        slot += width - 1
    out_ref[...] = current[len(rounds)]


def butterfly_sum(block, axis, radix=8):
    count = lax.axis_size(axis)
    if count & (count - 1) or count < 2:
        return lax.psum(block, axis)
    rounds = 0
    slots = 0
    stride = 1
    while stride < count:
        width = min(radix, count // stride)
        rounds += 1
        slots += width - 1
        stride *= width
    return pl.pallas_call(
        functools.partial(exchange_kernel, count, radix),
        out_shape=jax.ShapeDtypeStruct(block.shape, block.dtype),
        in_specs=[pl.BlockSpec(memory_space=pltpu.VMEM)],
        out_specs=pl.BlockSpec(memory_space=pltpu.VMEM),
        scratch_shapes=[
            pltpu.VMEM((slots,) + block.shape, block.dtype),
            pltpu.VMEM((rounds + 1,) + block.shape, block.dtype),
            pltpu.SemaphoreType.DMA((slots,)),
            pltpu.SemaphoreType.DMA((slots,)),
        ],
        compiler_params=pltpu.CompilerParams(collective_id=0, has_side_effects=True),
    )(block)


def padded(block, sides, width):
    for axis, dim in sides:
        count = lax.axis_size(axis)
        forward = [(i, i + 1) for i in range(count - 1)]
        forward.append((count - 1, 0))
        backward = [(target, source) for source, target in forward]
        low = lax.ppermute(
            lax.slice_in_dim(block, block.shape[dim] - width, None, axis=dim), axis, forward
        )
        high = lax.ppermute(lax.slice_in_dim(block, 0, width, axis=dim), axis, backward)
        block = jnp.concatenate([low, block, high], axis=dim)
    return block


def lat_mask(field):
    rows = lax.broadcasted_iota(jnp.int32, field.shape, field.ndim - 1)
    return jnp.where(rows > 0, field, jnp.zeros_like(field))


def below(field):
    return jnp.concatenate([jnp.zeros_like(field[..., :1]), field[..., :-1]], axis=-1)


def above(field):
    return jnp.concatenate([field[..., 1:], jnp.zeros_like(field[..., :1])], axis=-1)


def lon(x, start, stop):
    first, last, _ = slice(start, stop).indices(x.shape[-3])
    return lax.slice_in_dim(x, first, last, axis=x.ndim - 3)


def forward_core(widened, east, north):
    a_pos = jnp.maximum(east, 0.0)
    b_neg = jnp.minimum(east, 0.0)
    c_pos = jnp.maximum(lon(north, 1, -1), 0.0)
    d_neg = jnp.minimum(lon(north, 1, -1), 0.0)
    flux_w = lon(a_pos, 1, None) * lon(widened, 0, -1) + lon(b_neg, 1, None) * lon(widened, 1, None)
    inner = lon(widened, 1, -1)
    flux_s = c_pos * below(inner) + d_neg * inner
    flux_n = above(flux_s)
    return inner - (lon(flux_w, 1, None) - lon(flux_w, 0, -1)) - (flux_n - flux_s)


def adjoint_core(widened, east, north):
    a_pos = jnp.maximum(east, 0.0)
    b_neg = lon(jnp.minimum(east, 0.0), 1, -1)
    c_pos = jnp.maximum(lon(north, 1, -1), 0.0)
    d_neg = jnp.minimum(lon(north, 1, -1), 0.0)
    a_east = lon(a_pos, 2, None)
    c_north = above(c_pos)
    inner = lon(widened, 1, -1)
    west_val = lon(widened, 0, -2)
    east_val = lon(widened, 2, None)
    return (
        inner * (1.0 - a_east + b_neg - c_north + d_neg)
        - b_neg * west_val
        + a_east * east_val
        - d_neg * below(inner)
        + c_north * above(inner)
    )


def four_steps(state, east, north, weight):
    span = state.shape[-3]
    for step in range(2):
        state = forward_core(state, lon(east, step, span - step), lon(north, step, span - step))
    state = lon(weight, 2, span - 2) * state
    for step in range(2, 4):
        state = adjoint_core(state, lon(east, step, span - step), lon(north, step, span - step))
    return state


def coarsen(sketch):
    probe_count, lon_count, level_count, lat_count = sketch.shape
    summed = sketch.reshape(probe_count, lon_count // 4, 4, level_count, lat_count).sum(axis=2)
    rows = lax.broadcasted_iota(jnp.int32, (lat_count, lat_count // 4), 0) // 4
    cols = lax.broadcasted_iota(jnp.int32, (lat_count, lat_count // 4), 1)
    average = jnp.where(rows == cols, 1.0 / 16.0, 0.0).astype(jnp.float32)
    coarse = jnp.dot(
        summed.reshape(-1, lat_count),
        average,
        precision=lax.Precision.HIGHEST,
        preferred_element_type=jnp.float32,
    )
    return coarse.reshape(probe_count, lon_count // 4, level_count, lat_count // 4)


def stencil_kernel(q_ref, a_ref, b_ref, c_ref, d_ref, w_ref, n_ref, k_ref, o_ref):
    span = q_ref.shape[1]
    lat = q_ref.shape[-1]
    field = q_ref[0]
    state = field
    for step in range(2):
        lo, hi = step, span - step
        east_a = a_ref[lo:hi]
        east_b = b_ref[lo:hi]
        north_c = c_ref[lo + 1:hi - 1]
        north_d = d_ref[lo + 1:hi - 1]
        flux_w = east_a[1:] * state[:-1] + east_b[1:] * state[1:]
        inner = state[1:-1]
        flux_s = north_c * pltpu.roll(inner, 1, 2) + north_d * inner
        flux_n = pltpu.roll(flux_s, lat - 1, 2)
        state = inner - (flux_w[1:] - flux_w[:-1]) - (flux_n - flux_s)
    state = w_ref[2:span - 2] * state
    for step in range(2, 4):
        lo, hi = step, span - step
        west_b = b_ref[lo + 1:hi - 1]
        east_a = a_ref[lo + 2:hi]
        north_d = d_ref[lo + 1:hi - 1]
        north_up = n_ref[lo + 1:hi - 1]
        inner = state[1:-1]
        state = (
            inner * k_ref[lo + 1:hi - 1]
            - west_b * state[:-2]
            + east_a * state[2:]
            - north_d * pltpu.roll(inner, 1, 2)
            + north_up * pltpu.roll(inner, lat - 1, 2)
        )
    sketch = field[4:span - 4] + state
    groups = sketch.shape[0] // 4
    for g in range(groups):
        o_ref[0, g] = ((sketch[4 * g] + sketch[4 * g + 1]) + sketch[4 * g + 2]) + sketch[4 * g + 3]


def stencil_sums(slab, east, north, weight):
    probe_count, span, level_count, lat_count = slab.shape
    groups = (span - 8) // 4
    east_a = jnp.maximum(east, 0.0)
    east_b = jnp.minimum(east, 0.0)
    north_c = jnp.maximum(north, 0.0)
    north_d = jnp.minimum(north, 0.0)
    north_up = above(north_c)
    next_a = jnp.concatenate([east_a[1:], jnp.zeros_like(east_a[:1])], axis=0)
    centre = 1.0 - next_a + east_b - north_up + north_d
    winds = (east_a, east_b, north_c, north_d, weight, north_up, centre)
    full = pl.BlockSpec((span, level_count, lat_count), lambda i: (0, 0, 0))
    elements = probe_count * span * level_count * lat_count
    return pl.pallas_call(
        stencil_kernel,
        out_shape=jax.ShapeDtypeStruct((probe_count, groups, level_count, lat_count), slab.dtype),
        grid=(probe_count,),
        in_specs=[pl.BlockSpec((1, span, level_count, lat_count), lambda i: (i, 0, 0, 0))] + [full] * 7,
        out_specs=pl.BlockSpec((1, groups, level_count, lat_count), lambda i: (i, 0, 0, 0)),
        cost_estimate=pl.CostEstimate(
            flops=50 * elements, transcendentals=0, bytes_accessed=4 * elements + 28 * span * level_count * lat_count
        ),
    )(slab, *winds)


def lat_average(summed):
    probe_count, groups, level_count, lat_count = summed.shape
    rows = lax.broadcasted_iota(jnp.int32, (lat_count, lat_count // 4), 0) // 4
    cols = lax.broadcasted_iota(jnp.int32, (lat_count, lat_count // 4), 1)
    average = jnp.where(rows == cols, 1.0 / 16.0, 0.0).astype(jnp.float32)
    coarse = jnp.dot(
        summed.reshape(-1, lat_count),
        average,
        precision=lax.Precision.HIGHEST,
        preferred_element_type=jnp.float32,
    )
    return coarse.reshape(probe_count, groups, level_count, lat_count // 4)


def body(increments, winds, obs_weight):
    probe_count, lon_count, level_count, lat_count = increments.shape
    halo = 4
    pack = (increments, winds[0][None], lat_mask(winds[1])[None], obs_weight[None])
    count = lax.axis_size("lon")
    forward = [(i, (i + 1) % count) for i in range(count)]
    backward = [((i + 1) % count, i) for i in range(count)]
    west_edge = jnp.concatenate([part[:, lon_count - halo:] for part in pack], axis=0)
    east_edge = jnp.concatenate([part[:, :halo] for part in pack], axis=0)
    from_west = lax.ppermute(west_edge, "lon", forward)
    from_east = lax.ppermute(east_edge, "lon", backward)
    bounds = ((0, probe_count), (probe_count, probe_count + 1),
              (probe_count + 1, probe_count + 2), (probe_count + 2, probe_count + 3))

    def fields(parts):
        return parts[0], parts[1][0], parts[2][0], parts[3][0]

    inner = lat_average(stencil_sums(*fields(pack)))
    sides = [
        jnp.stack([
            jnp.concatenate([from_west[lo:hi], part[:, :2 * halo]], axis=1),
            jnp.concatenate([part[:, lon_count - 2 * halo:], from_east[lo:hi]], axis=1),
        ])
        for part, (lo, hi) in zip(pack, bounds)
    ]
    rim = four_steps(sides[0], sides[1], sides[2], sides[3])
    west = coarsen(increments[:, :halo] + rim[0])
    east = coarsen(increments[:, lon_count - halo:] + rim[1])
    coarse = jnp.concatenate([west, inner, east], axis=1)
    coarse = coarse.reshape(probe_count, -1)
    all_probes = probe_count * lax.axis_size("probe")
    ident = jnp.eye(all_probes, dtype=jnp.float32)
    full_panel = lax.all_gather(coarse, "probe", axis=0, tiled=True)
    local_gram = jnp.dot(
        full_panel,
        full_panel.T,
        precision=lax.Precision.HIGHEST,
        preferred_element_type=jnp.float32,
    )
    gram = butterfly_sum(local_gram, "lon")
    lower = lax.linalg.cholesky(gram, symmetrize_input=False)
    inverse = lax.linalg.triangular_solve(lower, ident, left_side=True, lower=True)
    own_rows = lax.dynamic_slice_in_dim(
        inverse, lax.axis_index("probe") * probe_count, probe_count, 0
    )
    basis = jnp.dot(
        own_rows, full_panel, precision=lax.Precision.HIGHEST, preferred_element_type=jnp.float32
    )
    return (basis.reshape(probe_count, lon_count // 4, -1), lower.T)


def solution(mesh):
    in_specs = (P("probe", "lon", None, None), P(None, "lon", None, None), P("lon", None, None))
    out_specs = (P("probe", "lon", None), P())
    return jax.shard_map(body, mesh=mesh, in_specs=in_specs, out_specs=out_specs, check_vma=False)
```

```python
import functools

import jax
import jax.numpy as jnp
from jax import lax
from jax.experimental import pallas as pl
from jax.experimental.pallas import tpu as pltpu
from jax.sharding import PartitionSpec as P

MESH = pl.DeviceIdType.MESH


def from_behind(block, axis, distance):
    devices = range(lax.axis_size(axis))
    route = [((i - distance) % len(devices), i) for i in devices]
    return lax.ppermute(block, axis, route)


def exchange_kernel(count, radix, block_ref, out_ref, held, current, send_sem, recv_sem):
    me = lax.axis_index("lon")
    rounds = []
    stride = 1
    while stride < count:
        width = min(radix, count // stride)
        rounds.append((stride, width))
        stride *= width
    partners = [me ^ (j * stride) for stride, width in rounds for j in range(1, width)]

    barrier = pltpu.get_barrier_semaphore()
    for partner in partners:
        pl.semaphore_signal(barrier, inc=1, device_id={"lon": partner}, device_id_type=MESH)
    pl.semaphore_wait(barrier, len(partners))

    current[0] = block_ref[...]
    slot = 0
    for step, (stride, width) in enumerate(rounds):
        copies = []
        for j in range(1, width):
            copy = pltpu.make_async_remote_copy(
                src_ref=current.at[step],
                dst_ref=held.at[slot + j - 1],
                send_sem=send_sem.at[slot + j - 1],
                recv_sem=recv_sem.at[slot + j - 1],
                device_id={"lon": me ^ (j * stride)},
                device_id_type=MESH,
            )
            copy.start()
            copies.append(copy)
        for copy in copies:
            copy.wait()
        terms = [current[step]] + [held[slot + j - 1] for j in range(1, width)]
        while len(terms) > 1:
            terms = [terms[k] + terms[k + 1] for k in range(0, len(terms), 2)]
        current[step + 1] = terms[0]
        slot += width - 1
    out_ref[...] = current[len(rounds)]


def butterfly_sum(block, axis, radix=4):
    count = lax.axis_size(axis)
    if count & (count - 1) or count < 2:
        return lax.psum(block, axis)
    rounds = 0
    slots = 0
    stride = 1
    while stride < count:
        width = min(radix, count // stride)
        rounds += 1
        slots += width - 1
        stride *= width
    return pl.pallas_call(
        functools.partial(exchange_kernel, count, radix),
        out_shape=jax.ShapeDtypeStruct(block.shape, block.dtype),
        in_specs=[pl.BlockSpec(memory_space=pltpu.VMEM)],
        out_specs=pl.BlockSpec(memory_space=pltpu.VMEM),
        scratch_shapes=[
            pltpu.VMEM((slots,) + block.shape, block.dtype),
            pltpu.VMEM((rounds + 1,) + block.shape, block.dtype),
            pltpu.SemaphoreType.DMA((slots,)),
            pltpu.SemaphoreType.DMA((slots,)),
        ],
        compiler_params=pltpu.CompilerParams(collective_id=0, has_side_effects=True),
    )(block)


def padded(block, sides, width):
    for axis, dim in sides:
        count = lax.axis_size(axis)
        forward = [(i, i + 1) for i in range(count - 1)]
        forward.append((count - 1, 0))
        backward = [(target, source) for source, target in forward]
        low = lax.ppermute(
            lax.slice_in_dim(block, block.shape[dim] - width, None, axis=dim), axis, forward
        )
        high = lax.ppermute(lax.slice_in_dim(block, 0, width, axis=dim), axis, backward)
        block = jnp.concatenate([low, block, high], axis=dim)
    return block


def lat_mask(field):
    rows = lax.broadcasted_iota(jnp.int32, field.shape, field.ndim - 1)
    return jnp.where(rows > 0, field, jnp.zeros_like(field))


def below(field):
    return jnp.concatenate([jnp.zeros_like(field[..., :1]), field[..., :-1]], axis=-1)


def above(field):
    return jnp.concatenate([field[..., 1:], jnp.zeros_like(field[..., :1])], axis=-1)


def lon(x, start, stop):
    first, last, _ = slice(start, stop).indices(x.shape[-3])
    return lax.slice_in_dim(x, first, last, axis=x.ndim - 3)


def forward_core(widened, east, north):
    a_pos = jnp.maximum(east, 0.0)
    b_neg = jnp.minimum(east, 0.0)
    c_pos = jnp.maximum(lon(north, 1, -1), 0.0)
    d_neg = jnp.minimum(lon(north, 1, -1), 0.0)
    flux_w = lon(a_pos, 1, None) * lon(widened, 0, -1) + lon(b_neg, 1, None) * lon(widened, 1, None)
    inner = lon(widened, 1, -1)
    flux_s = c_pos * below(inner) + d_neg * inner
    flux_n = above(flux_s)
    return inner - (lon(flux_w, 1, None) - lon(flux_w, 0, -1)) - (flux_n - flux_s)


def adjoint_core(widened, east, north):
    a_pos = jnp.maximum(east, 0.0)
    b_neg = lon(jnp.minimum(east, 0.0), 1, -1)
    c_pos = jnp.maximum(lon(north, 1, -1), 0.0)
    d_neg = jnp.minimum(lon(north, 1, -1), 0.0)
    a_east = lon(a_pos, 2, None)
    c_north = above(c_pos)
    inner = lon(widened, 1, -1)
    west_val = lon(widened, 0, -2)
    east_val = lon(widened, 2, None)
    return (
        inner * (1.0 - a_east + b_neg - c_north + d_neg)
        - b_neg * west_val
        + a_east * east_val
        - d_neg * below(inner)
        + c_north * above(inner)
    )


def four_steps(state, east, north, weight):
    span = state.shape[-3]
    for step in range(2):
        state = forward_core(state, lon(east, step, span - step), lon(north, step, span - step))
    state = lon(weight, 2, span - 2) * state
    for step in range(2, 4):
        state = adjoint_core(state, lon(east, step, span - step), lon(north, step, span - step))
    return state


def coarsen(sketch):
    probe_count, lon_count, level_count, lat_count = sketch.shape
    summed = sketch.reshape(probe_count, lon_count // 4, 4, level_count, lat_count).sum(axis=2)
    rows = lax.broadcasted_iota(jnp.int32, (lat_count, lat_count // 4), 0) // 4
    cols = lax.broadcasted_iota(jnp.int32, (lat_count, lat_count // 4), 1)
    average = jnp.where(rows == cols, 1.0 / 16.0, 0.0).astype(jnp.float32)
    coarse = jnp.dot(
        summed.reshape(-1, lat_count),
        average,
        precision=lax.Precision.HIGHEST,
        preferred_element_type=jnp.float32,
    )
    return coarse.reshape(probe_count, lon_count // 4, level_count, lat_count // 4)


def stencil_kernel(q_ref, a_ref, b_ref, c_ref, d_ref, w_ref, n_ref, k_ref, o_ref):
    span = q_ref.shape[1]
    lat = q_ref.shape[-1]
    field = q_ref[0]
    state = field
    for step in range(2):
        lo, hi = step, span - step
        east_a = a_ref[lo:hi]
        east_b = b_ref[lo:hi]
        north_c = c_ref[lo + 1:hi - 1]
        north_d = d_ref[lo + 1:hi - 1]
        flux_w = east_a[1:] * state[:-1] + east_b[1:] * state[1:]
        inner = state[1:-1]
        flux_s = north_c * pltpu.roll(inner, 1, 2) + north_d * inner
        flux_n = pltpu.roll(flux_s, lat - 1, 2)
        state = inner - (flux_w[1:] - flux_w[:-1]) - (flux_n - flux_s)
    state = w_ref[2:span - 2] * state
    for step in range(2, 4):
        lo, hi = step, span - step
        west_b = b_ref[lo + 1:hi - 1]
        east_a = a_ref[lo + 2:hi]
        north_d = d_ref[lo + 1:hi - 1]
        north_up = n_ref[lo + 1:hi - 1]
        inner = state[1:-1]
        state = (
            inner * k_ref[lo + 1:hi - 1]
            - west_b * state[:-2]
            + east_a * state[2:]
            - north_d * pltpu.roll(inner, 1, 2)
            + north_up * pltpu.roll(inner, lat - 1, 2)
        )
    sketch = field[4:span - 4] + state
    groups = sketch.shape[0] // 4
    for g in range(groups):
        o_ref[0, g] = ((sketch[4 * g] + sketch[4 * g + 1]) + sketch[4 * g + 2]) + sketch[4 * g + 3]


def stencil_sums(slab, east, north, weight):
    probe_count, span, level_count, lat_count = slab.shape
    groups = (span - 8) // 4
    east_a = jnp.maximum(east, 0.0)
    east_b = jnp.minimum(east, 0.0)
    north_c = jnp.maximum(north, 0.0)
    north_d = jnp.minimum(north, 0.0)
    north_up = above(north_c)
    next_a = jnp.concatenate([east_a[1:], jnp.zeros_like(east_a[:1])], axis=0)
    centre = 1.0 - next_a + east_b - north_up + north_d
    winds = (east_a, east_b, north_c, north_d, weight, north_up, centre)
    full = pl.BlockSpec((span, level_count, lat_count), lambda i: (0, 0, 0))
    elements = probe_count * span * level_count * lat_count
    return pl.pallas_call(
        stencil_kernel,
        out_shape=jax.ShapeDtypeStruct((probe_count, groups, level_count, lat_count), slab.dtype),
        grid=(probe_count,),
        in_specs=[pl.BlockSpec((1, span, level_count, lat_count), lambda i: (i, 0, 0, 0))] + [full] * 7,
        out_specs=pl.BlockSpec((1, groups, level_count, lat_count), lambda i: (i, 0, 0, 0)),
        cost_estimate=pl.CostEstimate(
            flops=50 * elements, transcendentals=0, bytes_accessed=4 * elements + 28 * span * level_count * lat_count
        ),
    )(slab, *winds)


def lat_average(summed):
    probe_count, groups, level_count, lat_count = summed.shape
    rows = lax.broadcasted_iota(jnp.int32, (lat_count, lat_count // 4), 0) // 4
    cols = lax.broadcasted_iota(jnp.int32, (lat_count, lat_count // 4), 1)
    average = jnp.where(rows == cols, 1.0 / 16.0, 0.0).astype(jnp.float32)
    coarse = jnp.dot(
        summed.reshape(-1, lat_count),
        average,
        precision=lax.Precision.HIGHEST,
        preferred_element_type=jnp.float32,
    )
    return coarse.reshape(probe_count, groups, level_count, lat_count // 4)


def body(increments, winds, obs_weight):
    probe_count, lon_count, level_count, lat_count = increments.shape
    halo = 4
    pack = (increments, winds[0][None], lat_mask(winds[1])[None], obs_weight[None])
    count = lax.axis_size("lon")
    forward = [(i, (i + 1) % count) for i in range(count)]
    backward = [((i + 1) % count, i) for i in range(count)]
    west_width = (halo, halo - 1, halo - 1, halo - 2)
    east_width = (halo, halo, halo - 1, halo - 2)
    west_edge = jnp.concatenate(
        [part[:, lon_count - width:].reshape((-1,) + part.shape[2:])
         for part, width in zip(pack, west_width)], axis=0)
    east_edge = jnp.concatenate(
        [part[:, :width].reshape((-1,) + part.shape[2:])
         for part, width in zip(pack, east_width)], axis=0)
    from_west = lax.ppermute(west_edge, "lon", forward)
    from_east = lax.ppermute(east_edge, "lon", backward)

    def unpack(flat, widths, west_side):
        parts, row = [], 0
        for part, width in zip(pack, widths):
            rows = part.shape[0] * width
            piece = flat[row:row + rows].reshape((part.shape[0], width) + part.shape[2:])
            fill = jnp.zeros((part.shape[0], halo - width) + part.shape[2:], part.dtype)
            parts.append(jnp.concatenate([fill, piece] if west_side else [piece, fill], axis=1))
            row += rows
        return parts

    west_parts = unpack(from_west, west_width, True)
    east_parts = unpack(from_east, east_width, False)

    def fields(parts):
        return parts[0], parts[1][0], parts[2][0], parts[3][0]

    inner = lat_average(stencil_sums(*fields(pack)))
    sides = [
        jnp.stack([
            jnp.concatenate([west_part, part[:, :2 * halo]], axis=1),
            jnp.concatenate([part[:, lon_count - 2 * halo:], east_part], axis=1),
        ])
        for part, west_part, east_part in zip(pack, west_parts, east_parts)
    ]
    rim = four_steps(sides[0], sides[1], sides[2], sides[3])
    west = coarsen(increments[:, :halo] + rim[0])
    east = coarsen(increments[:, lon_count - halo:] + rim[1])
    coarse = jnp.concatenate([west, inner, east], axis=1)
    coarse = coarse.reshape(probe_count, -1)
    all_probes = probe_count * lax.axis_size("probe")
    ident = jnp.eye(all_probes, dtype=jnp.float32)
    full_panel = lax.all_gather(coarse, "probe", axis=0, tiled=True)
    local_gram = jnp.dot(
        full_panel,
        full_panel.T,
        precision=lax.Precision.HIGHEST,
        preferred_element_type=jnp.float32,
    )
    gram = butterfly_sum(local_gram, "lon")
    lower = lax.linalg.cholesky(gram, symmetrize_input=False)
    inverse = lax.linalg.triangular_solve(lower, ident, left_side=True, lower=True)
    own_rows = lax.dynamic_slice_in_dim(
        inverse, lax.axis_index("probe") * probe_count, probe_count, 0
    )
    basis = lax.dot_general(
        own_rows,
        full_panel.reshape(all_probes, lon_count // 4, -1),
        (((1,), (0,)), ((), ())),
        precision=lax.Precision.HIGHEST,
        preferred_element_type=jnp.float32,
    )
    return (basis, lower.T)


def solution(mesh):
    in_specs = (P("probe", "lon", None, None), P(None, "lon", None, None), P("lon", None, None))
    out_specs = (P("probe", "lon", None), P())
    return jax.shard_map(body, mesh=mesh, in_specs=in_specs, out_specs=out_specs, check_vma=False)
```

```python
import functools

import jax
import jax.numpy as jnp
from jax import lax
from jax.experimental import pallas as pl
from jax.experimental.pallas import tpu as pltpu
from jax.sharding import PartitionSpec as P

MESH = pl.DeviceIdType.MESH


def from_behind(block, axis, distance):
    devices = range(lax.axis_size(axis))
    route = [((i - distance) % len(devices), i) for i in devices]
    return lax.ppermute(block, axis, route)


def exchange_kernel(count, radix, block_ref, out_ref, held, current, send_sem, recv_sem):
    me = lax.axis_index("lon")
    rounds = []
    stride = 1
    while stride < count:
        width = min(radix, count // stride)
        rounds.append((stride, width))
        stride *= width
    partners = [me ^ (j * stride) for stride, width in rounds for j in range(1, width)]

    barrier = pltpu.get_barrier_semaphore()
    for partner in partners:
        pl.semaphore_signal(barrier, inc=1, device_id={"lon": partner}, device_id_type=MESH)
    pl.semaphore_wait(barrier, len(partners))

    current[0] = block_ref[...]
    slot = 0
    for step, (stride, width) in enumerate(rounds):
        copies = []
        for j in range(1, width):
            copy = pltpu.make_async_remote_copy(
                src_ref=current.at[step],
                dst_ref=held.at[slot + j - 1],
                send_sem=send_sem.at[slot + j - 1],
                recv_sem=recv_sem.at[slot + j - 1],
                device_id={"lon": me ^ (j * stride)},
                device_id_type=MESH,
            )
            copy.start()
            copies.append(copy)
        for copy in copies:
            copy.wait()
        terms = [current[step]] + [held[slot + j - 1] for j in range(1, width)]
        while len(terms) > 1:
            terms = [terms[k] + terms[k + 1] for k in range(0, len(terms), 2)]
        current[step + 1] = terms[0]
        slot += width - 1
    out_ref[...] = current[len(rounds)]


def butterfly_sum(block, axis, radix=4):
    count = lax.axis_size(axis)
    if count & (count - 1) or count < 2:
        return lax.psum(block, axis)
    rounds = 0
    slots = 0
    stride = 1
    while stride < count:
        width = min(radix, count // stride)
        rounds += 1
        slots += width - 1
        stride *= width
    return pl.pallas_call(
        functools.partial(exchange_kernel, count, radix),
        out_shape=jax.ShapeDtypeStruct(block.shape, block.dtype),
        in_specs=[pl.BlockSpec(memory_space=pltpu.VMEM)],
        out_specs=pl.BlockSpec(memory_space=pltpu.VMEM),
        scratch_shapes=[
            pltpu.VMEM((slots,) + block.shape, block.dtype),
            pltpu.VMEM((rounds + 1,) + block.shape, block.dtype),
            pltpu.SemaphoreType.DMA((slots,)),
            pltpu.SemaphoreType.DMA((slots,)),
        ],
        compiler_params=pltpu.CompilerParams(collective_id=0, has_side_effects=True),
    )(block)


def padded(block, sides, width):
    for axis, dim in sides:
        count = lax.axis_size(axis)
        forward = [(i, i + 1) for i in range(count - 1)]
        forward.append((count - 1, 0))
        backward = [(target, source) for source, target in forward]
        low = lax.ppermute(
            lax.slice_in_dim(block, block.shape[dim] - width, None, axis=dim), axis, forward
        )
        high = lax.ppermute(lax.slice_in_dim(block, 0, width, axis=dim), axis, backward)
        block = jnp.concatenate([low, block, high], axis=dim)
    return block


def lat_mask(field):
    rows = lax.broadcasted_iota(jnp.int32, field.shape, field.ndim - 1)
    return jnp.where(rows > 0, field, jnp.zeros_like(field))


def below(field):
    return jnp.concatenate([jnp.zeros_like(field[..., :1]), field[..., :-1]], axis=-1)


def above(field):
    return jnp.concatenate([field[..., 1:], jnp.zeros_like(field[..., :1])], axis=-1)


def lon(x, start, stop):
    first, last, _ = slice(start, stop).indices(x.shape[-3])
    return lax.slice_in_dim(x, first, last, axis=x.ndim - 3)


def forward_core(widened, east, north):
    a_pos = jnp.maximum(east, 0.0)
    b_neg = jnp.minimum(east, 0.0)
    c_pos = jnp.maximum(lon(north, 1, -1), 0.0)
    d_neg = jnp.minimum(lon(north, 1, -1), 0.0)
    flux_w = lon(a_pos, 1, None) * lon(widened, 0, -1) + lon(b_neg, 1, None) * lon(widened, 1, None)
    inner = lon(widened, 1, -1)
    flux_s = c_pos * below(inner) + d_neg * inner
    flux_n = above(flux_s)
    return inner - (lon(flux_w, 1, None) - lon(flux_w, 0, -1)) - (flux_n - flux_s)


def adjoint_core(widened, east, north):
    a_pos = jnp.maximum(east, 0.0)
    b_neg = lon(jnp.minimum(east, 0.0), 1, -1)
    c_pos = jnp.maximum(lon(north, 1, -1), 0.0)
    d_neg = jnp.minimum(lon(north, 1, -1), 0.0)
    a_east = lon(a_pos, 2, None)
    c_north = above(c_pos)
    inner = lon(widened, 1, -1)
    west_val = lon(widened, 0, -2)
    east_val = lon(widened, 2, None)
    return (
        inner * (1.0 - a_east + b_neg - c_north + d_neg)
        - b_neg * west_val
        + a_east * east_val
        - d_neg * below(inner)
        + c_north * above(inner)
    )


def four_steps(state, east, north, weight):
    span = state.shape[-3]
    for step in range(2):
        state = forward_core(state, lon(east, step, span - step), lon(north, step, span - step))
    state = lon(weight, 2, span - 2) * state
    for step in range(2, 4):
        state = adjoint_core(state, lon(east, step, span - step), lon(north, step, span - step))
    return state


def coarsen(sketch):
    probe_count, lon_count, level_count, lat_count = sketch.shape
    summed = sketch.reshape(probe_count, lon_count // 4, 4, level_count, lat_count).sum(axis=2)
    rows = lax.broadcasted_iota(jnp.int32, (lat_count, lat_count // 4), 0) // 4
    cols = lax.broadcasted_iota(jnp.int32, (lat_count, lat_count // 4), 1)
    average = jnp.where(rows == cols, 1.0 / 16.0, 0.0).astype(jnp.float32)
    coarse = jnp.dot(
        summed.reshape(-1, lat_count),
        average,
        precision=lax.Precision.HIGHEST,
        preferred_element_type=jnp.float32,
    )
    return coarse.reshape(probe_count, lon_count // 4, level_count, lat_count // 4)


def stencil_kernel(q_ref, a_ref, b_ref, c_ref, d_ref, w_ref, n_ref, k_ref, o_ref):
    for row in range(q_ref.shape[0]):
        stencil_row(row, q_ref, a_ref, b_ref, c_ref, d_ref, w_ref, n_ref, k_ref, o_ref)


def stencil_row(row, q_ref, a_ref, b_ref, c_ref, d_ref, w_ref, n_ref, k_ref, o_ref):
    span = q_ref.shape[1]
    lat = q_ref.shape[-1]
    field = q_ref[row]
    state = field
    for step in range(2):
        lo, hi = step, span - step
        east_a = a_ref[lo:hi]
        east_b = b_ref[lo:hi]
        north_c = c_ref[lo + 1:hi - 1]
        north_d = d_ref[lo + 1:hi - 1]
        flux_w = east_a[1:] * state[:-1] + east_b[1:] * state[1:]
        inner = state[1:-1]
        flux_s = north_c * pltpu.roll(inner, 1, 2) + north_d * inner
        flux_n = pltpu.roll(flux_s, lat - 1, 2)
        state = inner - (flux_w[1:] - flux_w[:-1]) - (flux_n - flux_s)
    state = w_ref[2:span - 2] * state
    for step in range(2, 4):
        lo, hi = step, span - step
        west_b = b_ref[lo + 1:hi - 1]
        east_a = a_ref[lo + 2:hi]
        north_d = d_ref[lo + 1:hi - 1]
        north_up = n_ref[lo + 1:hi - 1]
        inner = state[1:-1]
        state = (
            inner * k_ref[lo + 1:hi - 1]
            - west_b * state[:-2]
            + east_a * state[2:]
            - north_d * pltpu.roll(inner, 1, 2)
            + north_up * pltpu.roll(inner, lat - 1, 2)
        )
    sketch = field[4:span - 4] + state
    groups = sketch.shape[0] // 4
    for g in range(groups):
        o_ref[row, g] = ((sketch[4 * g] + sketch[4 * g + 1]) + sketch[4 * g + 2]) + sketch[4 * g + 3]


def stencil_sums(slab, east, north, weight):
    probe_count, span, level_count, lat_count = slab.shape
    groups = (span - 8) // 4
    east_a = jnp.maximum(east, 0.0)
    east_b = jnp.minimum(east, 0.0)
    north_c = jnp.maximum(north, 0.0)
    north_d = jnp.minimum(north, 0.0)
    north_up = above(north_c)
    next_a = jnp.concatenate([east_a[1:], jnp.zeros_like(east_a[:1])], axis=0)
    centre = 1.0 - next_a + east_b - north_up + north_d
    winds = (east_a, east_b, north_c, north_d, weight, north_up, centre)
    block = 4 if probe_count % 4 == 0 else 1
    full = pl.BlockSpec((span, level_count, lat_count), lambda i: (0, 0, 0))
    elements = probe_count * span * level_count * lat_count
    return pl.pallas_call(
        stencil_kernel,
        out_shape=jax.ShapeDtypeStruct((probe_count, groups, level_count, lat_count), slab.dtype),
        grid=(probe_count // block,),
        in_specs=[pl.BlockSpec((block, span, level_count, lat_count), lambda i: (i, 0, 0, 0))]
        + [full] * 7,
        out_specs=pl.BlockSpec((block, groups, level_count, lat_count), lambda i: (i, 0, 0, 0)),
        cost_estimate=pl.CostEstimate(
            flops=50 * elements, transcendentals=0, bytes_accessed=4 * elements + 28 * span * level_count * lat_count
        ),
    )(slab, *winds)


def lat_average(summed):
    probe_count, groups, level_count, lat_count = summed.shape
    rows = lax.broadcasted_iota(jnp.int32, (lat_count, lat_count // 4), 0) // 4
    cols = lax.broadcasted_iota(jnp.int32, (lat_count, lat_count // 4), 1)
    average = jnp.where(rows == cols, 1.0 / 16.0, 0.0).astype(jnp.float32)
    coarse = jnp.dot(
        summed.reshape(-1, lat_count),
        average,
        precision=lax.Precision.HIGHEST,
        preferred_element_type=jnp.float32,
    )
    return coarse.reshape(probe_count, groups, level_count, lat_count // 4)


def body(increments, winds, obs_weight):
    probe_count, lon_count, level_count, lat_count = increments.shape
    halo = 4
    pack = (increments, winds[0][None], lat_mask(winds[1])[None], obs_weight[None])
    count = lax.axis_size("lon")
    forward = [(i, (i + 1) % count) for i in range(count)]
    backward = [((i + 1) % count, i) for i in range(count)]
    west_edge = jnp.concatenate([part[:, lon_count - halo:] for part in pack], axis=0)
    east_edge = jnp.concatenate([part[:, :halo] for part in pack], axis=0)
    from_west = lax.ppermute(west_edge, "lon", forward)
    from_east = lax.ppermute(east_edge, "lon", backward)
    bounds = ((0, probe_count), (probe_count, probe_count + 1),
              (probe_count + 1, probe_count + 2), (probe_count + 2, probe_count + 3))

    def fields(parts):
        return parts[0], parts[1][0], parts[2][0], parts[3][0]

    inner = lat_average(stencil_sums(*fields(pack)))
    sides = [
        jnp.stack([
            jnp.concatenate([from_west[lo:hi], part[:, :2 * halo]], axis=1),
            jnp.concatenate([part[:, lon_count - 2 * halo:], from_east[lo:hi]], axis=1),
        ])
        for part, (lo, hi) in zip(pack, bounds)
    ]
    rim = four_steps(sides[0], sides[1], sides[2], sides[3])
    west = coarsen(increments[:, :halo] + rim[0])
    east = coarsen(increments[:, lon_count - halo:] + rim[1])
    coarse = jnp.concatenate([west, inner, east], axis=1)
    coarse = coarse.reshape(probe_count, -1)
    all_probes = probe_count * lax.axis_size("probe")
    ident = jnp.eye(all_probes, dtype=jnp.float32)
    full_panel = lax.all_gather(coarse, "probe", axis=0, tiled=True)
    local_gram = jnp.dot(
        full_panel,
        full_panel.T,
        precision=lax.Precision.HIGHEST,
        preferred_element_type=jnp.float32,
    )
    gram = butterfly_sum(local_gram, "lon")
    lower = lax.linalg.cholesky(gram, symmetrize_input=False)
    inverse = lax.linalg.triangular_solve(lower, ident, left_side=True, lower=True)
    own_rows = lax.dynamic_slice_in_dim(
        inverse, lax.axis_index("probe") * probe_count, probe_count, 0
    )
    basis = jnp.dot(
        own_rows, full_panel, precision=lax.Precision.HIGHEST, preferred_element_type=jnp.float32
    )
    return (basis.reshape(probe_count, lon_count // 4, -1), lower.T)


def solution(mesh):
    in_specs = (P("probe", "lon", None, None), P(None, "lon", None, None), P("lon", None, None))
    out_specs = (P("probe", "lon", None), P())
    return jax.shard_map(body, mesh=mesh, in_specs=in_specs, out_specs=out_specs, check_vma=False)
```

```python
import functools

import jax
import jax.numpy as jnp
from jax import lax
from jax.experimental import pallas as pl
from jax.experimental.pallas import tpu as pltpu
from jax.sharding import PartitionSpec as P

MESH = pl.DeviceIdType.MESH


def from_behind(block, axis, distance):
    devices = range(lax.axis_size(axis))
    route = [((i - distance) % len(devices), i) for i in devices]
    return lax.ppermute(block, axis, route)


def exchange_kernel(count, radix, block_ref, out_ref, held, current, send_sem, recv_sem):
    me = lax.axis_index("lon")
    rounds = []
    stride = 1
    while stride < count:
        width = min(radix, count // stride)
        rounds.append((stride, width))
        stride *= width
    partners = [me ^ (j * stride) for stride, width in rounds for j in range(1, width)]

    barrier = pltpu.get_barrier_semaphore()
    for partner in partners:
        pl.semaphore_signal(barrier, inc=1, device_id={"lon": partner}, device_id_type=MESH)
    pl.semaphore_wait(barrier, len(partners))

    current[0] = block_ref[...]
    slot = 0
    for step, (stride, width) in enumerate(rounds):
        copies = []
        for j in range(1, width):
            copy = pltpu.make_async_remote_copy(
                src_ref=current.at[step],
                dst_ref=held.at[slot + j - 1],
                send_sem=send_sem.at[slot + j - 1],
                recv_sem=recv_sem.at[slot + j - 1],
                device_id={"lon": me ^ (j * stride)},
                device_id_type=MESH,
            )
            copy.start()
            copies.append(copy)
        for copy in copies:
            copy.wait()
        terms = [current[step]] + [held[slot + j - 1] for j in range(1, width)]
        while len(terms) > 1:
            terms = [terms[k] + terms[k + 1] for k in range(0, len(terms), 2)]
        current[step + 1] = terms[0]
        slot += width - 1
    out_ref[...] = current[len(rounds)]


def butterfly_sum(block, axis, radix=4):
    count = lax.axis_size(axis)
    if count & (count - 1) or count < 2:
        return lax.psum(block, axis)
    rounds = 0
    slots = 0
    stride = 1
    while stride < count:
        width = min(radix, count // stride)
        rounds += 1
        slots += width - 1
        stride *= width
    return pl.pallas_call(
        functools.partial(exchange_kernel, count, radix),
        out_shape=jax.ShapeDtypeStruct(block.shape, block.dtype),
        in_specs=[pl.BlockSpec(memory_space=pltpu.VMEM)],
        out_specs=pl.BlockSpec(memory_space=pltpu.VMEM),
        scratch_shapes=[
            pltpu.VMEM((slots,) + block.shape, block.dtype),
            pltpu.VMEM((rounds + 1,) + block.shape, block.dtype),
            pltpu.SemaphoreType.DMA((slots,)),
            pltpu.SemaphoreType.DMA((slots,)),
        ],
        compiler_params=pltpu.CompilerParams(collective_id=0, has_side_effects=True),
    )(block)


def padded(block, sides, width):
    for axis, dim in sides:
        count = lax.axis_size(axis)
        forward = [(i, i + 1) for i in range(count - 1)]
        forward.append((count - 1, 0))
        backward = [(target, source) for source, target in forward]
        low = lax.ppermute(
            lax.slice_in_dim(block, block.shape[dim] - width, None, axis=dim), axis, forward
        )
        high = lax.ppermute(lax.slice_in_dim(block, 0, width, axis=dim), axis, backward)
        block = jnp.concatenate([low, block, high], axis=dim)
    return block


def lat_mask(field):
    rows = lax.broadcasted_iota(jnp.int32, field.shape, field.ndim - 1)
    return jnp.where(rows > 0, field, jnp.zeros_like(field))


def below(field):
    return jnp.concatenate([jnp.zeros_like(field[..., :1]), field[..., :-1]], axis=-1)


def above(field):
    return jnp.concatenate([field[..., 1:], jnp.zeros_like(field[..., :1])], axis=-1)


def lon(x, start, stop):
    first, last, _ = slice(start, stop).indices(x.shape[-3])
    return lax.slice_in_dim(x, first, last, axis=x.ndim - 3)


def forward_core(widened, east, north):
    a_pos = jnp.maximum(east, 0.0)
    b_neg = jnp.minimum(east, 0.0)
    c_pos = jnp.maximum(lon(north, 1, -1), 0.0)
    d_neg = jnp.minimum(lon(north, 1, -1), 0.0)
    flux_w = lon(a_pos, 1, None) * lon(widened, 0, -1) + lon(b_neg, 1, None) * lon(widened, 1, None)
    inner = lon(widened, 1, -1)
    flux_s = c_pos * below(inner) + d_neg * inner
    flux_n = above(flux_s)
    return inner - (lon(flux_w, 1, None) - lon(flux_w, 0, -1)) - (flux_n - flux_s)


def adjoint_core(widened, east, north):
    a_pos = jnp.maximum(east, 0.0)
    b_neg = lon(jnp.minimum(east, 0.0), 1, -1)
    c_pos = jnp.maximum(lon(north, 1, -1), 0.0)
    d_neg = jnp.minimum(lon(north, 1, -1), 0.0)
    a_east = lon(a_pos, 2, None)
    c_north = above(c_pos)
    inner = lon(widened, 1, -1)
    west_val = lon(widened, 0, -2)
    east_val = lon(widened, 2, None)
    return (
        inner * (1.0 - a_east + b_neg - c_north + d_neg)
        - b_neg * west_val
        + a_east * east_val
        - d_neg * below(inner)
        + c_north * above(inner)
    )


def four_steps(state, east, north, weight):
    span = state.shape[-3]
    for step in range(2):
        state = forward_core(state, lon(east, step, span - step), lon(north, step, span - step))
    state = lon(weight, 2, span - 2) * state
    for step in range(2, 4):
        state = adjoint_core(state, lon(east, step, span - step), lon(north, step, span - step))
    return state


def coarsen(sketch):
    probe_count, lon_count, level_count, lat_count = sketch.shape
    summed = sketch.reshape(probe_count, lon_count // 4, 4, level_count, lat_count).sum(axis=2)
    rows = lax.broadcasted_iota(jnp.int32, (lat_count, lat_count // 4), 0) // 4
    cols = lax.broadcasted_iota(jnp.int32, (lat_count, lat_count // 4), 1)
    average = jnp.where(rows == cols, 1.0 / 16.0, 0.0).astype(jnp.float32)
    coarse = jnp.dot(
        summed.reshape(-1, lat_count),
        average,
        precision=lax.Precision.HIGHEST,
        preferred_element_type=jnp.float32,
    )
    return coarse.reshape(probe_count, lon_count // 4, level_count, lat_count // 4)


def stencil_kernel(q_ref, a_ref, b_ref, c_ref, d_ref, w_ref, n_ref, k_ref, o_ref):
    for row in range(q_ref.shape[0]):
        stencil_row(row, q_ref, a_ref, b_ref, c_ref, d_ref, w_ref, n_ref, k_ref, o_ref)


def stencil_row(row, q_ref, a_ref, b_ref, c_ref, d_ref, w_ref, n_ref, k_ref, o_ref):
    span = q_ref.shape[1]
    lat = q_ref.shape[-1]
    field = q_ref[row]
    state = field
    for step in range(2):
        lo, hi = step, span - step
        east_a = a_ref[lo:hi]
        east_b = b_ref[lo:hi]
        north_c = c_ref[lo + 1:hi - 1]
        north_d = d_ref[lo + 1:hi - 1]
        flux_w = east_a[1:] * state[:-1] + east_b[1:] * state[1:]
        inner = state[1:-1]
        flux_s = north_c * pltpu.roll(inner, 1, 2) + north_d * inner
        flux_n = pltpu.roll(flux_s, lat - 1, 2)
        state = inner - (flux_w[1:] - flux_w[:-1]) - (flux_n - flux_s)
    state = w_ref[2:span - 2] * state
    for step in range(2, 4):
        lo, hi = step, span - step
        west_b = b_ref[lo + 1:hi - 1]
        east_a = a_ref[lo + 2:hi]
        north_d = d_ref[lo + 1:hi - 1]
        north_up = n_ref[lo + 1:hi - 1]
        inner = state[1:-1]
        state = (
            inner * k_ref[lo + 1:hi - 1]
            - west_b * state[:-2]
            + east_a * state[2:]
            - north_d * pltpu.roll(inner, 1, 2)
            + north_up * pltpu.roll(inner, lat - 1, 2)
        )
    sketch = field[4:span - 4] + state
    groups = sketch.shape[0] // 4
    for g in range(groups):
        o_ref[row, g] = ((sketch[4 * g] + sketch[4 * g + 1]) + sketch[4 * g + 2]) + sketch[4 * g + 3]


def stencil_sums(slab, east, north, weight):
    probe_count, span, level_count, lat_count = slab.shape
    groups = (span - 8) // 4
    east_a = jnp.maximum(east, 0.0)
    east_b = jnp.minimum(east, 0.0)
    north_c = jnp.maximum(north, 0.0)
    north_d = jnp.minimum(north, 0.0)
    north_up = above(north_c)
    next_a = jnp.concatenate([east_a[1:], jnp.zeros_like(east_a[:1])], axis=0)
    centre = 1.0 - next_a + east_b - north_up + north_d
    winds = (east_a, east_b, north_c, north_d, weight, north_up, centre)
    block = 4 if probe_count % 4 == 0 else 1
    full = pl.BlockSpec((span, level_count, lat_count), lambda i: (0, 0, 0))
    elements = probe_count * span * level_count * lat_count
    return pl.pallas_call(
        stencil_kernel,
        out_shape=jax.ShapeDtypeStruct((probe_count, groups, level_count, lat_count), slab.dtype),
        grid=(probe_count // block,),
        in_specs=[pl.BlockSpec((block, span, level_count, lat_count), lambda i: (i, 0, 0, 0))]
        + [full] * 7,
        out_specs=pl.BlockSpec((block, groups, level_count, lat_count), lambda i: (i, 0, 0, 0)),
        cost_estimate=pl.CostEstimate(
            flops=50 * elements, transcendentals=0, bytes_accessed=4 * elements + 28 * span * level_count * lat_count
        ),
    )(slab, *winds)


def lat_average(summed):
    probe_count, groups, level_count, lat_count = summed.shape
    rows = lax.broadcasted_iota(jnp.int32, (lat_count, lat_count // 4), 0) // 4
    cols = lax.broadcasted_iota(jnp.int32, (lat_count, lat_count // 4), 1)
    average = jnp.where(rows == cols, 1.0 / 16.0, 0.0).astype(jnp.float32)
    coarse = jnp.dot(
        summed.reshape(-1, lat_count),
        average,
        precision=lax.Precision.HIGHEST,
        preferred_element_type=jnp.float32,
    )
    return coarse.reshape(probe_count, groups, level_count, lat_count // 4)


def body(increments, winds, obs_weight):
    probe_count, lon_count, level_count, lat_count = increments.shape
    halo = 4
    pack = (increments, winds[0][None], lat_mask(winds[1])[None], obs_weight[None])
    count = lax.axis_size("lon")
    forward = [(i, (i + 1) % count) for i in range(count)]
    backward = [((i + 1) % count, i) for i in range(count)]
    west_edge = jnp.concatenate([part[:, lon_count - halo:] for part in pack], axis=0)
    east_edge = jnp.concatenate([part[:, :halo] for part in pack], axis=0)
    from_west = lax.ppermute(west_edge, "lon", forward)
    from_east = lax.ppermute(east_edge, "lon", backward)
    bounds = ((0, probe_count), (probe_count, probe_count + 1),
              (probe_count + 1, probe_count + 2), (probe_count + 2, probe_count + 3))

    def fields(parts):
        return parts[0], parts[1][0], parts[2][0], parts[3][0]

    inner = lat_average(stencil_sums(*fields(pack)))
    sides = [
        jnp.stack([
            jnp.concatenate([from_west[lo:hi], part[:, :2 * halo]], axis=1),
            jnp.concatenate([part[:, lon_count - 2 * halo:], from_east[lo:hi]], axis=1),
        ])
        for part, (lo, hi) in zip(pack, bounds)
    ]
    rim = four_steps(sides[0], sides[1], sides[2], sides[3])
    edges = jnp.stack([increments[:, :halo], increments[:, lon_count - halo:]]) + rim
    edges = coarsen(edges.reshape((-1,) + edges.shape[2:]))
    west, east = edges[:probe_count], edges[probe_count:]
    coarse = jnp.concatenate([west, inner, east], axis=1)
    coarse = coarse.reshape(probe_count, -1)
    all_probes = probe_count * lax.axis_size("probe")
    ident = jnp.eye(all_probes, dtype=jnp.float32)
    full_panel = lax.all_gather(coarse, "probe", axis=0, tiled=True)
    local_gram = jnp.dot(
        full_panel,
        full_panel.T,
        precision=lax.Precision.HIGHEST,
        preferred_element_type=jnp.float32,
    )
    gram = butterfly_sum(local_gram, "lon")
    lower = lax.linalg.cholesky(gram, symmetrize_input=False)
    inverse = lax.linalg.triangular_solve(lower, ident, left_side=True, lower=True)
    own_rows = lax.dynamic_slice_in_dim(
        inverse, lax.axis_index("probe") * probe_count, probe_count, 0
    )
    basis = jnp.dot(
        own_rows, full_panel, precision=lax.Precision.HIGHEST, preferred_element_type=jnp.float32
    )
    return (basis.reshape(probe_count, lon_count // 4, -1), lower.T)


def solution(mesh):
    in_specs = (P("probe", "lon", None, None), P(None, "lon", None, None), P("lon", None, None))
    out_specs = (P("probe", "lon", None), P())
    return jax.shard_map(body, mesh=mesh, in_specs=in_specs, out_specs=out_specs, check_vma=False)
```
